256 devices in a mesh: dp: 4 (over y_lo, core), space: 64 (over z, y_hi, x).
Axes of the slice: x: 4, y: 4 (y_hi: 2, y_lo: 2; y = y_hi * 2 + y_lo), z: 8, core: 2. Of those that a mesh axis runs over, the one named last changes fastest.
Arguments:
- inputs: bfloat16 [12, 64, 4, 8192], P('dp', 'space'), may hold values from -6 to 6
- mask_one: int32 [12, 64, 16, 8192], P('dp', 'space'), may hold values 0 or 1
- place_one: int32 [12, 64, 16, 1024], P('dp', 'space'), may hold values from 0 to 7
- pooled_one: bfloat16 [12, 64, 16, 1024], P('dp', 'space'), may hold values from 0 to 2
- w_two: bfloat16 [27, 16, 32], replicated, may hold values from -0.21875 to 0.21875
- mask_two: int32 [12, 64, 32, 1024], P('dp', 'space'), may hold values 0 or 1
- place_two: int32 [12, 64, 32, 128], P('dp', 'space'), may hold values from 0 to 7
- grad_two: bfloat16 [12, 64, 32, 128], P('dp', 'space'), may hold values from -24 to 24
Outputs:
- grad_pooled: bfloat16 [12, 64, 16, 1024], P('dp', 'space')
- grad_w_one: float32 [27, 4, 16], replicated
- grad_w_two: float32 [27, 16, 32], replicated
The draws below stay inside these ranges and needn't reach their ends.
All inputs are finite; a program needn't handle non-finite values. No bound on the sum of `mask_one` or of `mask_two` on one device may be relied on, other than what follows from the above.
Results may differ from the reference program's by a relative error of at most 0.0029.
Values may be sent and summed in bfloat16 or wider, within the bound.
A program may use at most 128 MiB of HBM per device.

```python
import jax
import jax.numpy as jnp
from jax import lax

C_IN = 4
C_ONE = 16
C_TWO = 32
BX = 4
BY = 8
BZ = 256
SIDE = 4
SAMPLES = 12
BLOCKS = 64
CELLS = 8192
TERMS_ONE = 6291456
TERMS_TWO = 786432


def touch_ends(array, key, least, high):
    longest = array.shape.index(max(array.shape))
    spots = []
    for shift in (0, 1):
        where = [jax.random.randint(jax.random.fold_in(key, axis), (), 0, length) for axis, length in enumerate(array.shape)]
        where[longest] = (where[longest] + shift) % array.shape[longest]
        spots.append(tuple(where))
    return array.at[spots[0]].set(least).at[spots[1]].set(high)


def steps_of(own_key, extent, split, low, high):
    gain = 1.0
    for axis_at, parts in split:
        steps = jax.random.uniform(jax.random.fold_in(jax.random.fold_in(own_key, 6), axis_at), (parts,), jnp.float32, low / len(split), high / len(split))
        gain = gain * jnp.repeat(jnp.exp(steps), extent[axis_at] // parts).reshape((-1,) + (1,) * (len(extent) - 1 - axis_at))
    return gain


def bell_draw(rng, shape, deviation, most, split=(), dtype=jnp.bfloat16):
    loudness = steps_of(rng, shape, split, -0.22, 0.18) if split else 1.0
    values = jax.random.normal(rng, shape, jnp.float32) * deviation * loudness
    return jnp.minimum(jnp.maximum(values, -most), most).astype(dtype)


def setup_inputs(seed: int = 0) -> dict:
    seeds = jax.random.split(jax.random.key(seed), 9)
    inputs = bell_draw(seeds[0], (SAMPLES, BLOCKS, C_IN, CELLS), 1.0, 6.0, ((0, 4), (1, 64)))
    mask_one = touch_ends((jax.random.randint(seeds[1], (SAMPLES, BLOCKS, C_ONE, CELLS), 0, 2) < 1).astype(jnp.int32), jax.random.fold_in(seeds[1], 1), 0, 1)
    place_one = touch_ends(jax.random.randint(seeds[2], (SAMPLES, BLOCKS, C_ONE, CELLS // 8), 0, 8), jax.random.fold_in(seeds[2], 1), 0, 7).astype(jnp.int32)
    pooled_one = jnp.clip(2.0 * jax.random.uniform(seeds[3], (SAMPLES, BLOCKS, C_ONE, CELLS // 8), jnp.float32) ** steps_of(seeds[3], (SAMPLES, BLOCKS, C_ONE, CELLS // 8), ((0, 4), (1, 64)), -0.2, 0.2), 0.0, 2.0).astype(jnp.bfloat16)
    w_two = bell_draw(seeds[4], (27, C_ONE, C_TWO), (27 * C_TWO) ** -0.5, 0.21875)
    mask_two = touch_ends((jax.random.randint(seeds[5], (SAMPLES, BLOCKS, C_TWO, CELLS // 8), 0, 2) < 1).astype(jnp.int32), jax.random.fold_in(seeds[5], 1), 0, 1)
    place_two = touch_ends(jax.random.randint(seeds[6], (SAMPLES, BLOCKS, C_TWO, CELLS // 64), 0, 8), jax.random.fold_in(seeds[6], 1), 0, 7).astype(jnp.int32)
    grad_two = bell_draw(seeds[7], (SAMPLES, BLOCKS, C_TWO, CELLS // 64), 4.0, 24.0, ((0, 4), (1, 64)))
    return {"inputs": inputs, "mask_one": mask_one, "place_one": place_one, "pooled_one": pooled_one, "w_two": w_two, "mask_two": mask_two, "place_two": place_two, "grad_two": grad_two}


def to_box(blocks, channels, size_x, size_y, size_z):
    shaped = blocks.reshape(SIDE, SIDE, SIDE, channels, size_x, size_y, size_z)
    shaped = jnp.transpose(shaped, (3, 0, 4, 1, 5, 2, 6))
    return shaped.reshape(channels, SIDE * size_x, SIDE * size_y, SIDE * size_z)


def from_box(whole, channels, size_x, size_y, size_z):
    shaped = whole.reshape(channels, SIDE, size_x, SIDE, size_y, SIDE, size_z)
    shaped = jnp.transpose(shaped, (1, 3, 5, 0, 2, 4, 6))
    return shaped.reshape(SIDE * SIDE * SIDE, channels, size_x * size_y * size_z)


def spread(pooled, position):
    zeros = jnp.zeros_like(pooled)
    pieces = [jnp.where(position == k, pooled, zeros) for k in range(8)]
    stacked = jnp.stack(pieces, axis=-1)
    chans, size_x, size_y, size_z = pooled.shape
    stacked = stacked.reshape(chans, size_x, size_y, size_z, 2, 2, 2)
    stacked = jnp.transpose(stacked, (0, 1, 4, 2, 5, 3, 6))
    return stacked.reshape(chans, 2 * size_x, 2 * size_y, 2 * size_z)


def offsets():
    return [(ox, oy, oz) for ox in (-1, 0, 1) for oy in (-1, 0, 1) for oz in (-1, 0, 1)]


def one_sample(inputs, mask_one, place_one, pooled_one, w_two, mask_two, place_two, grad_two):
    half_x, half_y, half_z = BX // 2, BY // 2, BZ // 2
    quarter_x, quarter_y, quarter_z = BX // 4, BY // 4, BZ // 4
    gtwo = to_box(grad_two, C_TWO, quarter_x, quarter_y, quarter_z)
    ptwo = to_box(place_two, C_TWO, quarter_x, quarter_y, quarter_z)
    mtwo = to_box(mask_two, C_TWO, half_x, half_y, half_z)
    grad_conv_two = jnp.where(mtwo == 1, spread(gtwo, ptwo), jnp.zeros((), jnp.bfloat16)).astype(jnp.bfloat16)
    pooled = to_box(pooled_one, C_ONE, half_x, half_y, half_z)
    flat_two = grad_conv_two.reshape(C_TWO, -1)
    wgrad_two = []
    grad_sum = jnp.zeros((C_ONE, flat_two.shape[1]), jnp.float32)
    for index, (ox, oy, oz) in enumerate(offsets()):
        ahead = jnp.roll(pooled, (-ox, -oy, -oz), axis=(1, 2, 3)).reshape(C_ONE, -1)
        wgrad_two.append(jnp.dot(ahead, flat_two.T, preferred_element_type=jnp.float32))
        behind = jnp.roll(grad_conv_two, (ox, oy, oz), axis=(1, 2, 3)).reshape(C_TWO, -1)
        grad_sum = grad_sum + jnp.dot(w_two[index], behind, preferred_element_type=jnp.float32)
    grad_pooled = grad_sum.astype(jnp.bfloat16).reshape(C_ONE, SIDE * half_x, SIDE * half_y, SIDE * half_z)
    pone = to_box(place_one, C_ONE, half_x, half_y, half_z)
    mone = to_box(mask_one, C_ONE, BX, BY, BZ)
    grad_conv_one = jnp.where(mone == 1, spread(grad_pooled, pone), jnp.zeros((), jnp.bfloat16)).astype(jnp.bfloat16)
    flat_one = grad_conv_one.reshape(C_ONE, -1)
    source = to_box(inputs, C_IN, BX, BY, BZ)
    wgrad_one = []
    for ox, oy, oz in offsets():
        ahead = jnp.roll(source, (-ox, -oy, -oz), axis=(1, 2, 3)).reshape(C_IN, -1)
        wgrad_one.append(jnp.dot(ahead, flat_one.T, preferred_element_type=jnp.float32))
    blocks_out = from_box(grad_pooled, C_ONE, half_x, half_y, half_z)
    return blocks_out, jnp.stack(wgrad_one), jnp.stack(wgrad_two)


def reference(inputs, mask_one, place_one, pooled_one, w_two, mask_two, place_two, grad_two):
    def per_sample(items):
        return one_sample(items[0], items[1], items[2], items[3], w_two, items[4], items[5], items[6])

    grad_pooled, wgrad_one, wgrad_two = lax.map(per_sample, (inputs, mask_one, place_one, pooled_one, mask_two, place_two, grad_two))
    grad_w_one = jnp.sum(wgrad_one, axis=0) * (float(TERMS_ONE) ** -0.5)
    grad_w_two = jnp.sum(wgrad_two, axis=0) * (float(TERMS_TWO) ** -0.5)
    return grad_pooled, grad_w_one, grad_w_two
```

```python
import jax
import jax.numpy as jnp
from jax import lax
from jax.experimental import pallas as pl
from jax.experimental.pallas import tpu as pltpu
from jax.sharding import PartitionSpec as P

C_IN, C_ONE, C_TWO = 4, 16, 32
BX, BY, BZ = 4, 8, 256
S = 3
MESH = pl.DeviceIdType.MESH
F32, BF16, I32 = jnp.float32, jnp.bfloat16, jnp.int32
TILES = 20
TOTAL = 6291456
NEIGHBOURS = [
    (di, dj, dk)
    for di in (-1, 0, 1)
    for dj in (-1, 0, 1)
    for dk in (-1, 0, 1)
    if (di, dj, dk) != (0, 0, 0)
]
XY = [(di, dj) for di in (-1, 0, 1) for dj in (-1, 0, 1) if (di, dj) != (0, 0)]
NT = (((1,), (1,)), ((), ()))
NN = (((1,), (0,)), ((), ()))
TN = (((0,), (0,)), ((), ()))


def dot(a, b, dims=NN):
    return lax.dot_general(a, b, dims, preferred_element_type=F32)


def iota(shape, dim):
    return lax.broadcasted_iota(I32, shape, dim)


def one_hot(cond):
    return jnp.where(cond, 1.0, 0.0).astype(BF16)


def kernel(
    inp, mask_one, place_one, pooled, w_two, mask_two, place_two, grad_two,
    gp_out, w1_out, w2_out,
    mp, yb, tk, rx, ry, rt, z3, wp, pst, tbuf,
    iyb, rix, riy, in32, ko, rk, lhs, sel, gc, acc1,
    wg, r1, r2, fin,
    g_send, g_recv, i_send, i_recv, k_send, k_recv,
    s1_send, s1_recv, s2_send, s2_recv, s3_send, s3_recv,
):
    dp = lax.axis_index("dp")
    sp = lax.axis_index("space")
    bi, bj, bk = sp // 16, (sp // 4) % 4, sp % 4
    zc, t8 = sp // 8, sp % 8
    men = dp * 8 + t8

    def near(di, dj, dk):
        other = ((bi + di + 4) % 4) * 16 + ((bj + dj + 4) % 4) * 4 + (bk + dk + 4) % 4
        return {"space": other}

    def plane(n):
        return {"dp": n // 8, "space": zc * 8 + n % 8}

    def column(zz):
        return {"space": zz * 8 + t8}

    barrier = pltpu.get_barrier_semaphore()
    for d in NEIGHBOURS:
        pl.semaphore_signal(barrier, inc=1, device_id=near(*d), device_id_type=MESH)
    for n in range(1, 32):
        pl.semaphore_signal(barrier, inc=1, device_id=plane((men + n) % 32), device_id_type=MESH)
    for n in range(1, 8):
        pl.semaphore_signal(barrier, inc=1, device_id=column((zc + n) % 8), device_id_type=MESH)

    er, ec = iota((128, 768), 0), iota((128, 768), 1)
    ez = ec % 128 - (ec // 256 - 1)
    e3 = one_hot((er // 64 == (ec // 128) % 2) & (ez >= 0) & (ez < 128) & (ez // 2 == er % 64))
    e0 = e3[:, 256:512]
    p_b = place_two[...].astype(F32).astype(BF16)
    p_up = dot(p_b, e0)
    par = (iota((96, 256), 1) % 2).astype(F32)
    keep = jnp.zeros((96, 256), jnp.bool_)
    for dx in range(2):
        for dy in range(2):
            tiles = [(dx * 4 + 2 * qy + dy) * 128 for qy in range(2)]
            m = jnp.concatenate([mask_two[:, t : t + 128] for t in tiles], axis=1)
            keep = keep | ((p_up == par + float(4 * dx + 2 * dy)) & (m == 1))
    kept = dot(one_hot(keep), e0, NT)
    m_f = jnp.where(kept > 0.5, grad_two[...].astype(F32), 0.0)
    p_f = p_b.astype(F32)
    m_b = m_f.astype(BF16)
    mp[0] = m_b
    mp[1] = p_b
    low = iota((96, 128), 1) < 64
    yb[0] = jnp.where(low, m_f, pltpu.roll(p_f, 64, 1)).astype(BF16)
    yb[1] = jnp.where(low, pltpu.roll(m_f, 64, 1), p_f).astype(BF16)
    tr, tc = iota((16, 128), 0), iota((16, 128), 1)
    tk[...] = jnp.zeros_like(tk)
    for side, edge in ((0, 63), (1, 0)):
        pick_m = one_hot((tr < 2) & (tc == tr * 64 + edge))
        pick_p = one_hot((tr >= 2) & (tr < 4) & (tc == (tr - 2) * 64 + edge))
        tk[side, :, 0:96] = (dot(pick_m, m_b, NT) + dot(pick_p, p_b, NT)).astype(BF16)

    for q, y in ((0, 0), (1, 7)):
        for x in range(4):
            at = x * 2048 + y * 256
            iyb[q, :, :, x * 256 : (x + 1) * 256] = inp[:, :, at : at + 256]

    pl.semaphore_wait(barrier, 64)

    def g_copy(n, d):
        di, dj, dk = d
        if dk != 0:
            src = tk.at[0 if dk > 0 else 1]
            dst = rt.at[(1 - di) * 3 + 1 - dj, 0 if dk > 0 else 1]
        elif dj == 0:
            src, dst = mp, rx.at[(1 - di) // 2]
        else:
            src = yb.at[(1 + dj) // 2]
            dst = ry.at[1 - di, (1 - dj) // 2]
        return pltpu.make_async_remote_copy(
            src_ref=src, dst_ref=dst, send_sem=g_send.at[n], recv_sem=g_recv.at[n],
            device_id=near(*d), device_id_type=MESH,
        )

    def i_copy(n, d):
        di, dj = d
        if dj == 0:
            at = 3 * 2048 if di > 0 else 0
            src, dst = inp.at[:, :, at : at + 2048], rix.at[(1 - di) // 2]
        else:
            q = (1 + dj) // 2
            if di == 0:
                src = iyb.at[q]
                dst = riy.at[(1 - dj) // 2, :, :, 256 : 256 + 1024]
            else:
                at = 768 if di > 0 else 0
                to = 0 if di > 0 else 1280
                src = iyb.at[q, :, :, at : at + 256]
                dst = riy.at[(1 - dj) // 2, :, :, to : to + 256]
        return pltpu.make_async_remote_copy(
            src_ref=src, dst_ref=dst, send_sem=i_send.at[n], recv_sem=i_recv.at[n],
            device_id=near(di, dj, 0), device_id_type=MESH,
        )

    g_copies = [g_copy(n, d) for n, d in enumerate(NEIGHBOURS)]
    i_copies = [i_copy(n, d) for n, d in enumerate(XY)]
    for d, c in zip(NEIGHBOURS, g_copies):
        if d[2] != 0:
            c.start()
    for d, c in zip(NEIGHBOURS, g_copies):
        if d[2] == 0:
            c.start()
    for c in i_copies:
        c.start()

    for o9 in range(9):
        wp[o9 * 16 : o9 * 16 + 16, :] = jnp.concatenate(
            [w_two[o9 * 3 + b].astype(F32) for b in range(3)], axis=1
        ).astype(BF16)
    pst[...] = jnp.zeros_like(pst)
    for ox in range(3):
        for oy in range(3):
            o9 = ox * 3 + oy
            for qx in range(2):
                for qy in range(4):
                    to = ((qx + 2 - ox) * 6 + qy + 2 - oy) * 128
                    at = (qx * 4 + qy) * 128
                    for s in range(S):
                        pst[s, o9 * 16 : o9 * 16 + 16, to : to + 128] = pooled[
                            s * 16 : s * 16 + 16, at : at + 128
                        ]
    e1r, e1c = iota((128, 256), 0), iota((128, 256), 1)
    e1 = one_hot(e1c // 2 == e1r)
    par1 = (iota((48, 256), 1) % 2).astype(F32)
    for hx in range(2):
        for hy in range(4):
            at = (hx * 4 + hy) * 128
            up = dot(place_one[:, at : at + 128].astype(F32).astype(BF16), e1)
            for dx in range(2):
                for dy in range(2):
                    to = ((2 * hx + dx) * 8 + 2 * hy + dy) * 256
                    ok = (up == par1 + float(4 * dx + 2 * dy)) & (mask_one[:, to : to + 256] == 1)
                    sel[:, to : to + 256] = one_hot(ok)

    for n in range(8):
        i_copies[n].wait_recv()
    in32[...] = jnp.zeros_like(in32)
    for s in range(S):
        for x in range(6):
            for y in range(10):
                if 1 <= y <= 8:
                    if 1 <= x <= 4:
                        at = ((x - 1) * 8 + y - 1) * 256
                        v = inp[s, :, at : at + 256]
                    else:
                        at = (y - 1) * 256
                        v = rix[0 if x == 0 else 1, s, :, at : at + 256]
                else:
                    v = riy[0 if y == 0 else 1, s, :, x * 256 : x * 256 + 256]
                in32[s * 6 + x, 4 * y : 4 * y + 4, :] = v.astype(F32)
    lane48 = iota((48, 128), 1)
    for side in range(2):
        o = jnp.zeros((48, 128), F32)
        for l in range(18):
            tile = in32[l, :, 128:256] if side == 0 else in32[l, :, 0:128]
            edge = 127 if side == 0 else 0
            o = jnp.where(lane48 == l, pltpu.roll(tile, (l - edge) % 128, 1), o)
        ko[side] = o

    def k_copy(side):
        return pltpu.make_async_remote_copy(
            src_ref=ko.at[side], dst_ref=rk.at[side],
            send_sem=k_send.at[side], recv_sem=k_recv.at[side],
            device_id=near(0, 0, 1 if side == 0 else -1), device_id_type=MESH,
        )

    k_copies = [k_copy(0), k_copy(1)]
    for c in k_copies:
        c.start()

    for n in range(26):
        g_copies[n].wait_recv()
    fr, fc = iota((32, 768), 0), iota((32, 768), 1)
    f_in, f_mid, f_b = fc % 128, (fc // 128) % 2, fc // 256
    left = (f_b == 2) & (f_in == 0)
    right = (f_b == 0) & (f_in == 127)

    def halo_rows(row):
        return one_hot((left & (fr == row)) | (right & (fr == 16 + row)))

    f_m, f_p = halo_rows(f_mid), halo_rows(2 + f_mid)
    f_y = [halo_rows(2 * f_mid + q) for q in range(2)]
    lane = (iota((96, 128), 1) % 2).astype(F32)
    dz = [1.0 - lane, lane, 1.0 - lane]

    def put(b, x, y, dx, dy, um, up):
        v = jnp.where(up == dz[b] + float(4 * dx + 2 * dy), um, 0.0).astype(BF16)
        to = (x * 6 + y) * 128
        for s in range(S):
            z3[s, b * 32 : b * 32 + 32, to : to + 128] = v[s * 32 : s * 32 + 32]

    for di in (-1, 0, 1):
        for dj in (-1, 0, 1):
            stack = rt[(di + 1) * 3 + dj + 1].reshape(32, 128)[:, 0:96]
            xs = {-1: [(0, 1)], 0: [(1, 0), (2, 1)], 1: [(3, 0)]}[di]
            if dj == 0:
                ref = mp if di == 0 else rx.at[(di + 1) // 2]
                um = dot(ref[0], e3) + dot(stack, f_m, TN)
                up = dot(ref[1], e3) + dot(stack, f_p, TN)
                for b in range(3):
                    for qy in range(2):
                        at = (b * 2 + qy) * 128
                        for x, dx in xs:
                            for dy in range(2):
                                put(b, x, 1 + 2 * qy + dy, dx, dy, um[:, at : at + 128], up[:, at : at + 128])
            else:
                q = 1 if dj < 0 else 0
                u = dot(ry[di + 1, (dj + 1) // 2], e3) + dot(stack, f_y[q], TN)
                for b in range(3):
                    at = b * 256
                    for x, dx in xs:
                        put(b, x, 0 if dj < 0 else 5, dx, q, u[:, at : at + 128], u[:, at + 128 : at + 256])

    w2 = jnp.zeros((144, 96), F32)
    for s in range(S):
        for x in range(4):
            tbuf[:, x * 768 : x * 768 + 768] = dot(wp[...], z3[s, :, x * 768 : x * 768 + 768])
        w2 = w2 + dot(pst[s], z3[s], NT)
        for x in range(2):
            for y in range(4):
                a = jnp.zeros((16, 128), F32)
                for ox in range(3):
                    for oy in range(3):
                        r = (ox * 3 + oy) * 16
                        at = ((x + 2 - ox) * 6 + y + 2 - oy) * 128
                        a = a + tbuf[r : r + 16, at : at + 128]
                gp_out[s * 16 : s * 16 + 16, (x * 4 + y) * 128 : (x * 4 + y) * 128 + 128] = a.astype(BF16)
    w2 = jnp.concatenate([w2, jnp.zeros((144, 32), F32)], axis=1)
    for i in range(18):
        wg[i] = w2[i * 8 : i * 8 + 8]

    for c in k_copies:
        c.wait_recv()
    lane256 = iota((48, 256), 1)
    for l in range(18):
        v = in32[l]
        below = jnp.concatenate([pltpu.roll(rk[0], (0 - l) % 128, 1), jnp.zeros((48, 128), F32)], axis=1)
        above = jnp.concatenate([jnp.zeros((48, 128), F32), pltpu.roll(rk[1], (127 - l) % 128, 1)], axis=1)
        lhs[l, 0:48, :] = jnp.where(lane256 == 0, below, pltpu.roll(v, 1, 1)).astype(BF16)
        lhs[l, 48:96, :] = v.astype(BF16)
        lhs[l, 96:144, :] = jnp.where(lane256 == 255, above, pltpu.roll(v, 255, 1)).astype(BF16)

    for hx in range(2):
        for hy in range(4):
            at = (hx * 4 + hy) * 128
            up = dot(gp_out[:, at : at + 128], e1)
            for dx in range(2):
                for dy in range(2):
                    x, y = 2 * hx + dx, 2 * hy + dy
                    to = (x * 8 + y) * 256
                    v = (up * sel[:, to : to + 256].astype(F32)).astype(BF16)
                    for s in range(S):
                        gc[s, x, y * 16 : y * 16 + 16, :] = v[s * 16 : s * 16 + 16]
    a1 = jnp.zeros((432, 128), F32)
    for s in range(S):
        for x in range(4):
            three = lhs[s * 6 + x : s * 6 + x + 3].reshape(432, 256)
            a1 = a1 + dot(three, gc[s, x], NT)
    acc1[...] = a1

    row8, lane8 = iota((8, 128), 0), iota((8, 128), 1)
    packed = [jnp.zeros((8, 128), F32), jnp.zeros((8, 128), F32)]
    for ox in range(3):
        for oy in range(3):
            for b in range(3):
                o = ox * 9 + oy * 3 + b
                t = jnp.zeros((8, 128), F32)
                for i in range(5):
                    r = ox * 144 + b * 48 + i * 8
                    t = t + jnp.where(2 * i + row8 // 4 == lane8 // 16 + oy, acc1[r : r + 8, :], 0.0)
                t = t + pltpu.roll(t, 4, 0)
                t = t + pltpu.roll(t, 16, 1)
                t = t + pltpu.roll(t, 32, 1)
                t = t + pltpu.roll(t, 64, 1)
                k = o % 16
                packed[o // 16] = jnp.where(
                    (row8 // 4 == k // 8) & (lane8 // 16 == k % 8), t, packed[o // 16]
                )
    wg[18] = packed[0]
    wg[19] = packed[1]

    def p1(o):
        return pltpu.make_async_remote_copy(
            src_ref=wg.at[o], dst_ref=r1.at[men], send_sem=s1_send.at[o], recv_sem=s1_recv.at[men],
            device_id=plane(o), device_id_type=MESH,
        )

    def p1_from(n):
        return pltpu.make_async_remote_copy(
            src_ref=wg.at[0], dst_ref=r1.at[n], send_sem=s1_send.at[0], recv_sem=s1_recv.at[n],
            device_id=plane(n), device_id_type=MESH,
        )

    def p2(zz):
        return pltpu.make_async_remote_copy(
            src_ref=r2.at[zc], dst_ref=r2.at[zc], send_sem=s2_send.at[zz], recv_sem=s2_recv.at[zc],
            device_id=column(zz), device_id_type=MESH,
        )

    def p2_from(zz):
        return pltpu.make_async_remote_copy(
            src_ref=r2.at[zz], dst_ref=r2.at[zz], send_sem=s2_send.at[zz], recv_sem=s2_recv.at[zz],
            device_id=column(zz), device_id_type=MESH,
        )

    def p3(n):
        return pltpu.make_async_remote_copy(
            src_ref=fin.at[men], dst_ref=fin.at[men], send_sem=s3_send.at[n], recv_sem=s3_recv.at[men],
            device_id=plane(n), device_id_type=MESH,
        )

    def p3_from(o):
        return pltpu.make_async_remote_copy(
            src_ref=fin.at[o], dst_ref=fin.at[o], send_sem=s3_send.at[0], recv_sem=s3_recv.at[o],
            device_id=plane(o), device_id_type=MESH,
        )

    for o in range(TILES):
        @pl.when(men != o)
        def _():
            p1(o).start()

    owner = men < TILES

    @pl.when(owner)
    def _():
        r1[men] = wg[men]
        for n in range(32):
            @pl.when(men != n)
            def _():
                p1_from(n).wait_recv()
        total = r1[0]
        for n in range(1, 32):
            total = total + r1[n]
        r2[zc] = total
        for zz in range(8):
            @pl.when(zc != zz)
            def _():
                p2(zz).start()
        for zz in range(8):
            @pl.when(zc != zz)
            def _():
                p2_from(zz).wait_recv()
        total = r2[0]
        for zz in range(1, 8):
            total = total + r2[zz]
        fin[men] = total
        for n in range(32):
            @pl.when(men != n)
            def _():
                p3(n).start()

    for o in range(TILES):
        @pl.when(men != o)
        def _():
            p3_from(o).wait_recv()

    for o9 in range(9):
        for h in range(2):
            v = fin[2 * o9 + h] * (float(TOTAL // 8) ** -0.5)
            for b in range(3):
                w2_out[o9 * 3 + b, h * 8 : h * 8 + 8, :] = v[:, b * 32 : b * 32 + 32]
    for i in range(2):
        v = fin[18 + i] * (float(TOTAL) ** -0.5)
        for k in range(16 if i == 0 else 11):
            w1_out[i * 16 + k] = v[(k // 8) * 4 : (k // 8) * 4 + 4, (k % 8) * 16 : (k % 8) * 16 + 16]

    for c in g_copies + i_copies + k_copies:
        c.wait_send()
    for o in range(TILES):
        @pl.when(men != o)
        def _():
            p1(o).wait_send()

    @pl.when(owner)
    def _():
        for zz in range(8):
            @pl.when(zc != zz)
            def _():
                p2(zz).wait_send()
        for n in range(32):
            @pl.when(men != n)
            def _():
                p3(n).wait_send()


def local(inputs, mask_one, place_one, pooled_one, w_two, mask_two, place_two, grad_two):
    vm = pl.BlockSpec(memory_space=pltpu.VMEM)
    dma = pltpu.SemaphoreType.DMA
    gp, w1, w2 = pl.pallas_call(
        kernel,
        out_shape=(
            jax.ShapeDtypeStruct((48, 1024), BF16),
            jax.ShapeDtypeStruct((27, 4, 16), F32),
            jax.ShapeDtypeStruct((27, 16, 32), F32),
        ),
        in_specs=[vm] * 8,
        out_specs=(vm, vm, vm),
        scratch_shapes=[
            pltpu.VMEM((2, 96, 128), BF16),
            pltpu.VMEM((2, 96, 128), BF16),
            pltpu.VMEM((2, 16, 128), BF16),
            pltpu.VMEM((2, 2, 96, 128), BF16),
            pltpu.VMEM((3, 2, 96, 128), BF16),
            pltpu.VMEM((9, 2, 16, 128), BF16),
            pltpu.VMEM((S, 96, 3072), BF16),
            pltpu.VMEM((144, 96), BF16),
            pltpu.VMEM((S, 144, 3072), BF16),
            pltpu.VMEM((144, 3072), F32),
            pltpu.VMEM((2, S, 4, 1024), BF16),
            pltpu.VMEM((2, S, 4, 2048), BF16),
            pltpu.VMEM((2, S, 4, 1536), BF16),
            pltpu.VMEM((18, 48, 256), F32),
            pltpu.VMEM((2, 48, 128), F32),
            pltpu.VMEM((2, 48, 128), F32),
            pltpu.VMEM((18, 144, 256), BF16),
            pltpu.VMEM((48, 8192), BF16),
            pltpu.VMEM((S, 4, 128, 256), BF16),
            pltpu.VMEM((432, 128), F32),
            pltpu.VMEM((TILES, 8, 128), F32),
            pltpu.VMEM((32, 8, 128), F32),
            pltpu.VMEM((8, 8, 128), F32),
            pltpu.VMEM((TILES, 8, 128), F32),
            dma((26,)), dma((26,)), dma((8,)), dma((8,)), dma((2,)), dma((2,)),
            dma((TILES,)), dma((32,)), dma((8,)), dma((8,)), dma((32,)), dma((TILES,)),
        ],
        compiler_params=pltpu.CompilerParams(
            collective_id=0, has_side_effects=True, vmem_limit_bytes=56 * 1024 * 1024
        ),
        name="whole",
    )(
        inputs.reshape(S, 4, 8192),
        mask_one.reshape(48, 8192),
        place_one.reshape(48, 1024),
        pooled_one.reshape(48, 1024),
        w_two,
        mask_two.reshape(96, 1024),
        place_two.reshape(96, 128),
        grad_two.reshape(96, 128),
    )
    return gp.reshape(S, 1, 16, 1024), w1, w2


def solution(mesh):
    spec = P("dp", "space", None, None)
    return jax.shard_map(
        local,
        mesh=mesh,
        in_specs=(spec, spec, spec, spec, P(), spec, spec, spec),
        out_specs=(spec, P(), P()),
        check_vma=False,
    )
```

```python
import jax
import jax.numpy as jnp
from jax import lax
from jax.experimental import pallas as pl
from jax.experimental.pallas import tpu as pltpu
from jax.sharding import PartitionSpec as P

C_IN, C_ONE, C_TWO = 4, 16, 32
BX, BY, BZ = 4, 8, 256
S = 3
MESH = pl.DeviceIdType.MESH
F32, BF16, I32 = jnp.float32, jnp.bfloat16, jnp.int32
TILES = 18
TOTAL = 6291456
NEIGHBOURS = [
    (di, dj, dk)
    for di in (-1, 0, 1)
    for dj in (-1, 0, 1)
    for dk in (-1, 0, 1)
    if (di, dj, dk) != (0, 0, 0)
]
XY = [(di, dj) for di in (-1, 0, 1) for dj in (-1, 0, 1) if (di, dj) != (0, 0)]
NT = (((1,), (1,)), ((), ()))
NN = (((1,), (0,)), ((), ()))
TN = (((0,), (0,)), ((), ()))


def dot(a, b, dims=NN):
    return lax.dot_general(a, b, dims, preferred_element_type=F32)


def iota(shape, dim):
    return lax.broadcasted_iota(I32, shape, dim)


def one_hot(cond):
    return jnp.where(cond, 1.0, 0.0).astype(BF16)


def kernel(
    inp_h, mask_one_h, place_one_h, pooled_h, w_two_h, mask_two_h, place_two_h, grad_two_h,
    gp_h, fin_h,
    inp, mask_one, place_one, pooled, w_two, mask_two, place_two, grad_two, gp,
    mp, yb, tk, rx, ry, rt, z3, wp, pst, tbuf,
    iyb, rix, riy, in32, ko, rk, lhs, sel, gc, acc1,
    wg, r1, r2, fin, qbuf, own1, c1, c2, c3,
    g_send, g_recv, i_send, i_recv, k_send, k_recv,
    s1_send, s1_recv, s2_send, s2_recv, s3_send, s3_recv,
    t1_send, t1_recv, t2_send, t2_recv, t3_send, t3_recv, t4_send, t4_recv,
    l_sem, o_sem,
):
    dp = lax.axis_index("dp")
    sp = lax.axis_index("space")
    bi, bj, bk = sp // 16, (sp // 4) % 4, sp % 4
    zc, t8 = sp // 8, sp % 8
    men = dp * 8 + t8

    def near(di, dj, dk):
        other = ((bi + di + 4) % 4) * 16 + ((bj + dj + 4) % 4) * 4 + (bk + dk + 4) % 4
        return {"space": other}

    def plane(n):
        return {"dp": n // 8, "space": zc * 8 + n % 8}

    def column(zz):
        return {"space": zz * 8 + t8}

    def p1(o):
        return pltpu.make_async_remote_copy(
            src_ref=wg.at[o], dst_ref=r1.at[men], send_sem=s1_send.at[o], recv_sem=s1_recv.at[men],
            device_id=plane(o), device_id_type=MESH,
        )

    def p1_from(n):
        return pltpu.make_async_remote_copy(
            src_ref=wg.at[0], dst_ref=r1.at[n], send_sem=s1_send.at[0], recv_sem=s1_recv.at[n],
            device_id=plane(n), device_id_type=MESH,
        )

    def p2(zz):
        return pltpu.make_async_remote_copy(
            src_ref=r2.at[zc], dst_ref=r2.at[zc], send_sem=s2_send.at[zz], recv_sem=s2_recv.at[zc],
            device_id=column(zz), device_id_type=MESH,
        )

    def p2_from(zz):
        return pltpu.make_async_remote_copy(
            src_ref=r2.at[zz], dst_ref=r2.at[zz], send_sem=s2_send.at[zz], recv_sem=s2_recv.at[zz],
            device_id=column(zz), device_id_type=MESH,
        )

    def p3(n):
        return pltpu.make_async_remote_copy(
            src_ref=fin.at[men], dst_ref=fin.at[men], send_sem=s3_send.at[n], recv_sem=s3_recv.at[men],
            device_id=plane(n), device_id_type=MESH,
        )

    def p3_from(o):
        return pltpu.make_async_remote_copy(
            src_ref=fin.at[o], dst_ref=fin.at[o], send_sem=s3_send.at[0], recv_sem=s3_recv.at[o],
            device_id=plane(o), device_id_type=MESH,
        )

    core = dp % 2
    chip = (dp // 2) * 8 + t8

    def twin():
        return {"dp": dp + 1 - 2 * core}

    def chip_at(n):
        return {"dp": (n // 8) * 2 + core, "space": zc * 8 + n % 8}

    def t1():
        return pltpu.make_async_remote_copy(
            src_ref=own1.at[1 - core], dst_ref=c1, send_sem=t1_send, recv_sem=t1_recv,
            device_id=twin(), device_id_type=MESH,
        )

    def t2(n, slot):
        return pltpu.make_async_remote_copy(
            src_ref=c2.at[slot], dst_ref=c2.at[slot], send_sem=t2_send.at[n], recv_sem=t2_recv.at[slot],
            device_id=chip_at(n), device_id_type=MESH,
        )

    def t3(n, slot):
        return pltpu.make_async_remote_copy(
            src_ref=c3.at[slot], dst_ref=c3.at[slot], send_sem=t3_send.at[n], recv_sem=t3_recv.at[slot],
            device_id=column(n), device_id_type=MESH,
        )

    def t4(slot):
        return pltpu.make_async_remote_copy(
            src_ref=fin.at[TILES + slot], dst_ref=fin.at[TILES + slot], send_sem=t4_send, recv_sem=t4_recv,
            device_id=twin(), device_id_type=MESH,
        )

    loads = [
        pltpu.make_async_copy(a, b, l_sem.at[n])
        for n, (a, b) in enumerate(
            (
                (place_two_h, place_two),
                (mask_two_h, mask_two),
                (grad_two_h, grad_two),
                (inp_h, inp),
                (w_two_h, w_two),
                (pooled_h, pooled),
                (place_one_h, place_one),
                (mask_one_h, mask_one),
            )
        )
    ]
    for c in loads:
        c.start()

    barrier = pltpu.get_barrier_semaphore()
    for d in NEIGHBOURS:
        pl.semaphore_signal(barrier, inc=1, device_id=near(*d), device_id_type=MESH)
    for n in range(1, 32):
        pl.semaphore_signal(barrier, inc=1, device_id=plane((men + n) % 32), device_id_type=MESH)
    for n in range(1, 8):
        pl.semaphore_signal(barrier, inc=1, device_id=column((zc + n) % 8), device_id_type=MESH)

    er, ec = iota((128, 768), 0), iota((128, 768), 1)
    ez = ec % 128 - (ec // 256 - 1)
    e3 = one_hot((er // 64 == (ec // 128) % 2) & (ez >= 0) & (ez < 128) & (ez // 2 == er % 64))
    e0 = e3[:, 256:512]
    for c in loads[:3]:
        c.wait()
    p_b = place_two[...].astype(F32).astype(BF16)
    p_up = dot(p_b, e0)
    par = (iota((96, 256), 1) % 2).astype(F32)
    keep = jnp.zeros((96, 256), jnp.bool_)
    for dx in range(2):
        for dy in range(2):
            tiles = [(dx * 4 + 2 * qy + dy) * 128 for qy in range(2)]
            m = jnp.concatenate([mask_two[:, t : t + 128] for t in tiles], axis=1)
            keep = keep | ((p_up == par + float(4 * dx + 2 * dy)) & (m == 1))
    kept = dot(one_hot(keep), e0, NT)
    m_f = jnp.where(kept > 0.5, grad_two[...].astype(F32), 0.0)
    p_f = p_b.astype(F32)
    m_b = m_f.astype(BF16)
    mp[0] = m_b
    mp[1] = p_b
    low = iota((96, 128), 1) < 64
    yb[0] = jnp.where(low, m_f, pltpu.roll(p_f, 64, 1)).astype(BF16)
    yb[1] = jnp.where(low, pltpu.roll(m_f, 64, 1), p_f).astype(BF16)
    tr, tc = iota((16, 128), 0), iota((16, 128), 1)
    tk[...] = jnp.zeros_like(tk)
    for side, edge in ((0, 63), (1, 0)):
        pick_m = one_hot((tr < 2) & (tc == tr * 64 + edge))
        pick_p = one_hot((tr >= 2) & (tr < 4) & (tc == (tr - 2) * 64 + edge))
        tk[side, :, 0:96] = (dot(pick_m, m_b, NT) + dot(pick_p, p_b, NT)).astype(BF16)

    loads[3].wait()
    for q, y in ((0, 0), (1, 7)):
        for x in range(4):
            at = x * 2048 + y * 256
            iyb[q, :, :, x * 256 : (x + 1) * 256] = inp[:, :, at : at + 256]

    pl.semaphore_wait(barrier, 64)

    def g_copy(n, d):
        di, dj, dk = d
        if dk != 0:
            src = tk.at[0 if dk > 0 else 1]
            dst = rt.at[(1 - di) * 3 + 1 - dj, 0 if dk > 0 else 1]
        elif dj == 0:
            src, dst = mp, rx.at[(1 - di) // 2]
        else:
            src = yb.at[(1 + dj) // 2]
            dst = ry.at[1 - di, (1 - dj) // 2]
        return pltpu.make_async_remote_copy(
            src_ref=src, dst_ref=dst, send_sem=g_send.at[n], recv_sem=g_recv.at[n],
            device_id=near(*d), device_id_type=MESH,
        )

    def i_copy(n, d):
        di, dj = d
        if dj == 0:
            at = 3 * 2048 if di > 0 else 0
            src, dst = inp.at[:, :, at : at + 2048], rix.at[(1 - di) // 2]
        else:
            q = (1 + dj) // 2
            if di == 0:
                src = iyb.at[q]
                dst = riy.at[(1 - dj) // 2, :, :, 256 : 256 + 1024]
            else:
                at = 768 if di > 0 else 0
                to = 0 if di > 0 else 1280
                src = iyb.at[q, :, :, at : at + 256]
                dst = riy.at[(1 - dj) // 2, :, :, to : to + 256]
        return pltpu.make_async_remote_copy(
            src_ref=src, dst_ref=dst, send_sem=i_send.at[n], recv_sem=i_recv.at[n],
            device_id=near(di, dj, 0), device_id_type=MESH,
        )

    g_copies = [g_copy(n, d) for n, d in enumerate(NEIGHBOURS)]
    i_copies = [i_copy(n, d) for n, d in enumerate(XY)]
    for d, c in zip(NEIGHBOURS, g_copies):
        if d[2] != 0:
            c.start()
    for d, c in zip(NEIGHBOURS, g_copies):
        if d[2] == 0:
            c.start()
    for c in i_copies:
        c.start()

    qr, qc = iota((432, 128), 0), iota((432, 128), 1)
    for oy in range(3):
        qo = (qr // 144) * 9 + oy * 3 + (qr // 48) % 3
        qbuf[oy] = one_hot((qr % 4 == qc // 32) & (qc % 32 == qo) & (qr % 48 < 40))
    for c in loads[4:]:
        c.wait()
    for o9 in range(9):
        wp[o9 * 16 : o9 * 16 + 16, :] = jnp.concatenate(
            [w_two[o9 * 3 + b].astype(F32) for b in range(3)], axis=1
        ).astype(BF16)
    pst[...] = jnp.zeros_like(pst)
    for ox in range(3):
        for oy in range(3):
            o9 = ox * 3 + oy
            for qx in range(2):
                for qy in range(4):
                    to = ((qx + 2 - ox) * 6 + qy + 2 - oy) * 128
                    at = (qx * 4 + qy) * 128
                    for s in range(S):
                        pst[s, o9 * 16 : o9 * 16 + 16, to : to + 128] = pooled[
                            s * 16 : s * 16 + 16, at : at + 128
                        ]
    e1r, e1c = iota((128, 256), 0), iota((128, 256), 1)
    e1 = one_hot(e1c // 2 == e1r)
    par1 = (iota((48, 256), 1) % 2).astype(F32)
    for hx in range(2):
        for hy in range(4):
            at = (hx * 4 + hy) * 128
            up = dot(place_one[:, at : at + 128].astype(F32).astype(BF16), e1)
            for dx in range(2):
                for dy in range(2):
                    to = ((2 * hx + dx) * 8 + 2 * hy + dy) * 256
                    ok = (up == par1 + float(4 * dx + 2 * dy)) & (mask_one[:, to : to + 256] == 1)
                    sel[:, to : to + 256] = one_hot(ok)

    for n in range(26):
        g_copies[n].wait_recv()
    fr, fc = iota((32, 768), 0), iota((32, 768), 1)
    f_in, f_mid, f_b = fc % 128, (fc // 128) % 2, fc // 256
    left = (f_b == 2) & (f_in == 0)
    right = (f_b == 0) & (f_in == 127)

    def halo_rows(row):
        return one_hot((left & (fr == row)) | (right & (fr == 16 + row)))

    f_m, f_p = halo_rows(f_mid), halo_rows(2 + f_mid)
    f_y = [halo_rows(2 * f_mid + q) for q in range(2)]
    lane = (iota((96, 128), 1) % 2).astype(F32)
    dz = [1.0 - lane, lane, 1.0 - lane]

    def put(b, x, y, dx, dy, um, up):
        v = jnp.where(up == dz[b] + float(4 * dx + 2 * dy), um, 0.0).astype(BF16)
        to = (x * 6 + y) * 128
        for s in range(S):
            z3[s, b * 32 : b * 32 + 32, to : to + 128] = v[s * 32 : s * 32 + 32]

    for di in (-1, 0, 1):
        for dj in (-1, 0, 1):
            stack = rt[(di + 1) * 3 + dj + 1].reshape(32, 128)[:, 0:96]
            xs = {-1: [(0, 1)], 0: [(1, 0), (2, 1)], 1: [(3, 0)]}[di]
            if dj == 0:
                ref = mp if di == 0 else rx.at[(di + 1) // 2]
                um = dot(ref[0], e3) + dot(stack, f_m, TN)
                up = dot(ref[1], e3) + dot(stack, f_p, TN)
                for b in range(3):
                    for qy in range(2):
                        at = (b * 2 + qy) * 128
                        for x, dx in xs:
                            for dy in range(2):
                                put(b, x, 1 + 2 * qy + dy, dx, dy, um[:, at : at + 128], up[:, at : at + 128])
            else:
                q = 1 if dj < 0 else 0
                u = dot(ry[di + 1, (dj + 1) // 2], e3) + dot(stack, f_y[q], TN)
                for b in range(3):
                    at = b * 256
                    for x, dx in xs:
                        put(b, x, 0 if dj < 0 else 5, dx, q, u[:, at : at + 128], u[:, at + 128 : at + 256])

    w2 = jnp.zeros((144, 96), F32)
    for s in range(S):
        w2 = w2 + dot(pst[s], z3[s], NT)
    w2 = jnp.concatenate([w2, jnp.zeros((144, 32), F32)], axis=1)
    for i in range(TILES):
        wg[i] = w2[i * 8 : i * 8 + 8]
    for o in range(TILES):
        @pl.when(men != o)
        def _():
            p1(o).start()

    for s in range(S):
        for x in range(4):
            tbuf[:, x * 768 : x * 768 + 768] = dot(wp[...], z3[s, :, x * 768 : x * 768 + 768])
        for x in range(2):
            for y in range(4):
                a = jnp.zeros((16, 128), F32)
                for ox in range(3):
                    for oy in range(3):
                        r = (ox * 3 + oy) * 16
                        at = ((x + 2 - ox) * 6 + y + 2 - oy) * 128
                        a = a + tbuf[r : r + 16, at : at + 128]
                gp[s * 16 : s * 16 + 16, (x * 4 + y) * 128 : (x * 4 + y) * 128 + 128] = a.astype(BF16)
    gp_copy = pltpu.make_async_copy(gp, gp_h, o_sem.at[0])
    gp_copy.start()

    for n in range(8):
        i_copies[n].wait_recv()
    in32[...] = jnp.zeros_like(in32)
    for s in range(S):
        for x in range(6):
            for y in range(10):
                if 1 <= y <= 8:
                    if 1 <= x <= 4:
                        at = ((x - 1) * 8 + y - 1) * 256
                        v = inp[s, :, at : at + 256]
                    else:
                        at = (y - 1) * 256
                        v = rix[0 if x == 0 else 1, s, :, at : at + 256]
                else:
                    v = riy[0 if y == 0 else 1, s, :, x * 256 : x * 256 + 256]
                in32[s * 6 + x, 4 * y : 4 * y + 4, :] = v.astype(F32)
    lane48 = iota((48, 128), 1)
    for side in range(2):
        o = jnp.zeros((48, 128), F32)
        for l in range(18):
            tile = in32[l, :, 128:256] if side == 0 else in32[l, :, 0:128]
            edge = 127 if side == 0 else 0
            o = jnp.where(lane48 == l, pltpu.roll(tile, (l - edge) % 128, 1), o)
        ko[side] = o

    def k_copy(side):
        return pltpu.make_async_remote_copy(
            src_ref=ko.at[side], dst_ref=rk.at[side],
            send_sem=k_send.at[side], recv_sem=k_recv.at[side],
            device_id=near(0, 0, 1 if side == 0 else -1), device_id_type=MESH,
        )

    k_copies = [k_copy(0), k_copy(1)]
    for c in k_copies:
        c.start()

    for c in k_copies:
        c.wait_recv()
    lane256 = iota((48, 256), 1)
    for l in range(18):
        v = in32[l]
        below = jnp.concatenate([pltpu.roll(rk[0], (0 - l) % 128, 1), jnp.zeros((48, 128), F32)], axis=1)
        above = jnp.concatenate([jnp.zeros((48, 128), F32), pltpu.roll(rk[1], (127 - l) % 128, 1)], axis=1)
        lhs[l, 0:48, :] = jnp.where(lane256 == 0, below, pltpu.roll(v, 1, 1)).astype(BF16)
        lhs[l, 48:96, :] = v.astype(BF16)
        lhs[l, 96:144, :] = jnp.where(lane256 == 255, above, pltpu.roll(v, 255, 1)).astype(BF16)

    for hx in range(2):
        for hy in range(4):
            at = (hx * 4 + hy) * 128
            up = dot(gp[:, at : at + 128], e1)
            for dx in range(2):
                for dy in range(2):
                    x, y = 2 * hx + dx, 2 * hy + dy
                    to = (x * 8 + y) * 256
                    v = (up * sel[:, to : to + 256].astype(F32)).astype(BF16)
                    for s in range(S):
                        gc[s, x, y * 16 : y * 16 + 16, :] = v[s * 16 : s * 16 + 16]
    a1 = jnp.zeros((128, 432), F32)
    for s in range(S):
        for x in range(4):
            three = lhs[s * 6 + x : s * 6 + x + 3].reshape(432, 256)
            a1 = a1 + dot(gc[s, x], three, NT)
    acc1[...] = a1
    y_lane = (iota((16, 432), 1) % 48) // 4
    parts = []
    for oy in range(3):
        t = jnp.zeros((16, 432), F32)
        for y in range(8):
            t = t + jnp.where(y_lane == y + oy, acc1[y * 16 : y * 16 + 16, :], 0.0)
        parts.append(t)
    w1 = jnp.zeros((16, 128), F32)
    for oy in range(3):
        t = parts[oy]
        hi = t.astype(BF16)
        t = t - hi.astype(F32)
        mid = t.astype(BF16)
        low_part = (t - mid.astype(F32)).astype(BF16)
        r = dot(jnp.concatenate([hi, mid, low_part], axis=0), qbuf[oy])
        w1 = w1 + (r[0:16] + r[16:32] + r[32:48])
    own1[0] = w1[0:8]
    own1[1] = w1[8:16]

    t1().start()
    owner = men < TILES

    @pl.when(owner)
    def _():
        r1[men] = wg[men]
        for n in range(32):
            @pl.when(men != n)
            def _():
                p1_from(n).wait_recv()
        total = r1[0]
        for n in range(1, 32):
            total = total + r1[n]
        r2[zc] = total
        for zz in range(8):
            @pl.when(zc != zz)
            def _():
                p2(zz).start()

    t1().wait_recv()
    c2[chip] = own1[core] + c1[...]
    for n in range(16):
        @pl.when(chip != n)
        def _():
            t2(n, chip).start()

    @pl.when(owner)
    def _():
        for zz in range(8):
            @pl.when(zc != zz)
            def _():
                p2_from(zz).wait_recv()
        total = r2[0]
        for zz in range(1, 8):
            total = total + r2[zz]
        fin[men] = total
        for n in range(32):
            @pl.when(men != n)
            def _():
                p3(n).start()

    for n in range(16):
        @pl.when(chip != n)
        def _():
            t2(n, n).wait_recv()
    total = c2[0]
    for n in range(1, 16):
        total = total + c2[n]
    c3[zc] = total
    for n in range(8):
        @pl.when(zc != n)
        def _():
            t3(n, zc).start()
    for n in range(8):
        @pl.when(zc != n)
        def _():
            t3(n, n).wait_recv()
    total = c3[0]
    for n in range(1, 8):
        total = total + c3[n]
    fin[TILES + core] = total
    t4(core).start()

    for o in range(TILES):
        @pl.when(men != o)
        def _():
            p3_from(o).wait_recv()
    t4(1 - core).wait_recv()
    fin_copy = pltpu.make_async_copy(fin, fin_h, o_sem.at[1])
    fin_copy.start()

    for c in g_copies + i_copies + k_copies:
        c.wait_send()
    for o in range(TILES):
        @pl.when(men != o)
        def _():
            p1(o).wait_send()

    @pl.when(owner)
    def _():
        for zz in range(8):
            @pl.when(zc != zz)
            def _():
                p2(zz).wait_send()
        for n in range(32):
            @pl.when(men != n)
            def _():
                p3(n).wait_send()

    t1().wait_send()
    for n in range(16):
        @pl.when(chip != n)
        def _():
            t2(n, chip).wait_send()
    for n in range(8):
        @pl.when(zc != n)
        def _():
            t3(n, zc).wait_send()
    t4(core).wait_send()
    gp_copy.wait()
    fin_copy.wait()


def finish(gp, fin, gp_out, w1_out, w2_out):
    gp_out[...] = gp[...]
    for o9 in range(9):
        for h in range(2):
            v = fin[2 * o9 + h] * (float(TOTAL // 8) ** -0.5)
            for b in range(3):
                w2_out[o9 * 3 + b, h * 8 : h * 8 + 8, :] = v[:, b * 32 : b * 32 + 32]
    for i in range(2):
        v = fin[TILES + i] * (float(TOTAL) ** -0.5)
        for c in range(4):
            w1_out[c, i * 8 : i * 8 + 8, :] = v[:, c * 32 : c * 32 + 27]


def local(inputs, mask_one, place_one, pooled_one, w_two, mask_two, place_two, grad_two):
    vm = pl.BlockSpec(memory_space=pltpu.VMEM)
    anywhere = pl.BlockSpec(memory_space=pl.ANY)
    dma = pltpu.SemaphoreType.DMA
    gp, fin = pl.pallas_call(
        kernel,
        out_shape=(
            jax.ShapeDtypeStruct((48, 1024), BF16),
            jax.ShapeDtypeStruct((TILES + 2, 8, 128), F32),
        ),
        in_specs=[anywhere] * 8,
        out_specs=(anywhere, anywhere),
        scratch_shapes=[
            pltpu.VMEM((S, 4, 8192), BF16),
            pltpu.VMEM((48, 8192), I32),
            pltpu.VMEM((48, 1024), I32),
            pltpu.VMEM((48, 1024), BF16),
            pltpu.VMEM((27, 16, 32), BF16),
            pltpu.VMEM((96, 1024), I32),
            pltpu.VMEM((96, 128), I32),
            pltpu.VMEM((96, 128), BF16),
            pltpu.VMEM((48, 1024), BF16),
            pltpu.VMEM((2, 96, 128), BF16),
            pltpu.VMEM((2, 96, 128), BF16),
            pltpu.VMEM((2, 16, 128), BF16),
            pltpu.VMEM((2, 2, 96, 128), BF16),
            pltpu.VMEM((3, 2, 96, 128), BF16),
            pltpu.VMEM((9, 2, 16, 128), BF16),
            pltpu.VMEM((S, 96, 3072), BF16),
            pltpu.VMEM((144, 96), BF16),
            pltpu.VMEM((S, 144, 3072), BF16),
            pltpu.VMEM((144, 3072), F32),
            pltpu.VMEM((2, S, 4, 1024), BF16),
            pltpu.VMEM((2, S, 4, 2048), BF16),
            pltpu.VMEM((2, S, 4, 1536), BF16),
            pltpu.VMEM((18, 48, 256), F32),
            pltpu.VMEM((2, 48, 128), F32),
            pltpu.VMEM((2, 48, 128), F32),
            pltpu.VMEM((18, 144, 256), BF16),
            pltpu.VMEM((48, 8192), BF16),
            pltpu.VMEM((S, 4, 128, 256), BF16),
            pltpu.VMEM((128, 432), F32),
            pltpu.VMEM((TILES, 8, 128), F32),
            pltpu.VMEM((32, 8, 128), F32),
            pltpu.VMEM((8, 8, 128), F32),
            pltpu.VMEM((TILES + 2, 8, 128), F32),
            pltpu.VMEM((3, 432, 128), BF16),
            pltpu.VMEM((2, 8, 128), F32),
            pltpu.VMEM((8, 128), F32),
            pltpu.VMEM((16, 8, 128), F32),
            pltpu.VMEM((8, 8, 128), F32),
            dma((26,)), dma((26,)), dma((8,)), dma((8,)), dma((2,)), dma((2,)),
            dma((TILES,)), dma((32,)), dma((8,)), dma((8,)), dma((32,)), dma((TILES,)),
            dma, dma, dma((16,)), dma((16,)), dma((8,)), dma((8,)), dma, dma,
            dma((8,)), dma((2,)),
        ],
        compiler_params=pltpu.CompilerParams(
            collective_id=0, has_side_effects=True, vmem_limit_bytes=56 * 1024 * 1024
        ),
        name="whole",
    )(
        inputs.reshape(S, 4, 8192),
        mask_one.reshape(48, 8192),
        place_one.reshape(48, 1024),
        pooled_one.reshape(48, 1024),
        w_two,
        mask_two.reshape(96, 1024),
        place_two.reshape(96, 128),
        grad_two.reshape(96, 128),
    )
    gp, w1, w2 = pl.pallas_call(
        finish,
        out_shape=(
            jax.ShapeDtypeStruct((48, 1024), BF16),
            jax.ShapeDtypeStruct((4, 16, 27), F32),
            jax.ShapeDtypeStruct((27, 16, 32), F32),
        ),
        in_specs=[vm, vm],
        out_specs=(vm, vm, vm),
        name="finish",
    )(gp, fin)
    return gp.reshape(S, 1, 16, 1024), w1.transpose(2, 0, 1), w2


def solution(mesh):
    spec = P("dp", "space", None, None)
    return jax.shard_map(
        local,
        mesh=mesh,
        in_specs=(spec, spec, spec, spec, P(), spec, spec, spec),
        out_specs=(spec, P(), P()),
        check_vma=False,
    )
```

```python
import jax
import jax.numpy as jnp
from jax import lax
from jax.experimental import pallas as pl
from jax.experimental.pallas import tpu as pltpu
from jax.sharding import PartitionSpec as P

C_IN, C_ONE, C_TWO = 4, 16, 32
BX, BY, BZ = 4, 8, 256
S = 3
MESH = pl.DeviceIdType.MESH
F32, BF16, I32 = jnp.float32, jnp.bfloat16, jnp.int32
TILES = 18
TOTAL = 6291456
NEIGHBOURS = [
    (di, dj, dk)
    for di in (-1, 0, 1)
    for dj in (-1, 0, 1)
    for dk in (-1, 0, 1)
    if (di, dj, dk) != (0, 0, 0)
]
GREETED = [(-1, 0, 0), (1, 0, 0), (0, 0, -1), (0, 0, 1)]
XY = [(di, dj) for di in (-1, 0, 1) for dj in (-1, 0, 1) if (di, dj) != (0, 0)]
NT = (((1,), (1,)), ((), ()))
NN = (((1,), (0,)), ((), ()))
TN = (((0,), (0,)), ((), ()))


def dot(a, b, dims=NN):
    return lax.dot_general(a, b, dims, preferred_element_type=F32)


def iota(shape, dim):
    return lax.broadcasted_iota(I32, shape, dim)


def one_hot(cond):
    return jnp.where(cond, 1.0, 0.0).astype(BF16)


def kernel(
    inp_h, mask_one_h, place_one_h, pooled_h, w_two_h, mask_two_h, place_two_h, grad_two_h,
    gp_h, fin_h,
    inp, mask_one, place_one, pooled, w_two, mask_two, place_two, grad_two, gp,
    mp, yb, tk, rx, ry, rt, z3, wp, pst, tbuf,
    iyb, rix, riy, in32, ko, rk, lhs, sel, gc, acc1,
    wg, r1, r2, fin, qbuf, own1, c1, c2, c3,
    gx_send, gx_recv, gy_send, gy_recv, gt_send, gt_recv,
    ix_send, ix_recv, iy_send, iy_recv, k_send, k_recv,
    s1_send, s1_recv, s2_send, s2_recv, s3_send, s3_recv,
    t1_send, t1_recv, t2_send, t2_recv, t3_send, t3_recv, t4_send, t4_recv,
    l_sem, o_sem,
):
    dp = lax.axis_index("dp")
    sp = lax.axis_index("space")
    bi, bj, bk = sp // 16, (sp // 4) % 4, sp % 4
    zc, t8 = sp // 8, sp % 8
    men = dp * 8 + t8
    core = dp % 2
    chip = (dp // 2) * 8 + t8
    owner = ((core == 0) & (chip < 9)) | ((core == 1) & (chip >= 7))
    mine = jnp.where(core == 0, chip, chip + 2)

    def near(di, dj, dk):
        other = ((bi + di + 4) % 4) * 16 + ((bj + dj + 4) % 4) * 4 + (bk + dk + 4) % 4
        return {"space": other}

    def plane(n):
        return {"dp": n // 8, "space": zc * 8 + n % 8}

    def column(zz):
        return {"space": zz * 8 + t8}

    def twin():
        return {"dp": dp + 1 - 2 * core}

    def owner_of(o):
        n = o if o < 9 else o - 2
        return {"dp": (n // 8) * 2 + (0 if o < 9 else 1), "space": zc * 8 + n % 8}

    def is_mine(o):
        return owner & (mine == o)

    def p1(o):
        return pltpu.make_async_remote_copy(
            src_ref=wg.at[o], dst_ref=r1.at[men], send_sem=s1_send, recv_sem=s1_recv,
            device_id=owner_of(o), device_id_type=MESH,
        )

    def p2(n):
        return pltpu.make_async_remote_copy(
            src_ref=r2.at[zc], dst_ref=r2.at[zc], send_sem=s2_send, recv_sem=s2_recv,
            device_id=column((zc + n) % 8), device_id_type=MESH,
        )

    def p3(n):
        return pltpu.make_async_remote_copy(
            src_ref=fin.at[mine], dst_ref=fin.at[mine], send_sem=s3_send, recv_sem=s3_recv,
            device_id=plane((men + n) % 32), device_id_type=MESH,
        )

    def chip_at(n):
        return {"dp": (n // 8) * 2 + core, "space": zc * 8 + n % 8}

    def t1():
        return pltpu.make_async_remote_copy(
            src_ref=own1.at[1 - core], dst_ref=c1, send_sem=t1_send, recv_sem=t1_recv,
            device_id=twin(), device_id_type=MESH,
        )

    def t2(n):
        return pltpu.make_async_remote_copy(
            src_ref=c2.at[chip], dst_ref=c2.at[chip], send_sem=t2_send, recv_sem=t2_recv,
            device_id=chip_at((chip + n) % 16), device_id_type=MESH,
        )

    def t3(n):
        return pltpu.make_async_remote_copy(
            src_ref=c3.at[zc], dst_ref=c3.at[zc], send_sem=t3_send, recv_sem=t3_recv,
            device_id=column((zc + n) % 8), device_id_type=MESH,
        )

    def t4(slot):
        return pltpu.make_async_remote_copy(
            src_ref=fin.at[TILES + slot], dst_ref=fin.at[TILES + slot], send_sem=t4_send, recv_sem=t4_recv,
            device_id=twin(), device_id_type=MESH,
        )

    def group(ref, send_sem, recv_sem):
        return pltpu.make_async_remote_copy(
            src_ref=ref, dst_ref=ref, send_sem=send_sem, recv_sem=recv_sem,
            device_id=twin(), device_id_type=MESH,
        )

    gx_all, gy_all, gt_all = group(rx, gx_send, gx_recv), group(ry, gy_send, gy_recv), group(rt, gt_send, gt_recv)
    ix_all, iy_all, k_all = group(rix, ix_send, ix_recv), group(riy, iy_send, iy_recv), group(rk, k_send, k_recv)
    p1_got = group(r1.at[0:31], s1_send, s1_recv)
    p1_sent = group(wg.at[0 : TILES - 1], s1_send, s1_recv)
    p1_sent_all = group(wg, s1_send, s1_recv)
    p2_all = group(r2.at[0:7], s2_send, s2_recv)
    p3_sent = group(r1.at[0:31], s3_send, s3_recv)
    p3_got = group(fin.at[0 : TILES - 1], s3_send, s3_recv)
    p3_got_all = group(fin.at[0:TILES], s3_send, s3_recv)
    t2_all = group(c2.at[0:15], t2_send, t2_recv)
    t3_all = group(c3.at[0:7], t3_send, t3_recv)

    loads = [
        pltpu.make_async_copy(a, b, l_sem.at[n])
        for n, (a, b) in enumerate(
            (
                (place_two_h, place_two),
                (mask_two_h, mask_two),
                (grad_two_h, grad_two),
                (inp_h, inp),
                (w_two_h, w_two),
                (pooled_h, pooled),
                (place_one_h, place_one),
                (mask_one_h, mask_one),
            )
        )
    ]
    for c in loads:
        c.start()

    barrier = pltpu.get_barrier_semaphore()
    for d in NEIGHBOURS:
        if d in GREETED:
            continue
        pl.semaphore_signal(barrier, inc=1, device_id=near(*d), device_id_type=MESH)
    for n in range(1, 32):
        pl.semaphore_signal(barrier, inc=1, device_id=plane((men + n) % 32), device_id_type=MESH)
    for n in range(1, 8):
        pl.semaphore_signal(barrier, inc=1, device_id=column((zc + n) % 8), device_id_type=MESH)

    er, ec = iota((128, 768), 0), iota((128, 768), 1)
    ez = ec % 128 - (ec // 256 - 1)
    e3 = one_hot((er // 64 == (ec // 128) % 2) & (ez >= 0) & (ez < 128) & (ez // 2 == er % 64))
    e0 = e3[:, 256:512]
    for c in loads[:3]:
        c.wait()
    p_b = place_two[...].astype(F32).astype(BF16)
    p_up = dot(p_b, e0)
    par = (iota((96, 256), 1) % 2).astype(F32)
    keep = jnp.zeros((96, 256), jnp.bool_)
    for dx in range(2):
        for dy in range(2):
            tiles = [(dx * 4 + 2 * qy + dy) * 128 for qy in range(2)]
            m = jnp.concatenate([mask_two[:, t : t + 128] for t in tiles], axis=1)
            keep = keep | ((p_up == par + float(4 * dx + 2 * dy)) & (m == 1))
    kept = dot(one_hot(keep), e0, NT)
    m_f = jnp.where(kept > 0.5, grad_two[...].astype(F32), 0.0)
    p_f = p_b.astype(F32)
    m_b = m_f.astype(BF16)
    mp[0] = m_b
    mp[1] = p_b
    low = iota((96, 128), 1) < 64
    yb[0] = jnp.where(low, m_f, pltpu.roll(p_f, 64, 1)).astype(BF16)
    yb[1] = jnp.where(low, pltpu.roll(m_f, 64, 1), p_f).astype(BF16)
    tr, tc = iota((16, 128), 0), iota((16, 128), 1)
    tk[...] = jnp.zeros_like(tk)
    for side, edge in ((0, 63), (1, 0)):
        pick_m = one_hot((tr < 2) & (tc == tr * 64 + edge))
        pick_p = one_hot((tr >= 2) & (tr < 4) & (tc == (tr - 2) * 64 + edge))
        tk[side, :, 0:96] = (dot(pick_m, m_b, NT) + dot(pick_p, p_b, NT)).astype(BF16)

    loads[3].wait()
    for q, y in ((0, 0), (1, 7)):
        for x in range(4):
            at = x * 2048 + y * 256
            iyb[q, :, :, x * 256 : (x + 1) * 256] = inp[:, :, at : at + 256]

    pl.semaphore_wait(barrier, 60)

    def g_copy(n, d):
        di, dj, dk = d
        if dk != 0:
            src = tk.at[0 if dk > 0 else 1]
            dst = rt.at[(1 - di) * 3 + 1 - dj, 0 if dk > 0 else 1]
            sems = gt_send, gt_recv
        elif dj == 0:
            src, dst = mp, rx.at[(1 - di) // 2]
            sems = gx_send, gx_recv
        else:
            src = yb.at[(1 + dj) // 2]
            dst = ry.at[1 - di, (1 - dj) // 2]
            sems = gy_send, gy_recv
        return pltpu.make_async_remote_copy(
            src_ref=src, dst_ref=dst, send_sem=sems[0], recv_sem=sems[1],
            device_id=near(*d), device_id_type=MESH,
        )

    def i_copy(n, d):
        di, dj = d
        if dj == 0:
            at = 3 * 2048 if di > 0 else 0
            src, dst = inp.at[:, :, at : at + 2048], rix.at[(1 - di) // 2]
            sems = ix_send, ix_recv
        else:
            q = (1 + dj) // 2
            sems = iy_send, iy_recv
            if di == 0:
                src = iyb.at[q]
                dst = riy.at[(1 - dj) // 2, :, :, 256 : 256 + 1024]
            else:
                at = 768 if di > 0 else 0
                to = 0 if di > 0 else 1280
                src = iyb.at[q, :, :, at : at + 256]
                dst = riy.at[(1 - dj) // 2, :, :, to : to + 256]
        return pltpu.make_async_remote_copy(
            src_ref=src, dst_ref=dst, send_sem=sems[0], recv_sem=sems[1],
            device_id=near(di, dj, 0), device_id_type=MESH,
        )

    g_copies = [g_copy(n, d) for n, d in enumerate(NEIGHBOURS)]
    i_copies = [i_copy(n, d) for n, d in enumerate(XY)]
    for d, c in zip(NEIGHBOURS, g_copies):
        if d[2] != 0:
            c.start()
    for d, c in zip(NEIGHBOURS, g_copies):
        if d[2] == 0:
            c.start()
    for c in i_copies:
        c.start()

    qr, qc = iota((432, 128), 0), iota((432, 128), 1)
    for oy in range(3):
        qo = (qr // 144) * 9 + oy * 3 + (qr // 48) % 3
        qbuf[oy] = one_hot((qr % 4 == qc // 32) & (qc % 32 == qo) & (qr % 48 < 40))
    for c in loads[4:]:
        c.wait()
    for o9 in range(9):
        wp[o9 * 16 : o9 * 16 + 16, :] = jnp.concatenate(
            [w_two[o9 * 3 + b].astype(F32) for b in range(3)], axis=1
        ).astype(BF16)
    pst[...] = jnp.zeros_like(pst)
    for ox in range(3):
        for oy in range(3):
            o9 = ox * 3 + oy
            for qx in range(2):
                for qy in range(4):
                    to = ((qx + 2 - ox) * 6 + qy + 2 - oy) * 128
                    at = (qx * 4 + qy) * 128
                    for s in range(S):
                        pst[s, o9 * 16 : o9 * 16 + 16, to : to + 128] = pooled[
                            s * 16 : s * 16 + 16, at : at + 128
                        ]
    e1r, e1c = iota((128, 256), 0), iota((128, 256), 1)
    e1 = one_hot(e1c // 2 == e1r)
    par1 = (iota((48, 256), 1) % 2).astype(F32)
    for hx in range(2):
        for hy in range(4):
            at = (hx * 4 + hy) * 128
            up = dot(place_one[:, at : at + 128].astype(F32).astype(BF16), e1)
            for dx in range(2):
                for dy in range(2):
                    to = ((2 * hx + dx) * 8 + 2 * hy + dy) * 256
                    ok = (up == par1 + float(4 * dx + 2 * dy)) & (mask_one[:, to : to + 256] == 1)
                    sel[:, to : to + 256] = one_hot(ok)

    for c in (gt_all, gx_all, gy_all):
        c.wait_recv()
    fr, fc = iota((32, 768), 0), iota((32, 768), 1)
    f_in, f_mid, f_b = fc % 128, (fc // 128) % 2, fc // 256
    left = (f_b == 2) & (f_in == 0)
    right = (f_b == 0) & (f_in == 127)

    def halo_rows(row):
        return one_hot((left & (fr == row)) | (right & (fr == 16 + row)))

    f_m, f_p = halo_rows(f_mid), halo_rows(2 + f_mid)
    f_y = [halo_rows(2 * f_mid + q) for q in range(2)]
    lane = (iota((96, 128), 1) % 2).astype(F32)
    dz = [1.0 - lane, lane, 1.0 - lane]

    def put(b, x, y, dx, dy, um, up):
        v = jnp.where(up == dz[b] + float(4 * dx + 2 * dy), um, 0.0).astype(BF16)
        to = (x * 6 + y) * 128
        for s in range(S):
            z3[s, b * 32 : b * 32 + 32, to : to + 128] = v[s * 32 : s * 32 + 32]

    for di in (-1, 0, 1):
        for dj in (-1, 0, 1):
            stack = rt[(di + 1) * 3 + dj + 1].reshape(32, 128)[:, 0:96]
            xs = {-1: [(0, 1)], 0: [(1, 0), (2, 1)], 1: [(3, 0)]}[di]
            if dj == 0:
                ref = mp if di == 0 else rx.at[(di + 1) // 2]
                um = dot(ref[0], e3) + dot(stack, f_m, TN)
                up = dot(ref[1], e3) + dot(stack, f_p, TN)
                for b in range(3):
                    for qy in range(2):
                        at = (b * 2 + qy) * 128
                        for x, dx in xs:
                            for dy in range(2):
                                put(b, x, 1 + 2 * qy + dy, dx, dy, um[:, at : at + 128], up[:, at : at + 128])
            else:
                q = 1 if dj < 0 else 0
                u = dot(ry[di + 1, (dj + 1) // 2], e3) + dot(stack, f_y[q], TN)
                for b in range(3):
                    at = b * 256
                    for x, dx in xs:
                        put(b, x, 0 if dj < 0 else 5, dx, q, u[:, at : at + 128], u[:, at + 128 : at + 256])

    w2 = jnp.zeros((144, 96), F32)
    for s in range(S):
        w2 = w2 + dot(pst[s], z3[s], NT)
    w2 = jnp.concatenate([w2, jnp.zeros((144, 32), F32)], axis=1)
    for i in range(TILES):
        wg[i] = w2[i * 8 : i * 8 + 8]
    for o in range(TILES):
        @pl.when(~is_mine(o))
        def _():
            p1(o).start()

    for s in range(S):
        for x in range(4):
            tbuf[:, x * 768 : x * 768 + 768] = dot(wp[...], z3[s, :, x * 768 : x * 768 + 768])
        for x in range(2):
            for y in range(4):
                a = jnp.zeros((16, 128), F32)
                for ox in range(3):
                    for oy in range(3):
                        r = (ox * 3 + oy) * 16
                        at = ((x + 2 - ox) * 6 + y + 2 - oy) * 128
                        a = a + tbuf[r : r + 16, at : at + 128]
                gp[s * 16 : s * 16 + 16, (x * 4 + y) * 128 : (x * 4 + y) * 128 + 128] = a.astype(BF16)
    gp_copy = pltpu.make_async_copy(gp, gp_h, o_sem.at[0])
    gp_copy.start()

    for c in (ix_all, iy_all):
        c.wait_recv()
    in32[...] = jnp.zeros_like(in32)
    for s in range(S):
        for x in range(6):
            for y in range(10):
                if 1 <= y <= 8:
                    if 1 <= x <= 4:
                        at = ((x - 1) * 8 + y - 1) * 256
                        v = inp[s, :, at : at + 256]
                    else:
                        at = (y - 1) * 256
                        v = rix[0 if x == 0 else 1, s, :, at : at + 256]
                else:
                    v = riy[0 if y == 0 else 1, s, :, x * 256 : x * 256 + 256]
                in32[s * 6 + x, 4 * y : 4 * y + 4, :] = v.astype(F32)
    lane48 = iota((48, 128), 1)
    for side in range(2):
        o = jnp.zeros((48, 128), F32)
        for l in range(18):
            tile = in32[l, :, 128:256] if side == 0 else in32[l, :, 0:128]
            edge = 127 if side == 0 else 0
            o = jnp.where(lane48 == l, pltpu.roll(tile, (l - edge) % 128, 1), o)
        ko[side] = o

    def k_copy(side):
        return pltpu.make_async_remote_copy(
            src_ref=ko.at[side], dst_ref=rk.at[side],
            send_sem=k_send, recv_sem=k_recv,
            device_id=near(0, 0, 1 if side == 0 else -1), device_id_type=MESH,
        )

    k_copies = [k_copy(0), k_copy(1)]
    for c in k_copies:
        c.start()

    k_all.wait_recv()
    lane256 = iota((48, 256), 1)
    for l in range(18):
        v = in32[l]
        below = jnp.concatenate([pltpu.roll(rk[0], (0 - l) % 128, 1), jnp.zeros((48, 128), F32)], axis=1)
        above = jnp.concatenate([jnp.zeros((48, 128), F32), pltpu.roll(rk[1], (127 - l) % 128, 1)], axis=1)
        lhs[l, 0:48, :] = jnp.where(lane256 == 0, below, pltpu.roll(v, 1, 1)).astype(BF16)
        lhs[l, 48:96, :] = v.astype(BF16)
        lhs[l, 96:144, :] = jnp.where(lane256 == 255, above, pltpu.roll(v, 255, 1)).astype(BF16)

    for hx in range(2):
        for hy in range(4):
            at = (hx * 4 + hy) * 128
            up = dot(gp[:, at : at + 128], e1)
            for dx in range(2):
                for dy in range(2):
                    x, y = 2 * hx + dx, 2 * hy + dy
                    to = (x * 8 + y) * 256
                    v = (up * sel[:, to : to + 256].astype(F32)).astype(BF16)
                    for s in range(S):
                        gc[s, x, y * 16 : y * 16 + 16, :] = v[s * 16 : s * 16 + 16]
    a1 = jnp.zeros((128, 432), F32)
    for s in range(S):
        for x in range(4):
            three = lhs[s * 6 + x : s * 6 + x + 3].reshape(432, 256)
            a1 = a1 + dot(gc[s, x], three, NT)
    acc1[...] = a1
    y_lane = (iota((16, 432), 1) % 48) // 4
    parts = []
    for oy in range(3):
        t = jnp.zeros((16, 432), F32)
        for y in range(8):
            t = t + jnp.where(y_lane == y + oy, acc1[y * 16 : y * 16 + 16, :], 0.0)
        parts.append(t)
    w1 = jnp.zeros((16, 128), F32)
    for oy in range(3):
        t = parts[oy]
        hi = t.astype(BF16)
        t = t - hi.astype(F32)
        mid = t.astype(BF16)
        low_part = (t - mid.astype(F32)).astype(BF16)
        r = dot(jnp.concatenate([hi, mid, low_part], axis=0), qbuf[oy])
        w1 = w1 + (r[0:16] + r[16:32] + r[32:48])
    own1[0] = w1[0:8]
    own1[1] = w1[8:16]

    t1().start()

    @pl.when(owner)
    def _():
        p1_got.wait_recv()
        r1[men] = wg[mine]
        total = r1[0]
        for n in range(1, 32):
            total = total + r1[n]
        r2[zc] = total
        for n in range(1, 8):
            p2(n).start()

    t1().wait_recv()
    c2[chip] = own1[core] + c1[...]
    for n in range(1, 16):
        t2(n).start()

    @pl.when(owner)
    def _():
        p2_all.wait_recv()
        total = r2[0]
        for zz in range(1, 8):
            total = total + r2[zz]
        fin[mine] = total
        for n in range(1, 32):
            p3(n).start()

    t2_all.wait_recv()
    total = c2[0]
    for n in range(1, 16):
        total = total + c2[n]
    c3[zc] = total
    for n in range(1, 8):
        t3(n).start()
    t3_all.wait_recv()
    total = c3[0]
    for n in range(1, 8):
        total = total + c3[n]
    fin[TILES + core] = total
    t4(core).start()

    @pl.when(owner)
    def _():
        p3_got.wait_recv()

    @pl.when(~owner)
    def _():
        p3_got_all.wait_recv()

    t4(1 - core).wait_recv()
    fin_copy = pltpu.make_async_copy(fin, fin_h, o_sem.at[1])
    fin_copy.start()

    for c in (gt_all, gx_all, gy_all, ix_all, iy_all, k_all, t2_all, t3_all):
        c.wait_send()
    t1().wait_send()
    t4(core).wait_send()

    @pl.when(owner)
    def _():
        p1_sent.wait_send()
        p2_all.wait_send()
        p3_sent.wait_send()

    @pl.when(~owner)
    def _():
        p1_sent_all.wait_send()

    gp_copy.wait()
    fin_copy.wait()


def finish(gp, fin, gp_out, w1_out, w2_out):
    gp_out[...] = gp[...]
    for o9 in range(9):
        for h in range(2):
            v = fin[2 * o9 + h] * (float(TOTAL // 8) ** -0.5)
            for b in range(3):
                w2_out[o9 * 3 + b, h * 8 : h * 8 + 8, :] = v[:, b * 32 : b * 32 + 32]
    for i in range(2):
        v = fin[TILES + i] * (float(TOTAL) ** -0.5)
        for c in range(4):
            w1_out[c, i * 8 : i * 8 + 8, :] = v[:, c * 32 : c * 32 + 27]


def local(inputs, mask_one, place_one, pooled_one, w_two, mask_two, place_two, grad_two):
    vm = pl.BlockSpec(memory_space=pltpu.VMEM)
    anywhere = pl.BlockSpec(memory_space=pl.ANY)
    dma = pltpu.SemaphoreType.DMA
    gp, fin = pl.pallas_call(
        kernel,
        out_shape=(
            jax.ShapeDtypeStruct((48, 1024), BF16),
            jax.ShapeDtypeStruct((TILES + 2, 8, 128), F32),
        ),
        in_specs=[anywhere] * 8,
        out_specs=(anywhere, anywhere),
        scratch_shapes=[
            pltpu.VMEM((S, 4, 8192), BF16),
            pltpu.VMEM((48, 8192), I32),
            pltpu.VMEM((48, 1024), I32),
            pltpu.VMEM((48, 1024), BF16),
            pltpu.VMEM((27, 16, 32), BF16),
            pltpu.VMEM((96, 1024), I32),
            pltpu.VMEM((96, 128), I32),
            pltpu.VMEM((96, 128), BF16),
            pltpu.VMEM((48, 1024), BF16),
            pltpu.VMEM((2, 96, 128), BF16),
            pltpu.VMEM((2, 96, 128), BF16),
            pltpu.VMEM((2, 16, 128), BF16),
            pltpu.VMEM((2, 2, 96, 128), BF16),
            pltpu.VMEM((3, 2, 96, 128), BF16),
            pltpu.VMEM((9, 2, 16, 128), BF16),
            pltpu.VMEM((S, 96, 3072), BF16),
            pltpu.VMEM((144, 96), BF16),
            pltpu.VMEM((S, 144, 3072), BF16),
            pltpu.VMEM((144, 3072), F32),
            pltpu.VMEM((2, S, 4, 1024), BF16),
            pltpu.VMEM((2, S, 4, 2048), BF16),
            pltpu.VMEM((2, S, 4, 1536), BF16),
            pltpu.VMEM((18, 48, 256), F32),
            pltpu.VMEM((2, 48, 128), F32),
            pltpu.VMEM((2, 48, 128), F32),
            pltpu.VMEM((18, 144, 256), BF16),
            pltpu.VMEM((48, 8192), BF16),
            pltpu.VMEM((S, 4, 128, 256), BF16),
            pltpu.VMEM((128, 432), F32),
            pltpu.VMEM((TILES, 8, 128), F32),
            pltpu.VMEM((32, 8, 128), F32),
            pltpu.VMEM((8, 8, 128), F32),
            pltpu.VMEM((TILES + 2, 8, 128), F32),
            pltpu.VMEM((3, 432, 128), BF16),
            pltpu.VMEM((2, 8, 128), F32),
            pltpu.VMEM((8, 128), F32),
            pltpu.VMEM((16, 8, 128), F32),
            pltpu.VMEM((8, 8, 128), F32),
            *[dma] * 12,
            *[dma] * 6,
            *[dma] * 8,
            dma((8,)), dma((2,)),
        ],
        compiler_params=pltpu.CompilerParams(
            collective_id=0, has_side_effects=True, vmem_limit_bytes=56 * 1024 * 1024
        ),
        name="whole",
    )(
        inputs.reshape(S, 4, 8192),
        mask_one.reshape(48, 8192),
        place_one.reshape(48, 1024),
        pooled_one.reshape(48, 1024),
        w_two,
        mask_two.reshape(96, 1024),
        place_two.reshape(96, 128),
        grad_two.reshape(96, 128),
    )
    gp, w1, w2 = pl.pallas_call(
        finish,
        out_shape=(
            jax.ShapeDtypeStruct((48, 1024), BF16),
            jax.ShapeDtypeStruct((4, 16, 27), F32),
            jax.ShapeDtypeStruct((27, 16, 32), F32),
        ),
        in_specs=[vm, vm],
        out_specs=(vm, vm, vm),
        name="finish",
    )(gp, fin)
    return gp.reshape(S, 1, 16, 1024), w1.transpose(2, 0, 1), w2


def solution(mesh):
    spec = P("dp", "space", None, None)
    return jax.shard_map(
        local,
        mesh=mesh,
        in_specs=(spec, spec, spec, spec, P(), spec, spec, spec),
        out_specs=(spec, P(), P()),
        check_vma=False,
    )
```

```python
import jax
import jax.numpy as jnp
from jax import lax
from jax.experimental import pallas as pl
from jax.experimental.pallas import tpu as pltpu
from jax.sharding import PartitionSpec as P

C_IN, C_ONE, C_TWO = 4, 16, 32
BX, BY, BZ = 4, 8, 256
S = 3
MESH = pl.DeviceIdType.MESH
F32, BF16, I32 = jnp.float32, jnp.bfloat16, jnp.int32
TILES = 18
TOTAL = 6291456
NEIGHBOURS = [
    (di, dj, dk)
    for di in (-1, 0, 1)
    for dj in (-1, 0, 1)
    for dk in (-1, 0, 1)
    if (di, dj, dk) != (0, 0, 0)
]
GREETED = [(-1, 0, 0), (1, 0, 0), (0, 0, -1), (0, 0, 1)]
XY = [(di, dj) for di in (-1, 0, 1) for dj in (-1, 0, 1) if (di, dj) != (0, 0)]
NT = (((1,), (1,)), ((), ()))
NN = (((1,), (0,)), ((), ()))
TN = (((0,), (0,)), ((), ()))


def dot(a, b, dims=NN):
    return lax.dot_general(a, b, dims, preferred_element_type=F32)


def iota(shape, dim):
    return lax.broadcasted_iota(I32, shape, dim)


def one_hot(cond):
    return jnp.where(cond, 1.0, 0.0).astype(BF16)


def kernel(
    inp_h, mask_one_h, place_one_h, pooled_h, w_two_h, mask_two_h, place_two_h, grad_two_h,
    gp_h, fin_h,
    inp, mask_one, place_one, pooled, w_two, mask_two, place_two, grad_two, gp,
    mp, yb, tk, rx, ry, rt, z3, wp, pst, tbuf,
    iyb, rix, riy, in32, ko, rk, lhs, sel, gc, acc1,
    wg, r1, r2, fin, qbuf, ca, cb, cc,
    gx_send, gx_recv, gy_send, gy_recv, gt_send, gt_recv,
    ix_send, ix_recv, iy_send, iy_recv, k_send, k_recv,
    s1_send, s1_recv, s2_send, s2_recv, s3_send, s3_recv,
    s4_send, s4_recv, ta_send, ta_recv, tb_send, tb_recv, tc_send, tc_recv,
    l_sem, o_sem,
):
    dp = lax.axis_index("dp")
    sp = lax.axis_index("space")
    bi, bj, bk = sp // 16, (sp // 4) % 4, sp % 4
    zc, t8 = sp // 8, sp % 8
    men = dp * 8 + t8
    core = dp % 2
    chip = (dp // 2) * 8 + t8
    owner = ((core == 0) & (chip < 9)) | ((core == 1) & (chip >= 7))
    mine = jnp.where(core == 0, chip, chip + 2)

    def near(di, dj, dk):
        other = ((bi + di + 4) % 4) * 16 + ((bj + dj + 4) % 4) * 4 + (bk + dk + 4) % 4
        return {"space": other}

    def plane(n):
        return {"dp": n // 8, "space": zc * 8 + n % 8}

    def column(zz):
        return {"space": zz * 8 + t8}

    def twin():
        return {"dp": dp + 1 - 2 * core}

    def owner_of(o):
        n = o if o < 9 else o - 2
        return {"dp": (n // 8) * 2 + (0 if o < 9 else 1), "space": zc * 8 + n % 8}

    def is_mine(o):
        return owner & (mine == o)

    def p1(o):
        return pltpu.make_async_remote_copy(
            src_ref=wg.at[o], dst_ref=r1.at[men], send_sem=s1_send, recv_sem=s1_recv,
            device_id=owner_of(o), device_id_type=MESH,
        )

    def p2(n):
        return pltpu.make_async_remote_copy(
            src_ref=r2.at[zc], dst_ref=r2.at[zc], send_sem=s2_send, recv_sem=s2_recv,
            device_id=column((zc + n) % 8), device_id_type=MESH,
        )

    def p3(n):
        return pltpu.make_async_remote_copy(
            src_ref=fin.at[mine], dst_ref=fin.at[mine], send_sem=s3_send, recv_sem=s3_recv,
            device_id=chip_at((chip + n) % 16), device_id_type=MESH,
        )

    def p4(half):
        nine = fin.at[pl.ds(half * 9, 9)]
        return pltpu.make_async_remote_copy(
            src_ref=nine, dst_ref=nine, send_sem=s4_send, recv_sem=s4_recv,
            device_id=twin(), device_id_type=MESH,
        )

    def chip_at(n):
        return {"dp": (n // 8) * 2 + core, "space": zc * 8 + n % 8}

    y_lo, y_hi, x4 = dp // 2, t8 // 4, t8 % 4
    me_a = core * 4 + x4
    me_b = y_lo * 2 + y_hi

    def ta(n):
        a = (me_a + n) % 8
        return pltpu.make_async_remote_copy(
            src_ref=ca.at[me_a], dst_ref=ca.at[me_a], send_sem=ta_send, recv_sem=ta_recv,
            device_id={"dp": y_lo * 2 + a // 4, "space": zc * 8 + y_hi * 4 + a % 4}, device_id_type=MESH,
        )

    def tb(n):
        b = (me_b + n) % 4
        return pltpu.make_async_remote_copy(
            src_ref=cb.at[me_b], dst_ref=cb.at[me_b], send_sem=tb_send, recv_sem=tb_recv,
            device_id={"dp": (b // 2) * 2 + core, "space": zc * 8 + (b % 2) * 4 + x4}, device_id_type=MESH,
        )

    def tc_(n):
        return pltpu.make_async_remote_copy(
            src_ref=cc.at[zc], dst_ref=cc.at[zc], send_sem=tc_send, recv_sem=tc_recv,
            device_id=column((zc + n) % 8), device_id_type=MESH,
        )

    def group(ref, send_sem, recv_sem):
        return pltpu.make_async_remote_copy(
            src_ref=ref, dst_ref=ref, send_sem=send_sem, recv_sem=recv_sem,
            device_id=twin(), device_id_type=MESH,
        )

    gx_all, gy_all, gt_all = group(rx, gx_send, gx_recv), group(ry, gy_send, gy_recv), group(rt, gt_send, gt_recv)
    ix_all, iy_all, k_all = group(rix, ix_send, ix_recv), group(riy, iy_send, iy_recv), group(rk, k_send, k_recv)
    p1_got = group(r1.at[0:31], s1_send, s1_recv)
    p1_sent = group(wg.at[0 : TILES - 1], s1_send, s1_recv)
    p1_sent_all = group(wg, s1_send, s1_recv)
    p2_all = group(r2.at[0:7], s2_send, s2_recv)
    p3_sent = group(r1.at[0:15], s3_send, s3_recv)
    p3_got = group(fin.at[0:8], s3_send, s3_recv)
    p3_got_all = group(fin.at[0:9], s3_send, s3_recv)
    ta_all = group(ca.at[0:7], ta_send, ta_recv)
    tb_all = group(cb.at[0:3], tb_send, tb_recv)
    tc_all = group(cc.at[0:7], tc_send, tc_recv)

    barrier = pltpu.get_barrier_semaphore()
    for d in sorted(NEIGHBOURS, key=lambda d: -3 * abs(d[1]) - 2 * abs(d[0]) - abs(d[2])):
        if d in GREETED:
            continue
        pl.semaphore_signal(barrier, inc=1, device_id=near(*d), device_id_type=MESH)
    for n in range(1, 32):
        pl.semaphore_signal(barrier, inc=1, device_id=plane((men + n) % 32), device_id_type=MESH)
    for n in range(1, 8):
        pl.semaphore_signal(barrier, inc=1, device_id=column((zc + n) % 8), device_id_type=MESH)

    loads = [
        pltpu.make_async_copy(a, b, l_sem.at[n])
        for n, (a, b) in enumerate(
            (
                (place_two_h, place_two),
                (mask_two_h, mask_two),
                (grad_two_h, grad_two),
                (inp_h, inp),
                (w_two_h, w_two),
                (pooled_h, pooled),
                (place_one_h, place_one),
                (mask_one_h, mask_one),
            )
        )
    ]
    for c in loads:
        c.start()

    er, ec = iota((128, 768), 0), iota((128, 768), 1)
    ez = ec % 128 - (ec // 256 - 1)
    e3 = one_hot((er // 64 == (ec // 128) % 2) & (ez >= 0) & (ez < 128) & (ez // 2 == er % 64))
    e0 = e3[:, 256:512]
    for c in loads[:3]:
        c.wait()
    p_b = place_two[...].astype(F32).astype(BF16)
    p_up = dot(p_b, e0)
    par = (iota((96, 256), 1) % 2).astype(F32)
    keep = jnp.zeros((96, 256), jnp.bool_)
    for dx in range(2):
        for dy in range(2):
            tiles = [(dx * 4 + 2 * qy + dy) * 128 for qy in range(2)]
            m = jnp.concatenate([mask_two[:, t : t + 128] for t in tiles], axis=1)
            keep = keep | ((p_up == par + float(4 * dx + 2 * dy)) & (m == 1))
    kept = dot(one_hot(keep), e0, NT)
    m_f = jnp.where(kept > 0.5, grad_two[...].astype(F32), 0.0)
    p_f = p_b.astype(F32)
    m_b = m_f.astype(BF16)
    mp[0] = m_b
    mp[1] = p_b
    low = iota((96, 128), 1) < 64
    yb[0] = jnp.where(low, m_f, pltpu.roll(p_f, 64, 1)).astype(BF16)
    yb[1] = jnp.where(low, pltpu.roll(m_f, 64, 1), p_f).astype(BF16)
    tr, tc = iota((16, 128), 0), iota((16, 128), 1)
    tk[...] = jnp.zeros_like(tk)
    for side, edge in ((0, 63), (1, 0)):
        pick_m = one_hot((tr < 2) & (tc == tr * 64 + edge))
        pick_p = one_hot((tr >= 2) & (tr < 4) & (tc == (tr - 2) * 64 + edge))
        tk[side, :, 0:96] = (dot(pick_m, m_b, NT) + dot(pick_p, p_b, NT)).astype(BF16)

    loads[3].wait()
    for q, y in ((0, 0), (1, 7)):
        for x in range(4):
            at = x * 2048 + y * 256
            iyb[q, :, :, x * 256 : (x + 1) * 256] = inp[:, :, at : at + 256]

    pl.semaphore_wait(barrier, 60)

    def g_copy(n, d):
        di, dj, dk = d
        if dk != 0:
            src = tk.at[0 if dk > 0 else 1]
            dst = rt.at[(1 - di) * 3 + 1 - dj, 0 if dk > 0 else 1]
            sems = gt_send, gt_recv
        elif dj == 0:
            src, dst = mp, rx.at[(1 - di) // 2]
            sems = gx_send, gx_recv
        else:
            src = yb.at[(1 + dj) // 2]
            dst = ry.at[1 - di, (1 - dj) // 2]
            sems = gy_send, gy_recv
        return pltpu.make_async_remote_copy(
            src_ref=src, dst_ref=dst, send_sem=sems[0], recv_sem=sems[1],
            device_id=near(*d), device_id_type=MESH,
        )

    def i_copy(n, d):
        di, dj = d
        if dj == 0:
            at = 3 * 2048 if di > 0 else 0
            src, dst = inp.at[:, :, at : at + 2048], rix.at[(1 - di) // 2]
            sems = ix_send, ix_recv
        else:
            q = (1 + dj) // 2
            sems = iy_send, iy_recv
            if di == 0:
                src = iyb.at[q]
                dst = riy.at[(1 - dj) // 2, :, :, 256 : 256 + 1024]
            else:
                at = 768 if di > 0 else 0
                to = 0 if di > 0 else 1280
                src = iyb.at[q, :, :, at : at + 256]
                dst = riy.at[(1 - dj) // 2, :, :, to : to + 256]
        return pltpu.make_async_remote_copy(
            src_ref=src, dst_ref=dst, send_sem=sems[0], recv_sem=sems[1],
            device_id=near(di, dj, 0), device_id_type=MESH,
        )

    g_copies = [g_copy(n, d) for n, d in enumerate(NEIGHBOURS)]
    i_copies = [i_copy(n, d) for n, d in enumerate(XY)]
    for d, c in zip(NEIGHBOURS, g_copies):
        if d[2] != 0:
            c.start()
    for d, c in zip(NEIGHBOURS, g_copies):
        if d[2] == 0:
            c.start()
    for c in i_copies:
        c.start()

    qr, qc = iota((432, 128), 0), iota((432, 128), 1)
    for oy in range(3):
        qo = (qr // 144) * 9 + oy * 3 + (qr // 48) % 3
        qbuf[oy] = one_hot((qr % 4 == qc // 32) & (qc % 32 == qo) & (qr % 48 < 40))
    for c in loads[4:]:
        c.wait()
    for o9 in range(9):
        wp[o9 * 16 : o9 * 16 + 16, :] = jnp.concatenate(
            [w_two[o9 * 3 + b].astype(F32) for b in range(3)], axis=1
        ).astype(BF16)
    pst[...] = jnp.zeros_like(pst)
    for ox in range(3):
        for oy in range(3):
            o9 = ox * 3 + oy
            for qx in range(2):
                for qy in range(4):
                    to = ((qx + 2 - ox) * 6 + qy + 2 - oy) * 128
                    at = (qx * 4 + qy) * 128
                    for s in range(S):
                        pst[s, o9 * 16 : o9 * 16 + 16, to : to + 128] = pooled[
                            s * 16 : s * 16 + 16, at : at + 128
                        ]
    e1r, e1c = iota((128, 256), 0), iota((128, 256), 1)
    e1 = one_hot(e1c // 2 == e1r)
    par1 = (iota((48, 256), 1) % 2).astype(F32)
    for hx in range(2):
        for hy in range(4):
            at = (hx * 4 + hy) * 128
            up = dot(place_one[:, at : at + 128].astype(F32).astype(BF16), e1)
            for dx in range(2):
                for dy in range(2):
                    to = ((2 * hx + dx) * 8 + 2 * hy + dy) * 256
                    ok = (up == par1 + float(4 * dx + 2 * dy)) & (mask_one[:, to : to + 256] == 1)
                    sel[:, to : to + 256] = one_hot(ok)

    fr, fc = iota((32, 768), 0), iota((32, 768), 1)
    f_in, f_mid, f_b = fc % 128, (fc // 128) % 2, fc // 256
    left = (f_b == 2) & (f_in == 0)
    right = (f_b == 0) & (f_in == 127)

    def halo_rows(row):
        return one_hot((left & (fr == row)) | (right & (fr == 16 + row)))

    f_m, f_p = halo_rows(f_mid), halo_rows(2 + f_mid)
    f_y = [halo_rows(2 * f_mid + q) for q in range(2)]
    lane = (iota((96, 128), 1) % 2).astype(F32)
    dz = [1.0 - lane, lane, 1.0 - lane]
    gt_all.wait_recv()

    def put(b, x, y, dx, dy, um, up):
        v = jnp.where(up == dz[b] + float(4 * dx + 2 * dy), um, 0.0).astype(BF16)
        to = (x * 6 + y) * 128
        for s in range(S):
            z3[s, b * 32 : b * 32 + 32, to : to + 128] = v[s * 32 : s * 32 + 32]

    for dj in (0, -1, 1):
        if dj == -1:
            gy_all.wait_recv()
        for di in (0, -1, 1):
            if dj == 0 and di == -1:
                gx_all.wait_recv()
            stack = rt[(di + 1) * 3 + dj + 1].reshape(32, 128)[:, 0:96]
            xs = {-1: [(0, 1)], 0: [(1, 0), (2, 1)], 1: [(3, 0)]}[di]
            if dj == 0:
                ref = mp if di == 0 else rx.at[(di + 1) // 2]
                um = dot(ref[0], e3) + dot(stack, f_m, TN)
                up = dot(ref[1], e3) + dot(stack, f_p, TN)
                for b in range(3):
                    for qy in range(2):
                        at = (b * 2 + qy) * 128
                        for x, dx in xs:
                            for dy in range(2):
                                put(b, x, 1 + 2 * qy + dy, dx, dy, um[:, at : at + 128], up[:, at : at + 128])
            else:
                q = 1 if dj < 0 else 0
                u = dot(ry[di + 1, (dj + 1) // 2], e3) + dot(stack, f_y[q], TN)
                for b in range(3):
                    at = b * 256
                    for x, dx in xs:
                        put(b, x, 0 if dj < 0 else 5, dx, q, u[:, at : at + 128], u[:, at + 128 : at + 256])

    w2 = jnp.zeros((144, 96), F32)
    for s in range(S):
        w2 = w2 + dot(pst[s], z3[s], NT)
    w2 = jnp.concatenate([w2, jnp.zeros((144, 32), F32)], axis=1)
    for i in range(TILES):
        wg[i] = w2[i * 8 : i * 8 + 8]
    for o in range(TILES):
        @pl.when(~is_mine(o))
        def _():
            p1(o).start()

    for s in range(S):
        for x in range(4):
            tbuf[:, x * 768 : x * 768 + 768] = dot(wp[...], z3[s, :, x * 768 : x * 768 + 768])
        for x in range(2):
            for y in range(4):
                a = jnp.zeros((16, 128), F32)
                for ox in range(3):
                    for oy in range(3):
                        r = (ox * 3 + oy) * 16
                        at = ((x + 2 - ox) * 6 + y + 2 - oy) * 128
                        a = a + tbuf[r : r + 16, at : at + 128]
                gp[s * 16 : s * 16 + 16, (x * 4 + y) * 128 : (x * 4 + y) * 128 + 128] = a.astype(BF16)
    gp_copy = pltpu.make_async_copy(gp, gp_h, o_sem.at[0])
    gp_copy.start()

    for c in (ix_all, iy_all):
        c.wait_recv()
    in32[...] = jnp.zeros_like(in32)
    for s in range(S):
        for x in range(6):
            for y in range(10):
                if 1 <= y <= 8:
                    if 1 <= x <= 4:
                        at = ((x - 1) * 8 + y - 1) * 256
                        v = inp[s, :, at : at + 256]
                    else:
                        at = (y - 1) * 256
                        v = rix[0 if x == 0 else 1, s, :, at : at + 256]
                else:
                    v = riy[0 if y == 0 else 1, s, :, x * 256 : x * 256 + 256]
                in32[s * 6 + x, 4 * y : 4 * y + 4, :] = v.astype(F32)
    lane48 = iota((48, 128), 1)
    for side in range(2):
        o = jnp.zeros((48, 128), F32)
        for l in range(18):
            tile = in32[l, :, 128:256] if side == 0 else in32[l, :, 0:128]
            edge = 127 if side == 0 else 0
            o = jnp.where(lane48 == l, pltpu.roll(tile, (l - edge) % 128, 1), o)
        ko[side] = o

    def k_copy(side):
        return pltpu.make_async_remote_copy(
            src_ref=ko.at[side], dst_ref=rk.at[side],
            send_sem=k_send, recv_sem=k_recv,
            device_id=near(0, 0, 1 if side == 0 else -1), device_id_type=MESH,
        )

    k_copies = [k_copy(0), k_copy(1)]
    for c in k_copies:
        c.start()

    for hx in range(2):
        for hy in range(4):
            at = (hx * 4 + hy) * 128
            up = dot(gp[:, at : at + 128], e1)
            for dx in range(2):
                for dy in range(2):
                    x, y = 2 * hx + dx, 2 * hy + dy
                    to = (x * 8 + y) * 256
                    v = (up * sel[:, to : to + 256].astype(F32)).astype(BF16)
                    for s in range(S):
                        gc[s, x, y * 16 : y * 16 + 16, :] = v[s * 16 : s * 16 + 16]
    @pl.when(owner)
    def _():
        p1_got.wait_recv()
        r1[men] = wg[mine]
        total = r1[0]
        for n in range(1, 32):
            total = total + r1[n]
        r2[zc] = total
        for n in range(1, 8):
            p2(n).start()

    k_all.wait_recv()
    lane256 = iota((48, 256), 1)
    for l in range(18):
        v = in32[l]
        below = jnp.concatenate([pltpu.roll(rk[0], (0 - l) % 128, 1), jnp.zeros((48, 128), F32)], axis=1)
        above = jnp.concatenate([jnp.zeros((48, 128), F32), pltpu.roll(rk[1], (127 - l) % 128, 1)], axis=1)
        lhs[l, 0:48, :] = jnp.where(lane256 == 0, below, pltpu.roll(v, 1, 1)).astype(BF16)
        lhs[l, 48:96, :] = v.astype(BF16)
        lhs[l, 96:144, :] = jnp.where(lane256 == 255, above, pltpu.roll(v, 255, 1)).astype(BF16)

    a1 = jnp.zeros((128, 432), F32)
    for s in range(S):
        for x in range(4):
            three = lhs[s * 6 + x : s * 6 + x + 3].reshape(432, 256)
            a1 = a1 + dot(gc[s, x], three, NT)
    acc1[...] = a1
    y_lane = (iota((16, 432), 1) % 48) // 4
    parts = []
    for oy in range(3):
        t = jnp.zeros((16, 432), F32)
        for y in range(8):
            t = t + jnp.where(y_lane == y + oy, acc1[y * 16 : y * 16 + 16, :], 0.0)
        parts.append(t)
    w1 = jnp.zeros((16, 128), F32)
    for oy in range(3):
        t = parts[oy]
        hi = t.astype(BF16)
        t = t - hi.astype(F32)
        mid = t.astype(BF16)
        low_part = (t - mid.astype(F32)).astype(BF16)
        r = dot(jnp.concatenate([hi, mid, low_part], axis=0), qbuf[oy])
        w1 = w1 + (r[0:16] + r[16:32] + r[32:48])
    ca[me_a, 0] = w1[0:8]
    ca[me_a, 1] = w1[8:16]
    for n in range(1, 8):
        ta(n).start()

    @pl.when(owner)
    def _():
        p2_all.wait_recv()
        total = r2[0]
        for zz in range(1, 8):
            total = total + r2[zz]
        fin[mine] = total
        for n in range(1, 16):
            p3(n).start()

    ta_all.wait_recv()
    total = ca[0]
    for n in range(1, 8):
        total = total + ca[n]
    cb[me_b] = total
    for n in range(1, 4):
        tb(n).start()
    tb_all.wait_recv()
    total = cb[0]
    for n in range(1, 4):
        total = total + cb[n]
    cc[zc] = total
    for n in range(1, 8):
        tc_(n).start()

    @pl.when(owner)
    def _():
        p3_got.wait_recv()

    @pl.when(~owner)
    def _():
        p3_got_all.wait_recv()

    p4(core).start()
    tc_all.wait_recv()
    total = cc[0]
    for n in range(1, 8):
        total = total + cc[n]
    fin[TILES] = total[0]
    fin[TILES + 1] = total[1]
    p4(1 - core).wait_recv()
    fin_copy = pltpu.make_async_copy(fin, fin_h, o_sem.at[1])
    fin_copy.start()

    for c in (gt_all, gx_all, gy_all, ix_all, iy_all, k_all, ta_all, tb_all, tc_all):
        c.wait_send()
    p4(core).wait_send()

    @pl.when(owner)
    def _():
        p1_sent.wait_send()
        p2_all.wait_send()
        p3_sent.wait_send()

    @pl.when(~owner)
    def _():
        p1_sent_all.wait_send()

    gp_copy.wait()
    fin_copy.wait()


def finish(gp, fin, gp_out, w1_out, w2_out):
    gp_out[...] = gp[...]
    for o9 in range(9):
        for h in range(2):
            v = fin[2 * o9 + h] * (float(TOTAL // 8) ** -0.5)
            for b in range(3):
                w2_out[o9 * 3 + b, h * 8 : h * 8 + 8, :] = v[:, b * 32 : b * 32 + 32]
    for i in range(2):
        v = fin[TILES + i] * (float(TOTAL) ** -0.5)
        for c in range(4):
            w1_out[c, i * 8 : i * 8 + 8, :] = v[:, c * 32 : c * 32 + 27]


def local(inputs, mask_one, place_one, pooled_one, w_two, mask_two, place_two, grad_two):
    vm = pl.BlockSpec(memory_space=pltpu.VMEM)
    anywhere = pl.BlockSpec(memory_space=pl.ANY)
    dma = pltpu.SemaphoreType.DMA
    gp, fin = pl.pallas_call(
        kernel,
        out_shape=(
            jax.ShapeDtypeStruct((48, 1024), BF16),
            jax.ShapeDtypeStruct((TILES + 2, 8, 128), F32),
        ),
        in_specs=[anywhere] * 8,
        out_specs=(anywhere, anywhere),
        scratch_shapes=[
            pltpu.VMEM((S, 4, 8192), BF16),
            pltpu.VMEM((48, 8192), I32),
            pltpu.VMEM((48, 1024), I32),
            pltpu.VMEM((48, 1024), BF16),
            pltpu.VMEM((27, 16, 32), BF16),
            pltpu.VMEM((96, 1024), I32),
            pltpu.VMEM((96, 128), I32),
            pltpu.VMEM((96, 128), BF16),
            pltpu.VMEM((48, 1024), BF16),
            pltpu.VMEM((2, 96, 128), BF16),
            pltpu.VMEM((2, 96, 128), BF16),
            pltpu.VMEM((2, 16, 128), BF16),
            pltpu.VMEM((2, 2, 96, 128), BF16),
            pltpu.VMEM((3, 2, 96, 128), BF16),
            pltpu.VMEM((9, 2, 16, 128), BF16),
            pltpu.VMEM((S, 96, 3072), BF16),
            pltpu.VMEM((144, 96), BF16),
            pltpu.VMEM((S, 144, 3072), BF16),
            pltpu.VMEM((144, 3072), F32),
            pltpu.VMEM((2, S, 4, 1024), BF16),
            pltpu.VMEM((2, S, 4, 2048), BF16),
            pltpu.VMEM((2, S, 4, 1536), BF16),
            pltpu.VMEM((18, 48, 256), F32),
            pltpu.VMEM((2, 48, 128), F32),
            pltpu.VMEM((2, 48, 128), F32),
            pltpu.VMEM((18, 144, 256), BF16),
            pltpu.VMEM((48, 8192), BF16),
            pltpu.VMEM((S, 4, 128, 256), BF16),
            pltpu.VMEM((128, 432), F32),
            pltpu.VMEM((TILES, 8, 128), F32),
            pltpu.VMEM((32, 8, 128), F32),
            pltpu.VMEM((8, 8, 128), F32),
            pltpu.VMEM((TILES + 2, 8, 128), F32),
            pltpu.VMEM((3, 432, 128), BF16),
            pltpu.VMEM((8, 2, 8, 128), F32),
            pltpu.VMEM((4, 2, 8, 128), F32),
            pltpu.VMEM((8, 2, 8, 128), F32),
            *[dma] * 12,
            *[dma] * 6,
            *[dma] * 8,
            dma((8,)), dma((2,)),
        ],
        compiler_params=pltpu.CompilerParams(
            collective_id=0, has_side_effects=True, vmem_limit_bytes=56 * 1024 * 1024
        ),
        name="whole",
    )(
        inputs.reshape(S, 4, 8192),
        mask_one.reshape(48, 8192),
        place_one.reshape(48, 1024),
        pooled_one.reshape(48, 1024),
        w_two,
        mask_two.reshape(96, 1024),
        place_two.reshape(96, 128),
        grad_two.reshape(96, 128),
    )
    gp, w1, w2 = pl.pallas_call(
        finish,
        out_shape=(
            jax.ShapeDtypeStruct((48, 1024), BF16),
            jax.ShapeDtypeStruct((4, 16, 27), F32),
            jax.ShapeDtypeStruct((27, 16, 32), F32),
        ),
        in_specs=[vm, vm],
        out_specs=(vm, vm, vm),
        name="finish",
    )(gp, fin)
    return gp.reshape(S, 1, 16, 1024), w1.transpose(2, 0, 1), w2


def solution(mesh):
    spec = P("dp", "space", None, None)
    return jax.shard_map(
        local,
        mesh=mesh,
        in_specs=(spec, spec, spec, spec, P(), spec, spec, spec),
        out_specs=(spec, P(), P()),
        check_vma=False,
    )
```

```python
import jax
import jax.numpy as jnp
from jax import lax
from jax.experimental import pallas as pl
from jax.experimental.pallas import tpu as pltpu
from jax.sharding import PartitionSpec as P

C_IN, C_ONE, C_TWO = 4, 16, 32
BX, BY, BZ = 4, 8, 256
S = 3
MESH = pl.DeviceIdType.MESH
F32, BF16, I32 = jnp.float32, jnp.bfloat16, jnp.int32
TILES = 18
TOTAL = 6291456
NEIGHBOURS = [
    (di, dj, dk)
    for di in (-1, 0, 1)
    for dj in (-1, 0, 1)
    for dk in (-1, 0, 1)
    if (di, dj, dk) != (0, 0, 0)
]
GREETED = [(-1, 0, 0), (1, 0, 0), (0, 0, -1), (0, 0, 1)]
XY = [(di, dj) for di in (-1, 0, 1) for dj in (-1, 0, 1) if (di, dj) != (0, 0)]
NT = (((1,), (1,)), ((), ()))
NN = (((1,), (0,)), ((), ()))
TN = (((0,), (0,)), ((), ()))


def dot(a, b, dims=NN):
    return lax.dot_general(a, b, dims, preferred_element_type=F32)


def iota(shape, dim):
    return lax.broadcasted_iota(I32, shape, dim)


def one_hot(cond):
    return jnp.where(cond, 1.0, 0.0).astype(BF16)


def kernel(
    inp_h, mask_one_h, place_one_h, pooled_h, w_two_h, mask_two_h, place_two_h, grad_two_h,
    gp_h, fin_h,
    inp, mask_one, place_one, pooled, w_two, mask_two, place_two, grad_two, gp,
    mp, yb, tk, rx, ry, rt, z3, wp, pst, tbuf,
    iyb, rix, riy, in32, ko, rk, lhs, sel, gc, acc1,
    wg, r1, r2, fin, qbuf, own1, c1, c2, c3,
    gx_send, gx_recv, gy_send, gy_recv, gt_send, gt_recv,
    ix_send, ix_recv, iy_send, iy_recv, k_send, k_recv,
    s1_send, s1_recv, s2_send, s2_recv, s3_send, s3_recv,
    s4_send, s4_recv, ta_send, ta_recv, tb_send, tb_recv, tc_send, tc_recv,
    l_sem, o_sem,
):
    dp = lax.axis_index("dp")
    sp = lax.axis_index("space")
    bi, bj, bk = sp // 16, (sp // 4) % 4, sp % 4
    zc, t8 = sp // 8, sp % 8
    men = dp * 8 + t8
    core = dp % 2
    chip = (dp // 2) * 8 + t8
    owner = ((core == 0) & (chip < 9)) | ((core == 1) & (chip >= 7))
    mine = jnp.where(core == 0, chip, chip + 2)

    def near(di, dj, dk):
        other = ((bi + di + 4) % 4) * 16 + ((bj + dj + 4) % 4) * 4 + (bk + dk + 4) % 4
        return {"space": other}

    def plane(n):
        return {"dp": n // 8, "space": zc * 8 + n % 8}

    def column(zz):
        return {"space": zz * 8 + t8}

    def twin():
        return {"dp": dp + 1 - 2 * core}

    def owner_of(o):
        n = o if o < 9 else o - 2
        return {"dp": (n // 8) * 2 + (0 if o < 9 else 1), "space": zc * 8 + n % 8}

    def is_mine(o):
        return owner & (mine == o)

    def p1(o):
        return pltpu.make_async_remote_copy(
            src_ref=wg.at[o], dst_ref=r1.at[men], send_sem=s1_send, recv_sem=s1_recv,
            device_id=owner_of(o), device_id_type=MESH,
        )

    def p2(n):
        return pltpu.make_async_remote_copy(
            src_ref=r2.at[zc], dst_ref=r2.at[zc], send_sem=s2_send, recv_sem=s2_recv,
            device_id=column((zc + n) % 8), device_id_type=MESH,
        )

    def p3(n):
        return pltpu.make_async_remote_copy(
            src_ref=fin.at[mine], dst_ref=fin.at[mine], send_sem=s3_send, recv_sem=s3_recv,
            device_id=chip_at((chip + n) % 16), device_id_type=MESH,
        )

    def p4(half):
        nine = fin.at[pl.ds(half * 9, 9)]
        return pltpu.make_async_remote_copy(
            src_ref=nine, dst_ref=nine, send_sem=s4_send, recv_sem=s4_recv,
            device_id=twin(), device_id_type=MESH,
        )

    def chip_at(n):
        return {"dp": (n // 8) * 2 + core, "space": zc * 8 + n % 8}

    def t1():
        return pltpu.make_async_remote_copy(
            src_ref=own1.at[1 - core], dst_ref=c1, send_sem=ta_send, recv_sem=ta_recv,
            device_id=twin(), device_id_type=MESH,
        )

    def t2(n):
        return pltpu.make_async_remote_copy(
            src_ref=c2.at[chip], dst_ref=c2.at[chip], send_sem=tb_send, recv_sem=tb_recv,
            device_id=chip_at((chip + n) % 16), device_id_type=MESH,
        )

    def t3(n, to):
        return pltpu.make_async_remote_copy(
            src_ref=c3.at[core, zc], dst_ref=c3.at[core, zc], send_sem=tc_send, recv_sem=tc_recv,
            device_id={"dp": to, "space": ((zc + n) % 8) * 8 + t8}, device_id_type=MESH,
        )

    def group(ref, send_sem, recv_sem):
        return pltpu.make_async_remote_copy(
            src_ref=ref, dst_ref=ref, send_sem=send_sem, recv_sem=recv_sem,
            device_id=twin(), device_id_type=MESH,
        )

    gx_all, gy_all, gt_all = group(rx, gx_send, gx_recv), group(ry, gy_send, gy_recv), group(rt, gt_send, gt_recv)
    ix_all, iy_all, k_all = group(rix, ix_send, ix_recv), group(riy, iy_send, iy_recv), group(rk, k_send, k_recv)
    p1_got = group(r1.at[0:31], s1_send, s1_recv)
    p1_sent = group(wg.at[0 : TILES - 1], s1_send, s1_recv)
    p1_sent_all = group(wg, s1_send, s1_recv)
    p2_all = group(r2.at[0:7], s2_send, s2_recv)
    p3_sent = group(r1.at[0:15], s3_send, s3_recv)
    p3_got = group(fin.at[0:8], s3_send, s3_recv)
    p3_got_all = group(fin.at[0:9], s3_send, s3_recv)
    t2_all = group(c2.at[0:15], tb_send, tb_recv)
    t3_all = group(c2.at[0:15], tc_send, tc_recv)

    barrier = pltpu.get_barrier_semaphore()
    for d in sorted(NEIGHBOURS, key=lambda d: -3 * abs(d[1]) - 2 * abs(d[0]) - abs(d[2])):
        if d in GREETED:
            continue
        pl.semaphore_signal(barrier, inc=1, device_id=near(*d), device_id_type=MESH)
    for n in range(1, 32):
        pl.semaphore_signal(barrier, inc=1, device_id=plane((men + n) % 32), device_id_type=MESH)
    for n in range(1, 8):
        pl.semaphore_signal(barrier, inc=1, device_id=column((zc + n) % 8), device_id_type=MESH)
        other = {"dp": dp + 1 - 2 * core, "space": ((zc + n) % 8) * 8 + t8}
        pl.semaphore_signal(barrier, inc=1, device_id=other, device_id_type=MESH)

    loads = [
        pltpu.make_async_copy(a, b, l_sem.at[n])
        for n, (a, b) in enumerate(
            (
                (place_two_h, place_two),
                (mask_two_h, mask_two),
                (grad_two_h, grad_two),
                (inp_h, inp),
                (w_two_h, w_two),
                (pooled_h, pooled),
                (place_one_h, place_one),
                (mask_one_h, mask_one),
            )
        )
    ]
    for c in loads:
        c.start()

    er, ec = iota((128, 768), 0), iota((128, 768), 1)
    ez = ec % 128 - (ec // 256 - 1)
    e3 = one_hot((er // 64 == (ec // 128) % 2) & (ez >= 0) & (ez < 128) & (ez // 2 == er % 64))
    e0 = e3[:, 256:512]
    for c in loads[:3]:
        c.wait()
    p_b = place_two[...].astype(F32).astype(BF16)
    p_up = dot(p_b, e0)
    par = (iota((96, 256), 1) % 2).astype(F32)
    keep = jnp.zeros((96, 256), jnp.bool_)
    for dx in range(2):
        for dy in range(2):
            tiles = [(dx * 4 + 2 * qy + dy) * 128 for qy in range(2)]
            m = jnp.concatenate([mask_two[:, t : t + 128] for t in tiles], axis=1)
            keep = keep | ((p_up == par + float(4 * dx + 2 * dy)) & (m == 1))
    kept = dot(one_hot(keep), e0, NT)
    m_f = jnp.where(kept > 0.5, grad_two[...].astype(F32), 0.0)
    p_f = p_b.astype(F32)
    m_b = m_f.astype(BF16)
    mp[0] = m_b
    mp[1] = p_b
    low = iota((96, 128), 1) < 64
    yb[0] = jnp.where(low, m_f, pltpu.roll(p_f, 64, 1)).astype(BF16)
    yb[1] = jnp.where(low, pltpu.roll(m_f, 64, 1), p_f).astype(BF16)
    tr, tc = iota((16, 128), 0), iota((16, 128), 1)
    tk[...] = jnp.zeros_like(tk)
    for side, edge in ((0, 63), (1, 0)):
        pick_m = one_hot((tr < 2) & (tc == tr * 64 + edge))
        pick_p = one_hot((tr >= 2) & (tr < 4) & (tc == (tr - 2) * 64 + edge))
        tk[side, :, 0:96] = (dot(pick_m, m_b, NT) + dot(pick_p, p_b, NT)).astype(BF16)

    loads[3].wait()
    for q, y in ((0, 0), (1, 7)):
        for x in range(4):
            at = x * 2048 + y * 256
            iyb[q, :, :, x * 256 : (x + 1) * 256] = inp[:, :, at : at + 256]

    pl.semaphore_wait(barrier, 67)

    def g_copy(n, d):
        di, dj, dk = d
        if dk != 0:
            src = tk.at[0 if dk > 0 else 1]
            dst = rt.at[(1 - di) * 3 + 1 - dj, 0 if dk > 0 else 1]
            sems = gt_send, gt_recv
        elif dj == 0:
            src, dst = mp, rx.at[(1 - di) // 2]
            sems = gx_send, gx_recv
        else:
            src = yb.at[(1 + dj) // 2]
            dst = ry.at[1 - di, (1 - dj) // 2]
            sems = gy_send, gy_recv
        return pltpu.make_async_remote_copy(
            src_ref=src, dst_ref=dst, send_sem=sems[0], recv_sem=sems[1],
            device_id=near(*d), device_id_type=MESH,
        )

    def i_copy(n, d):
        di, dj = d
        if dj == 0:
            at = 3 * 2048 if di > 0 else 0
            src, dst = inp.at[:, :, at : at + 2048], rix.at[(1 - di) // 2]
            sems = ix_send, ix_recv
        else:
            q = (1 + dj) // 2
            sems = iy_send, iy_recv
            if di == 0:
                src = iyb.at[q]
                dst = riy.at[(1 - dj) // 2, :, :, 256 : 256 + 1024]
            else:
                at = 768 if di > 0 else 0
                to = 0 if di > 0 else 1280
                src = iyb.at[q, :, :, at : at + 256]
                dst = riy.at[(1 - dj) // 2, :, :, to : to + 256]
        return pltpu.make_async_remote_copy(
            src_ref=src, dst_ref=dst, send_sem=sems[0], recv_sem=sems[1],
            device_id=near(di, dj, 0), device_id_type=MESH,
        )

    g_copies = [g_copy(n, d) for n, d in enumerate(NEIGHBOURS)]
    i_copies = [i_copy(n, d) for n, d in enumerate(XY)]
    for d, c in zip(NEIGHBOURS, g_copies):
        if d[2] != 0:
            c.start()
    for d, c in zip(NEIGHBOURS, g_copies):
        if d[2] == 0:
            c.start()
    for c in i_copies:
        c.start()

    qr, qc = iota((432, 128), 0), iota((432, 128), 1)
    for oy in range(3):
        qo = (qr // 144) * 9 + oy * 3 + (qr // 48) % 3
        qbuf[oy] = one_hot((qr % 4 == qc // 32) & (qc % 32 == qo) & (qr % 48 < 40))
    for c in loads[4:]:
        c.wait()
    for o9 in range(9):
        wp[o9 * 16 : o9 * 16 + 16, :] = jnp.concatenate(
            [w_two[o9 * 3 + b].astype(F32) for b in range(3)], axis=1
        ).astype(BF16)
    pst[...] = jnp.zeros_like(pst)
    for ox in range(3):
        for oy in range(3):
            o9 = ox * 3 + oy
            for qx in range(2):
                for qy in range(4):
                    to = ((qx + 2 - ox) * 6 + qy + 2 - oy) * 128
                    at = (qx * 4 + qy) * 128
                    for s in range(S):
                        pst[s, o9 * 16 : o9 * 16 + 16, to : to + 128] = pooled[
                            s * 16 : s * 16 + 16, at : at + 128
                        ]
    e1r, e1c = iota((128, 256), 0), iota((128, 256), 1)
    e1 = one_hot(e1c // 2 == e1r)
    par1 = (iota((48, 256), 1) % 2).astype(F32)
    for hx in range(2):
        for hy in range(4):
            at = (hx * 4 + hy) * 128
            up = dot(place_one[:, at : at + 128].astype(F32).astype(BF16), e1)
            for dx in range(2):
                for dy in range(2):
                    to = ((2 * hx + dx) * 8 + 2 * hy + dy) * 256
                    ok = (up == par1 + float(4 * dx + 2 * dy)) & (mask_one[:, to : to + 256] == 1)
                    sel[:, to : to + 256] = one_hot(ok)

    fr, fc = iota((32, 768), 0), iota((32, 768), 1)
    f_in, f_mid, f_b = fc % 128, (fc // 128) % 2, fc // 256
    left = (f_b == 2) & (f_in == 0)
    right = (f_b == 0) & (f_in == 127)

    def halo_rows(row):
        return one_hot((left & (fr == row)) | (right & (fr == 16 + row)))

    f_m, f_p = halo_rows(f_mid), halo_rows(2 + f_mid)
    f_y = [halo_rows(2 * f_mid + q) for q in range(2)]
    lane = (iota((96, 128), 1) % 2).astype(F32)
    dz = [1.0 - lane, lane, 1.0 - lane]
    gt_all.wait_recv()

    def put(b, x, y, dx, dy, um, up):
        v = jnp.where(up == dz[b] + float(4 * dx + 2 * dy), um, 0.0).astype(BF16)
        to = (x * 6 + y) * 128
        for s in range(S):
            z3[s, b * 32 : b * 32 + 32, to : to + 128] = v[s * 32 : s * 32 + 32]

    for dj in (0, -1, 1):
        if dj == -1:
            gy_all.wait_recv()
        for di in (0, -1, 1):
            if dj == 0 and di == -1:
                gx_all.wait_recv()
            stack = rt[(di + 1) * 3 + dj + 1].reshape(32, 128)[:, 0:96]
            xs = {-1: [(0, 1)], 0: [(1, 0), (2, 1)], 1: [(3, 0)]}[di]
            if dj == 0:
                ref = mp if di == 0 else rx.at[(di + 1) // 2]
                um = dot(ref[0], e3) + dot(stack, f_m, TN)
                up = dot(ref[1], e3) + dot(stack, f_p, TN)
                for b in range(3):
                    for qy in range(2):
                        at = (b * 2 + qy) * 128
                        for x, dx in xs:
                            for dy in range(2):
                                put(b, x, 1 + 2 * qy + dy, dx, dy, um[:, at : at + 128], up[:, at : at + 128])
            else:
                q = 1 if dj < 0 else 0
                u = dot(ry[di + 1, (dj + 1) // 2], e3) + dot(stack, f_y[q], TN)
                for b in range(3):
                    at = b * 256
                    for x, dx in xs:
                        put(b, x, 0 if dj < 0 else 5, dx, q, u[:, at : at + 128], u[:, at + 128 : at + 256])

    w2 = jnp.zeros((144, 96), F32)
    for s in range(S):
        w2 = w2 + dot(pst[s], z3[s], NT)
    w2 = jnp.concatenate([w2, jnp.zeros((144, 32), F32)], axis=1)
    for i in range(TILES):
        wg[i] = w2[i * 8 : i * 8 + 8]
    for o in range(TILES):
        @pl.when(~is_mine(o))
        def _():
            p1(o).start()

    for s in range(S):
        for x in range(4):
            tbuf[:, x * 768 : x * 768 + 768] = dot(wp[...], z3[s, :, x * 768 : x * 768 + 768])
        for x in range(2):
            for y in range(4):
                a = jnp.zeros((16, 128), F32)
                for ox in range(3):
                    for oy in range(3):
                        r = (ox * 3 + oy) * 16
                        at = ((x + 2 - ox) * 6 + y + 2 - oy) * 128
                        a = a + tbuf[r : r + 16, at : at + 128]
                gp[s * 16 : s * 16 + 16, (x * 4 + y) * 128 : (x * 4 + y) * 128 + 128] = a.astype(BF16)
    gp_copy = pltpu.make_async_copy(gp, gp_h, o_sem.at[0])
    gp_copy.start()

    for c in (ix_all, iy_all):
        c.wait_recv()
    in32[...] = jnp.zeros_like(in32)
    for s in range(S):
        for x in range(6):
            for y in range(10):
                if 1 <= y <= 8:
                    if 1 <= x <= 4:
                        at = ((x - 1) * 8 + y - 1) * 256
                        v = inp[s, :, at : at + 256]
                    else:
                        at = (y - 1) * 256
                        v = rix[0 if x == 0 else 1, s, :, at : at + 256]
                else:
                    v = riy[0 if y == 0 else 1, s, :, x * 256 : x * 256 + 256]
                in32[s * 6 + x, 4 * y : 4 * y + 4, :] = v.astype(F32)
    lane48 = iota((48, 128), 1)
    for side in range(2):
        o = jnp.zeros((48, 128), F32)
        for l in range(18):
            tile = in32[l, :, 128:256] if side == 0 else in32[l, :, 0:128]
            edge = 127 if side == 0 else 0
            o = jnp.where(lane48 == l, pltpu.roll(tile, (l - edge) % 128, 1), o)
        ko[side] = o.astype(BF16)

    def k_copy(side):
        return pltpu.make_async_remote_copy(
            src_ref=ko.at[side], dst_ref=rk.at[side],
            send_sem=k_send, recv_sem=k_recv,
            device_id=near(0, 0, 1 if side == 0 else -1), device_id_type=MESH,
        )

    k_copies = [k_copy(0), k_copy(1)]
    for c in k_copies:
        c.start()

    for hx in range(2):
        for hy in range(4):
            at = (hx * 4 + hy) * 128
            up = dot(gp[:, at : at + 128], e1)
            for dx in range(2):
                for dy in range(2):
                    x, y = 2 * hx + dx, 2 * hy + dy
                    to = (x * 8 + y) * 256
                    v = (up * sel[:, to : to + 256].astype(F32)).astype(BF16)
                    for s in range(S):
                        gc[s, x, y * 16 : y * 16 + 16, :] = v[s * 16 : s * 16 + 16]
    k_all.wait_recv()
    lane256 = iota((48, 256), 1)
    edge_below, edge_above = rk[0].astype(F32), rk[1].astype(F32)
    for l in range(18):
        v = in32[l]
        below = jnp.concatenate([pltpu.roll(edge_below, (0 - l) % 128, 1), jnp.zeros((48, 128), F32)], axis=1)
        above = jnp.concatenate([jnp.zeros((48, 128), F32), pltpu.roll(edge_above, (127 - l) % 128, 1)], axis=1)
        lhs[l, 0:48, :] = jnp.where(lane256 == 0, below, pltpu.roll(v, 1, 1)).astype(BF16)
        lhs[l, 48:96, :] = v.astype(BF16)
        lhs[l, 96:144, :] = jnp.where(lane256 == 255, above, pltpu.roll(v, 255, 1)).astype(BF16)

    a1 = jnp.zeros((128, 432), F32)
    for s in range(S):
        for x in range(4):
            three = lhs[s * 6 + x : s * 6 + x + 3].reshape(432, 256)
            a1 = a1 + dot(gc[s, x], three, NT)
    acc1[...] = a1
    y_lane = (iota((16, 432), 1) % 48) // 4
    parts = []
    for oy in range(3):
        t = jnp.zeros((16, 432), F32)
        for y in range(8):
            t = t + jnp.where(y_lane == y + oy, acc1[y * 16 : y * 16 + 16, :], 0.0)
        parts.append(t)
    w1 = jnp.zeros((16, 128), F32)
    for oy in range(3):
        t = parts[oy]
        hi = t.astype(BF16)
        t = t - hi.astype(F32)
        mid = t.astype(BF16)
        low_part = (t - mid.astype(F32)).astype(BF16)
        r = dot(jnp.concatenate([hi, mid, low_part], axis=0), qbuf[oy])
        w1 = w1 + (r[0:16] + r[16:32] + r[32:48])
    own1[0] = w1[0:8]
    own1[1] = w1[8:16]
    t1().start()

    @pl.when(owner)
    def _():
        p1_got.wait_recv()
        r1[men] = wg[mine]
        total = r1[0]
        for n in range(1, 32):
            total = total + r1[n]
        r2[zc] = total
        for n in range(1, 8):
            p2(n).start()

    t1().wait_recv()
    c2[chip] = own1[core] + c1[...]
    for n in range(1, 16):
        t2(n).start()

    @pl.when(owner)
    def _():
        p2_all.wait_recv()
        total = r2[0]
        for zz in range(1, 8):
            total = total + r2[zz]
        fin[mine] = total
        for n in range(1, 16):
            p3(n).start()

    t2_all.wait_recv()
    total = c2[0]
    for n in range(1, 16):
        total = total + c2[n]
    c3[core, zc] = total
    for n in range(1, 8):
        t3(n, dp).start()
    t3(0, dp + 1 - 2 * core).start()
    for n in range(1, 8):
        t3(n, dp + 1 - 2 * core).start()

    @pl.when(owner)
    def _():
        p3_got.wait_recv()

    @pl.when(~owner)
    def _():
        p3_got_all.wait_recv()

    p4(core).start()
    t3_all.wait_recv()
    for half in range(2):
        total = c3[half, 0]
        for n in range(1, 8):
            total = total + c3[half, n]
        fin[TILES + half] = total
    p4(1 - core).wait_recv()
    fin_copy = pltpu.make_async_copy(fin, fin_h, o_sem.at[1])
    fin_copy.start()

    for c in (gt_all, gx_all, gy_all, ix_all, iy_all, k_all, t2_all, t3_all):
        c.wait_send()
    t1().wait_send()
    p4(core).wait_send()

    @pl.when(owner)
    def _():
        p1_sent.wait_send()
        p2_all.wait_send()
        p3_sent.wait_send()

    @pl.when(~owner)
    def _():
        p1_sent_all.wait_send()

    gp_copy.wait()
    fin_copy.wait()


def finish(gp, fin, gp_out, w1_out, w2_out):
    gp_out[...] = gp[...]
    for o9 in range(9):
        for h in range(2):
            v = fin[2 * o9 + h] * (float(TOTAL // 8) ** -0.5)
            for b in range(3):
                w2_out[o9 * 3 + b, h * 8 : h * 8 + 8, :] = v[:, b * 32 : b * 32 + 32]
    for i in range(2):
        v = fin[TILES + i] * (float(TOTAL) ** -0.5)
        for c in range(4):
            w1_out[c, i * 8 : i * 8 + 8, :] = v[:, c * 32 : c * 32 + 27]


def local(inputs, mask_one, place_one, pooled_one, w_two, mask_two, place_two, grad_two):
    vm = pl.BlockSpec(memory_space=pltpu.VMEM)
    anywhere = pl.BlockSpec(memory_space=pl.ANY)
    dma = pltpu.SemaphoreType.DMA
    gp, fin = pl.pallas_call(
        kernel,
        out_shape=(
            jax.ShapeDtypeStruct((48, 1024), BF16),
            jax.ShapeDtypeStruct((TILES + 2, 8, 128), F32),
        ),
        in_specs=[anywhere] * 8,
        out_specs=(anywhere, anywhere),
        scratch_shapes=[
            pltpu.VMEM((S, 4, 8192), BF16),
            pltpu.VMEM((48, 8192), I32),
            pltpu.VMEM((48, 1024), I32),
            pltpu.VMEM((48, 1024), BF16),
            pltpu.VMEM((27, 16, 32), BF16),
            pltpu.VMEM((96, 1024), I32),
            pltpu.VMEM((96, 128), I32),
            pltpu.VMEM((96, 128), BF16),
            pltpu.VMEM((48, 1024), BF16),
            pltpu.VMEM((2, 96, 128), BF16),
            pltpu.VMEM((2, 96, 128), BF16),
            pltpu.VMEM((2, 16, 128), BF16),
            pltpu.VMEM((2, 2, 96, 128), BF16),
            pltpu.VMEM((3, 2, 96, 128), BF16),
            pltpu.VMEM((9, 2, 16, 128), BF16),
            pltpu.VMEM((S, 96, 3072), BF16),
            pltpu.VMEM((144, 96), BF16),
            pltpu.VMEM((S, 144, 3072), BF16),
            pltpu.VMEM((144, 3072), F32),
            pltpu.VMEM((2, S, 4, 1024), BF16),
            pltpu.VMEM((2, S, 4, 2048), BF16),
            pltpu.VMEM((2, S, 4, 1536), BF16),
            pltpu.VMEM((18, 48, 256), F32),
            pltpu.VMEM((2, 48, 128), BF16),
            pltpu.VMEM((2, 48, 128), BF16),
            pltpu.VMEM((18, 144, 256), BF16),
            pltpu.VMEM((48, 8192), BF16),
            pltpu.VMEM((S, 4, 128, 256), BF16),
            pltpu.VMEM((128, 432), F32),
            pltpu.VMEM((TILES, 8, 128), F32),
            pltpu.VMEM((32, 8, 128), F32),
            pltpu.VMEM((8, 8, 128), F32),
            pltpu.VMEM((TILES + 2, 8, 128), F32),
            pltpu.VMEM((3, 432, 128), BF16),
            pltpu.VMEM((2, 8, 128), F32),
            pltpu.VMEM((8, 128), F32),
            pltpu.VMEM((16, 8, 128), F32),
            pltpu.VMEM((2, 8, 8, 128), F32),
            *[dma] * 12,
            *[dma] * 6,
            *[dma] * 8,
            dma((8,)), dma((2,)),
        ],
        compiler_params=pltpu.CompilerParams(
            collective_id=0, has_side_effects=True, vmem_limit_bytes=56 * 1024 * 1024
        ),
        name="whole",
    )(
        inputs.reshape(S, 4, 8192),
        mask_one.reshape(48, 8192),
        place_one.reshape(48, 1024),
        pooled_one.reshape(48, 1024),
        w_two,
        mask_two.reshape(96, 1024),
        place_two.reshape(96, 128),
        grad_two.reshape(96, 128),
    )
    gp, w1, w2 = pl.pallas_call(
        finish,
        out_shape=(
            jax.ShapeDtypeStruct((48, 1024), BF16),
            jax.ShapeDtypeStruct((4, 16, 27), F32),
            jax.ShapeDtypeStruct((27, 16, 32), F32),
        ),
        in_specs=[vm, vm],
        out_specs=(vm, vm, vm),
        name="finish",
    )(gp, fin)
    return gp.reshape(S, 1, 16, 1024), w1.transpose(2, 0, 1), w2


def solution(mesh):
    spec = P("dp", "space", None, None)
    return jax.shard_map(
        local,
        mesh=mesh,
        in_specs=(spec, spec, spec, spec, P(), spec, spec, spec),
        out_specs=(spec, P(), P()),
        check_vma=False,
    )
```

```python
import jax
import jax.numpy as jnp
from jax import lax
from jax.experimental import pallas as pl
from jax.experimental.pallas import tpu as pltpu
from jax.sharding import PartitionSpec as P

C_IN, C_ONE, C_TWO = 4, 16, 32
BX, BY, BZ = 4, 8, 256
S = 3
MESH = pl.DeviceIdType.MESH
F32, BF16, I32 = jnp.float32, jnp.bfloat16, jnp.int32
TILES = 18
TOTAL = 6291456
NEIGHBOURS = [
    (di, dj, dk)
    for di in (-1, 0, 1)
    for dj in (-1, 0, 1)
    for dk in (-1, 0, 1)
    if (di, dj, dk) != (0, 0, 0)
]
GREETED = [(-1, 0, 0), (1, 0, 0), (0, 0, -1), (0, 0, 1)]
XY = [(di, dj) for di in (-1, 0, 1) for dj in (-1, 0, 1) if (di, dj) != (0, 0)]
NT = (((1,), (1,)), ((), ()))
NN = (((1,), (0,)), ((), ()))
TN = (((0,), (0,)), ((), ()))


def dot(a, b, dims=NN):
    return lax.dot_general(a, b, dims, preferred_element_type=F32)


def iota(shape, dim):
    return lax.broadcasted_iota(I32, shape, dim)


def one_hot(cond):
    return jnp.where(cond, 1.0, 0.0).astype(BF16)


def kernel(
    inp_h, mask_one_h, place_one_h, pooled_h, w_two_h, mask_two_h, place_two_h, grad_two_h,
    gp_h, fin_h,
    inp, mask_one, place_one, pooled, w_two, mask_two, place_two, grad_two, gp,
    mp, yb, tk, rx, ry, rt, z3, wp, pst, tbuf,
    iyb, rix, riy, in32, rowsel, ysel, lhs, sel, gc, acc1,
    wg, r1, r2, fin, qbuf, own1, c1, c2, c3,
    gx_send, gx_recv, gy_send, gy_recv, gt_send, gt_recv,
    ix_send, ix_recv, iy_send, iy_recv,
    s1_send, s1_recv, s2_send, s2_recv, s3_send, s3_recv,
    s4_send, s4_recv, ta_send, ta_recv, tb_send, tb_recv, tc_send, tc_recv,
    l_sem, o_sem,
):
    dp = lax.axis_index("dp")
    sp = lax.axis_index("space")
    bi, bj, bk = sp // 16, (sp // 4) % 4, sp % 4
    zc, t8 = sp // 8, sp % 8
    men = dp * 8 + t8
    core = dp % 2
    chip = (dp // 2) * 8 + t8
    owner = ((core == 0) & (chip < 9)) | ((core == 1) & (chip >= 7))
    mine = jnp.where(core == 0, chip, chip + 2)

    def near(di, dj, dk):
        other = ((bi + di + 4) % 4) * 16 + ((bj + dj + 4) % 4) * 4 + (bk + dk + 4) % 4
        return {"space": other}

    def plane(n):
        return {"dp": n // 8, "space": zc * 8 + n % 8}

    def column(zz):
        return {"space": zz * 8 + t8}

    def twin():
        return {"dp": dp + 1 - 2 * core}

    def owner_of(o):
        n = o if o < 9 else o - 2
        return {"dp": (n // 8) * 2 + (0 if o < 9 else 1), "space": zc * 8 + n % 8}

    def is_mine(o):
        return owner & (mine == o)

    def p1(o):
        return pltpu.make_async_remote_copy(
            src_ref=wg.at[o], dst_ref=r1.at[men], send_sem=s1_send, recv_sem=s1_recv,
            device_id=owner_of(o), device_id_type=MESH,
        )

    def p2(n):
        return pltpu.make_async_remote_copy(
            src_ref=r2.at[zc], dst_ref=r2.at[zc], send_sem=s2_send, recv_sem=s2_recv,
            device_id=column((zc + n) % 8), device_id_type=MESH,
        )

    def p3(n):
        return pltpu.make_async_remote_copy(
            src_ref=fin.at[mine], dst_ref=fin.at[mine], send_sem=s3_send, recv_sem=s3_recv,
            device_id=chip_at((chip + n) % 16), device_id_type=MESH,
        )

    def p4(half):
        nine = fin.at[pl.ds(half * 9, 9)]
        return pltpu.make_async_remote_copy(
            src_ref=nine, dst_ref=nine, send_sem=s4_send, recv_sem=s4_recv,
            device_id=twin(), device_id_type=MESH,
        )

    def chip_at(n):
        return {"dp": (n // 8) * 2 + core, "space": zc * 8 + n % 8}

    def t1():
        return pltpu.make_async_remote_copy(
            src_ref=own1.at[1 - core], dst_ref=c1, send_sem=ta_send, recv_sem=ta_recv,
            device_id=twin(), device_id_type=MESH,
        )

    def t2(n):
        return pltpu.make_async_remote_copy(
            src_ref=c2.at[chip], dst_ref=c2.at[chip], send_sem=tb_send, recv_sem=tb_recv,
            device_id=chip_at((chip + n) % 16), device_id_type=MESH,
        )

    def t3(n, to):
        return pltpu.make_async_remote_copy(
            src_ref=c3.at[core, zc], dst_ref=c3.at[core, zc], send_sem=tc_send, recv_sem=tc_recv,
            device_id={"dp": to, "space": ((zc + n) % 8) * 8 + t8}, device_id_type=MESH,
        )

    def group(ref, send_sem, recv_sem):
        return pltpu.make_async_remote_copy(
            src_ref=ref, dst_ref=ref, send_sem=send_sem, recv_sem=recv_sem,
            device_id=twin(), device_id_type=MESH,
        )

    gx_all, gy_all, gt_all = group(rx, gx_send, gx_recv), group(ry, gy_send, gy_recv), group(rt, gt_send, gt_recv)
    ix_all, iy_all = group(rix, ix_send, ix_recv), group(riy, iy_send, iy_recv)
    p1_got = group(r1.at[0:31], s1_send, s1_recv)
    p1_sent = group(wg.at[0 : TILES - 1], s1_send, s1_recv)
    p1_sent_all = group(wg, s1_send, s1_recv)
    p2_all = group(r2.at[0:7], s2_send, s2_recv)
    p3_sent = group(r1.at[0:15], s3_send, s3_recv)
    p3_got = group(fin.at[0:8], s3_send, s3_recv)
    p3_got_all = group(fin.at[0:9], s3_send, s3_recv)
    t2_all = group(c2.at[0:15], tb_send, tb_recv)
    t3_all = group(c2.at[0:15], tc_send, tc_recv)

    barrier = pltpu.get_barrier_semaphore()
    for d in sorted(NEIGHBOURS, key=lambda d: -3 * abs(d[1]) - 2 * abs(d[0]) - abs(d[2])):
        if d in GREETED:
            continue
        pl.semaphore_signal(barrier, inc=1, device_id=near(*d), device_id_type=MESH)
    for n in range(1, 32):
        pl.semaphore_signal(barrier, inc=1, device_id=plane((men + n) % 32), device_id_type=MESH)
    for n in range(1, 8):
        pl.semaphore_signal(barrier, inc=1, device_id=column((zc + n) % 8), device_id_type=MESH)
        other = {"dp": dp + 1 - 2 * core, "space": ((zc + n) % 8) * 8 + t8}
        pl.semaphore_signal(barrier, inc=1, device_id=other, device_id_type=MESH)

    loads = [
        pltpu.make_async_copy(a, b, l_sem.at[n])
        for n, (a, b) in enumerate(
            (
                (place_two_h, place_two),
                (mask_two_h, mask_two),
                (grad_two_h, grad_two),
                (inp_h, inp),
                (w_two_h, w_two),
                (pooled_h, pooled),
                (place_one_h, place_one),
                (mask_one_h, mask_one),
            )
        )
    ]
    for c in loads:
        c.start()

    er, ec = iota((128, 768), 0), iota((128, 768), 1)
    ez = ec % 128 - (ec // 256 - 1)
    e3 = one_hot((er // 64 == (ec // 128) % 2) & (ez >= 0) & (ez < 128) & (ez // 2 == er % 64))
    e0 = e3[:, 256:512]
    for c in loads[:3]:
        c.wait()
    p_b = place_two[...].astype(F32).astype(BF16)
    p_up = dot(p_b, e0)
    par = (iota((96, 256), 1) % 2).astype(F32)
    keep = jnp.zeros((96, 256), jnp.bool_)
    for dx in range(2):
        for dy in range(2):
            tiles = [(dx * 4 + 2 * qy + dy) * 128 for qy in range(2)]
            m = jnp.concatenate([mask_two[:, t : t + 128] for t in tiles], axis=1)
            keep = keep | ((p_up == par + float(4 * dx + 2 * dy)) & (m == 1))
    kept = dot(one_hot(keep), e0, NT)
    m_f = jnp.where(kept > 0.5, grad_two[...].astype(F32), 0.0)
    p_f = p_b.astype(F32)
    m_b = m_f.astype(BF16)
    mp[0] = m_b
    mp[1] = p_b
    low = iota((96, 128), 1) < 64
    yb[0] = jnp.where(low, m_f, pltpu.roll(p_f, 64, 1)).astype(BF16)
    yb[1] = jnp.where(low, pltpu.roll(m_f, 64, 1), p_f).astype(BF16)
    tr, tc = iota((16, 128), 0), iota((16, 128), 1)
    loads[3].wait()
    row4, lane4 = iota((4, 128), 0), iota((4, 128), 1)
    for side, edge in ((0, 63), (1, 0)):
        pick_m = one_hot((tr < 2) & (tc == tr * 64 + edge))
        pick_p = one_hot((tr >= 2) & (tr < 4) & (tc == (tr - 2) * 64 + edge))
        rows = jnp.concatenate(
            [dot(pick_m, m_b, NT) + dot(pick_p, p_b, NT), jnp.zeros((16, 32), F32)], axis=1
        )
        for x in range(4):
            line = jnp.zeros((1, 128), F32)
            for s in range(S):
                a = jnp.zeros((4, 128), F32)
                for y in range(8):
                    at = (x * 8 + y) * 256 + (128 if side == 0 else 0)
                    v = inp[s, :, at : at + 128].astype(F32)
                    v = v[:, 127:128] if side == 0 else v[:, 0:1]
                    a = jnp.where(lane4 % 8 == y, jnp.broadcast_to(v, (4, 128)), a)
                a = jnp.where(lane4 // 8 == s * 4 + row4, a, 0.0)
                line = line + jnp.sum(a, axis=0, keepdims=True)
            rows = jnp.where(tr == 4 + x, jnp.broadcast_to(line, (16, 128)), rows)
        tk[side] = rows.astype(BF16)

    for q, y in ((0, 0), (1, 7)):
        for x in range(4):
            at = x * 2048 + y * 256
            iyb[q, :, :, x * 256 : (x + 1) * 256] = inp[:, :, at : at + 256]

    pl.semaphore_wait(barrier, 67)

    def g_copy(n, d):
        di, dj, dk = d
        if dk != 0:
            src = tk.at[0 if dk > 0 else 1]
            dst = rt.at[(1 - di) * 3 + 1 - dj, 0 if dk > 0 else 1]
            sems = gt_send, gt_recv
        elif dj == 0:
            src, dst = mp, rx.at[(1 - di) // 2]
            sems = gx_send, gx_recv
        else:
            src = yb.at[(1 + dj) // 2]
            dst = ry.at[1 - di, (1 - dj) // 2]
            sems = gy_send, gy_recv
        return pltpu.make_async_remote_copy(
            src_ref=src, dst_ref=dst, send_sem=sems[0], recv_sem=sems[1],
            device_id=near(*d), device_id_type=MESH,
        )

    def i_copy(n, d):
        di, dj = d
        if dj == 0:
            at = 3 * 2048 if di > 0 else 0
            src, dst = inp.at[:, :, at : at + 2048], rix.at[(1 - di) // 2]
            sems = ix_send, ix_recv
        else:
            q = (1 + dj) // 2
            sems = iy_send, iy_recv
            if di == 0:
                src = iyb.at[q]
                dst = riy.at[(1 - dj) // 2, :, :, 256 : 256 + 1024]
            else:
                at = 768 if di > 0 else 0
                to = 0 if di > 0 else 1280
                src = iyb.at[q, :, :, at : at + 256]
                dst = riy.at[(1 - dj) // 2, :, :, to : to + 256]
        return pltpu.make_async_remote_copy(
            src_ref=src, dst_ref=dst, send_sem=sems[0], recv_sem=sems[1],
            device_id=near(di, dj, 0), device_id_type=MESH,
        )

    g_copies = [g_copy(n, d) for n, d in enumerate(NEIGHBOURS)]
    i_copies = [i_copy(n, d) for n, d in enumerate(XY)]
    for d, c in zip(NEIGHBOURS, g_copies):
        if d[2] != 0:
            c.start()
    for d, c in zip(NEIGHBOURS, g_copies):
        if d[2] == 0:
            c.start()
    for c in i_copies:
        c.start()

    qr, qc = iota((432, 128), 0), iota((432, 128), 1)
    for oy in range(3):
        qo = (qr // 144) * 9 + oy * 3 + (qr // 48) % 3
        qbuf[oy] = one_hot((qr % 4 == qc // 32) & (qc % 32 == qo) & (qr % 48 < 40))
    for c in loads[4:]:
        c.wait()
    for o9 in range(9):
        wp[o9 * 16 : o9 * 16 + 16, :] = jnp.concatenate(
            [w_two[o9 * 3 + b].astype(F32) for b in range(3)], axis=1
        ).astype(BF16)
    pst[...] = jnp.zeros_like(pst)
    for ox in range(3):
        for oy in range(3):
            o9 = ox * 3 + oy
            for qx in range(2):
                for qy in range(4):
                    to = ((qx + 2 - ox) * 6 + qy + 2 - oy) * 128
                    at = (qx * 4 + qy) * 128
                    for s in range(S):
                        pst[s, o9 * 16 : o9 * 16 + 16, to : to + 128] = pooled[
                            s * 16 : s * 16 + 16, at : at + 128
                        ]
    e1r, e1c = iota((128, 256), 0), iota((128, 256), 1)
    e1 = one_hot(e1c // 2 == e1r)
    par1 = (iota((48, 256), 1) % 2).astype(F32)
    for hx in range(2):
        for hy in range(4):
            at = (hx * 4 + hy) * 128
            up = dot(place_one[:, at : at + 128].astype(F32).astype(BF16), e1)
            for dx in range(2):
                for dy in range(2):
                    to = ((2 * hx + dx) * 8 + 2 * hy + dy) * 256
                    ok = (up == par1 + float(4 * dx + 2 * dy)) & (mask_one[:, to : to + 256] == 1)
                    sel[:, to : to + 256] = one_hot(ok)

    in32[...] = jnp.zeros_like(in32)
    for s in range(S):
        for x in range(4):
            for y in range(8):
                at = (x * 8 + y) * 256
                in32[s * 6 + x + 1, 4 * y + 4 : 4 * y + 8, :] = inp[s, :, at : at + 256].astype(F32)
    sr, sc = iota((192, 288), 0), iota((192, 288), 1)
    xp = sr % 32 % 6
    from_i = jnp.where(xp == 0, 0, jnp.where(xp == 5, 2, 1))
    from_x = jnp.where(xp == 0, 3, jnp.where(xp == 5, 0, xp - 1))
    want = (from_i * 3 + (sr // 32) % 3) * 32 + (sr // 96) * 16 + 4 + from_x
    rowsel[...] = one_hot((sc == want) & (sr % 32 < 18))
    yr, yc = iota((48, 128), 0), iota((48, 128), 1)
    same = (yr % 4 == (yc // 8) % 4) & (yc < 96)
    ysel[0] = one_hot(same & (yr // 4 == 0) & (yc % 8 == 7))
    ysel[1] = one_hot(same & (yr // 4 >= 1) & (yr // 4 <= 8) & (yc % 8 == yr // 4 - 1))
    ysel[2] = one_hot(same & (yr // 4 == 9) & (yc % 8 == 0))

    fr, fc = iota((32, 768), 0), iota((32, 768), 1)
    f_in, f_mid, f_b = fc % 128, (fc // 128) % 2, fc // 256
    left = (f_b == 2) & (f_in == 0)
    right = (f_b == 0) & (f_in == 127)

    def halo_rows(row):
        return one_hot((left & (fr == row)) | (right & (fr == 16 + row)))

    f_m, f_p = halo_rows(f_mid), halo_rows(2 + f_mid)
    f_y = [halo_rows(2 * f_mid + q) for q in range(2)]
    lane = (iota((96, 128), 1) % 2).astype(F32)
    dz = [1.0 - lane, lane, 1.0 - lane]
    gt_all.wait_recv()

    def put(b, x, y, dx, dy, um, up):
        v = jnp.where(up == dz[b] + float(4 * dx + 2 * dy), um, 0.0).astype(BF16)
        to = (x * 6 + y) * 128
        for s in range(S):
            z3[s, b * 32 : b * 32 + 32, to : to + 128] = v[s * 32 : s * 32 + 32]

    for dj in (0, -1, 1):
        if dj == -1:
            gy_all.wait_recv()
        for di in (0, -1, 1):
            if dj == 0 and di == -1:
                gx_all.wait_recv()
            stack = rt[(di + 1) * 3 + dj + 1].reshape(32, 128)[:, 0:96]
            xs = {-1: [(0, 1)], 0: [(1, 0), (2, 1)], 1: [(3, 0)]}[di]
            if dj == 0:
                ref = mp if di == 0 else rx.at[(di + 1) // 2]
                um = dot(ref[0], e3) + dot(stack, f_m, TN)
                up = dot(ref[1], e3) + dot(stack, f_p, TN)
                for b in range(3):
                    for qy in range(2):
                        at = (b * 2 + qy) * 128
                        for x, dx in xs:
                            for dy in range(2):
                                put(b, x, 1 + 2 * qy + dy, dx, dy, um[:, at : at + 128], up[:, at : at + 128])
            else:
                q = 1 if dj < 0 else 0
                u = dot(ry[di + 1, (dj + 1) // 2], e3) + dot(stack, f_y[q], TN)
                for b in range(3):
                    at = b * 256
                    for x, dx in xs:
                        put(b, x, 0 if dj < 0 else 5, dx, q, u[:, at : at + 128], u[:, at + 128 : at + 256])

    w2 = jnp.zeros((144, 96), F32)
    for s in range(S):
        w2 = w2 + dot(pst[s], z3[s], NT)
    w2 = jnp.concatenate([w2, jnp.zeros((144, 32), F32)], axis=1)
    for i in range(TILES):
        wg[i] = w2[i * 8 : i * 8 + 8]
    for o in range(TILES):
        @pl.when(~is_mine(o))
        def _():
            p1(o).start()

    for s in range(S):
        for x in range(4):
            tbuf[:, x * 768 : x * 768 + 768] = dot(wp[...], z3[s, :, x * 768 : x * 768 + 768])
        for x in range(2):
            for y in range(4):
                a = jnp.zeros((16, 128), F32)
                for ox in range(3):
                    for oy in range(3):
                        r = (ox * 3 + oy) * 16
                        at = ((x + 2 - ox) * 6 + y + 2 - oy) * 128
                        a = a + tbuf[r : r + 16, at : at + 128]
                gp[s * 16 : s * 16 + 16, (x * 4 + y) * 128 : (x * 4 + y) * 128 + 128] = a.astype(BF16)
    gp_copy = pltpu.make_async_copy(gp, gp_h, o_sem.at[0])
    gp_copy.start()

    for hx in range(2):
        for hy in range(4):
            at = (hx * 4 + hy) * 128
            up = dot(gp[:, at : at + 128], e1)
            for dx in range(2):
                for dy in range(2):
                    x, y = 2 * hx + dx, 2 * hy + dy
                    to = (x * 8 + y) * 256
                    v = (up * sel[:, to : to + 256].astype(F32)).astype(BF16)
                    for s in range(S):
                        gc[s, x, y * 16 : y * 16 + 16, :] = v[s * 16 : s * 16 + 16]
    picked = dot(rowsel[...], rt[...].reshape(288, 128))
    picked = jnp.where(iota((192, 128), 1) // 32 == (iota((192, 128), 0) % 32) // 6, picked, 0.0).astype(BF16)
    edges = []
    for side in range(2):
        e = jnp.zeros((48, 32), F32)
        for j in range(3):
            r = side * 96 + j * 32
            e = e + dot(ysel[j], picked[r : r + 32], NT)
        edges.append(jnp.concatenate([e, jnp.zeros((48, 96), F32)], axis=1))
    edge_below, edge_above = edges

    for c in (ix_all, iy_all):
        c.wait_recv()
    for s in range(S):
        for x in range(6):
            for y in range(10):
                if 1 <= y <= 8:
                    if 1 <= x <= 4:
                        continue
                    at = (y - 1) * 256
                    v = rix[0 if x == 0 else 1, s, :, at : at + 256]
                else:
                    v = riy[0 if y == 0 else 1, s, :, x * 256 : x * 256 + 256]
                in32[s * 6 + x, 4 * y : 4 * y + 4, :] = v.astype(F32)

    lane256 = iota((48, 256), 1)
    for l in range(18):
        v = in32[l]
        below = jnp.concatenate([pltpu.roll(edge_below, (0 - l) % 128, 1), jnp.zeros((48, 128), F32)], axis=1)
        above = jnp.concatenate([jnp.zeros((48, 128), F32), pltpu.roll(edge_above, (127 - l) % 128, 1)], axis=1)
        lhs[l, 0:48, :] = jnp.where(lane256 == 0, below, pltpu.roll(v, 1, 1)).astype(BF16)
        lhs[l, 48:96, :] = v.astype(BF16)
        lhs[l, 96:144, :] = jnp.where(lane256 == 255, above, pltpu.roll(v, 255, 1)).astype(BF16)

    a1 = jnp.zeros((128, 432), F32)
    for s in range(S):
        for x in range(4):
            three = lhs[s * 6 + x : s * 6 + x + 3].reshape(432, 256)
            a1 = a1 + dot(gc[s, x], three, NT)
    acc1[...] = a1
    y_lane = (iota((16, 432), 1) % 48) // 4
    parts = []
    for oy in range(3):
        t = jnp.zeros((16, 432), F32)
        for y in range(8):
            t = t + jnp.where(y_lane == y + oy, acc1[y * 16 : y * 16 + 16, :], 0.0)
        parts.append(t)
    w1 = jnp.zeros((16, 128), F32)
    for oy in range(3):
        t = parts[oy]
        hi = t.astype(BF16)
        t = t - hi.astype(F32)
        mid = t.astype(BF16)
        low_part = (t - mid.astype(F32)).astype(BF16)
        r = dot(jnp.concatenate([hi, mid, low_part], axis=0), qbuf[oy])
        w1 = w1 + (r[0:16] + r[16:32] + r[32:48])
    own1[0] = w1[0:8]
    own1[1] = w1[8:16]
    t1().start()

    @pl.when(owner)
    def _():
        p1_got.wait_recv()
        r1[men] = wg[mine]
        total = r1[0]
        for n in range(1, 32):
            total = total + r1[n]
        r2[zc] = total
        for n in range(1, 8):
            p2(n).start()

    t1().wait_recv()
    c2[chip] = own1[core] + c1[...]
    for n in range(1, 16):
        t2(n).start()

    @pl.when(owner)
    def _():
        p2_all.wait_recv()
        total = r2[0]
        for zz in range(1, 8):
            total = total + r2[zz]
        fin[mine] = total
        for n in range(1, 16):
            p3(n).start()

    t2_all.wait_recv()
    total = c2[0]
    for n in range(1, 16):
        total = total + c2[n]
    c3[core, zc] = total
    for n in range(1, 8):
        t3(n, dp).start()
    t3(0, dp + 1 - 2 * core).start()
    for n in range(1, 8):
        t3(n, dp + 1 - 2 * core).start()

    @pl.when(owner)
    def _():
        p3_got.wait_recv()

    @pl.when(~owner)
    def _():
        p3_got_all.wait_recv()

    p4(core).start()
    t3_all.wait_recv()
    for half in range(2):
        total = c3[half, 0]
        for n in range(1, 8):
            total = total + c3[half, n]
        fin[TILES + half] = total
    p4(1 - core).wait_recv()
    fin_copy = pltpu.make_async_copy(fin, fin_h, o_sem.at[1])
    fin_copy.start()

    for c in (gt_all, gx_all, gy_all, ix_all, iy_all, t2_all, t3_all):
        c.wait_send()
    t1().wait_send()
    p4(core).wait_send()

    @pl.when(owner)
    def _():
        p1_sent.wait_send()
        p2_all.wait_send()
        p3_sent.wait_send()

    @pl.when(~owner)
    def _():
        p1_sent_all.wait_send()

    gp_copy.wait()
    fin_copy.wait()


def finish(gp, fin, gp_out, w1_out, w2_out):
    gp_out[...] = gp[...]
    for o9 in range(9):
        for h in range(2):
            v = fin[2 * o9 + h] * (float(TOTAL // 8) ** -0.5)
            for b in range(3):
                w2_out[o9 * 3 + b, h * 8 : h * 8 + 8, :] = v[:, b * 32 : b * 32 + 32]
    for i in range(2):
        v = fin[TILES + i] * (float(TOTAL) ** -0.5)
        for c in range(4):
            w1_out[c, i * 8 : i * 8 + 8, :] = v[:, c * 32 : c * 32 + 27]


def local(inputs, mask_one, place_one, pooled_one, w_two, mask_two, place_two, grad_two):
    vm = pl.BlockSpec(memory_space=pltpu.VMEM)
    anywhere = pl.BlockSpec(memory_space=pl.ANY)
    dma = pltpu.SemaphoreType.DMA
    gp, fin = pl.pallas_call(
        kernel,
        out_shape=(
            jax.ShapeDtypeStruct((48, 1024), BF16),
            jax.ShapeDtypeStruct((TILES + 2, 8, 128), F32),
        ),
        in_specs=[anywhere] * 8,
        out_specs=(anywhere, anywhere),
        scratch_shapes=[
            pltpu.VMEM((S, 4, 8192), BF16),
            pltpu.VMEM((48, 8192), I32),
            pltpu.VMEM((48, 1024), I32),
            pltpu.VMEM((48, 1024), BF16),
            pltpu.VMEM((27, 16, 32), BF16),
            pltpu.VMEM((96, 1024), I32),
            pltpu.VMEM((96, 128), I32),
            pltpu.VMEM((96, 128), BF16),
            pltpu.VMEM((48, 1024), BF16),
            pltpu.VMEM((2, 96, 128), BF16),
            pltpu.VMEM((2, 96, 128), BF16),
            pltpu.VMEM((2, 16, 128), BF16),
            pltpu.VMEM((2, 2, 96, 128), BF16),
            pltpu.VMEM((3, 2, 96, 128), BF16),
            pltpu.VMEM((9, 2, 16, 128), BF16),
            pltpu.VMEM((S, 96, 3072), BF16),
            pltpu.VMEM((144, 96), BF16),
            pltpu.VMEM((S, 144, 3072), BF16),
            pltpu.VMEM((144, 3072), F32),
            pltpu.VMEM((2, S, 4, 1024), BF16),
            pltpu.VMEM((2, S, 4, 2048), BF16),
            pltpu.VMEM((2, S, 4, 1536), BF16),
            pltpu.VMEM((18, 48, 256), F32),
            pltpu.VMEM((192, 288), BF16),
            pltpu.VMEM((3, 48, 128), BF16),
            pltpu.VMEM((18, 144, 256), BF16),
            pltpu.VMEM((48, 8192), BF16),
            pltpu.VMEM((S, 4, 128, 256), BF16),
            pltpu.VMEM((128, 432), F32),
            pltpu.VMEM((TILES, 8, 128), F32),
            pltpu.VMEM((32, 8, 128), F32),
            pltpu.VMEM((8, 8, 128), F32),
            pltpu.VMEM((TILES + 2, 8, 128), F32),
            pltpu.VMEM((3, 432, 128), BF16),
            pltpu.VMEM((2, 8, 128), F32),
            pltpu.VMEM((8, 128), F32),
            pltpu.VMEM((16, 8, 128), F32),
            pltpu.VMEM((2, 8, 8, 128), F32),
            *[dma] * 10,
            *[dma] * 6,
            *[dma] * 8,
            dma((8,)), dma((2,)),
        ],
        compiler_params=pltpu.CompilerParams(
            collective_id=0, has_side_effects=True, vmem_limit_bytes=56 * 1024 * 1024
        ),
        name="whole",
    )(
        inputs.reshape(S, 4, 8192),
        mask_one.reshape(48, 8192),
        place_one.reshape(48, 1024),
        pooled_one.reshape(48, 1024),
        w_two,
        mask_two.reshape(96, 1024),
        place_two.reshape(96, 128),
        grad_two.reshape(96, 128),
    )
    gp, w1, w2 = pl.pallas_call(
        finish,
        out_shape=(
            jax.ShapeDtypeStruct((48, 1024), BF16),
            jax.ShapeDtypeStruct((4, 16, 27), F32),
            jax.ShapeDtypeStruct((27, 16, 32), F32),
        ),
        in_specs=[vm, vm],
        out_specs=(vm, vm, vm),
        name="finish",
    )(gp, fin)
    return gp.reshape(S, 1, 16, 1024), w1.transpose(2, 0, 1), w2


def solution(mesh):
    spec = P("dp", "space", None, None)
    return jax.shard_map(
        local,
        mesh=mesh,
        in_specs=(spec, spec, spec, spec, P(), spec, spec, spec),
        out_specs=(spec, P(), P()),
        check_vma=False,
    )
```

```python
import jax
import jax.numpy as jnp
from jax import lax
from jax.experimental import pallas as pl
from jax.experimental.pallas import tpu as pltpu
from jax.sharding import PartitionSpec as P

C_IN, C_ONE, C_TWO = 4, 16, 32
BX, BY, BZ = 4, 8, 256
S = 3
MESH = pl.DeviceIdType.MESH
F32, BF16, I32 = jnp.float32, jnp.bfloat16, jnp.int32
CHUNKS, ROWS = 16, 9
TOTAL = 6291456
NEIGHBOURS = [
    (di, dj, dk)
    for di in (-1, 0, 1)
    for dj in (-1, 0, 1)
    for dk in (-1, 0, 1)
    if (di, dj, dk) != (0, 0, 0)
]
GREETED = [(-1, 0, 0), (1, 0, 0), (0, 0, -1), (0, 0, 1)]
XY = [(di, dj) for di in (-1, 0, 1) for dj in (-1, 0, 1) if (di, dj) != (0, 0)]
NT = (((1,), (1,)), ((), ()))
NN = (((1,), (0,)), ((), ()))
TN = (((0,), (0,)), ((), ()))


def dot(a, b, dims=NN):
    return lax.dot_general(a, b, dims, preferred_element_type=F32)


def iota(shape, dim):
    return lax.broadcasted_iota(I32, shape, dim)


def one_hot(cond):
    return jnp.where(cond, 1.0, 0.0).astype(BF16)


def kernel(
    inp_h, mask_one_h, place_one_h, pooled_h, w_two_h, mask_two_h, place_two_h, grad_two_h,
    gp_h, fin_h, one_h,
    inp, mask_one, place_one, pooled, w_two, mask_two, place_two, grad_two, gp,
    mp, yb, tk, rx, ry, rt, z3, wp, pst, tbuf,
    iyb, rix, riy, in32, rowsel, ysel, lhs, sel, gc, acc1,
    wg, r1, r2, fin, one, qbuf, own1, c1, c2, c3,
    gx_send, gx_recv, gy_send, gy_recv, gt_send, gt_recv,
    ix_send, ix_recv, iy_send, iy_recv,
    s1_send, s1_recv, s2_send, s2_recv, s3_send, s3_recv,
    ta_send, ta_recv, tb_send, tb_recv, tc_send, tc_recv,
    l_sem, o_sem,
):
    dp = lax.axis_index("dp")
    sp = lax.axis_index("space")
    bi, bj, bk = sp // 16, (sp // 4) % 4, sp % 4
    zc, t8 = sp // 8, sp % 8
    men = dp * 8 + t8
    core = dp % 2
    chip = (dp // 2) * 8 + t8
    owner = core == chip % 2

    def near(di, dj, dk):
        other = ((bi + di + 4) % 4) * 16 + ((bj + dj + 4) % 4) * 4 + (bk + dk + 4) % 4
        return {"space": other}

    def plane(n):
        return {"dp": n // 8, "space": zc * 8 + n % 8}

    def column(zz):
        return {"space": zz * 8 + t8}

    def twin():
        return {"dp": dp + 1 - 2 * core}

    def p1(o):
        return pltpu.make_async_remote_copy(
            src_ref=wg.at[o], dst_ref=r1.at[men], send_sem=s1_send, recv_sem=s1_recv,
            device_id={"dp": (o // 8) * 2 + o % 2, "space": zc * 8 + o % 8}, device_id_type=MESH,
        )

    def p2(n, to):
        return pltpu.make_async_remote_copy(
            src_ref=r2.at[zc], dst_ref=r2.at[zc], send_sem=s2_send, recv_sem=s2_recv,
            device_id={"dp": to, "space": ((zc + n) % 8) * 8 + t8}, device_id_type=MESH,
        )

    def p3(n):
        return pltpu.make_async_remote_copy(
            src_ref=fin.at[chip], dst_ref=fin.at[chip], send_sem=s3_send, recv_sem=s3_recv,
            device_id=chip_at((chip + n) % 16), device_id_type=MESH,
        )

    def chip_at(n):
        return {"dp": (n // 8) * 2 + core, "space": zc * 8 + n % 8}

    def t1():
        return pltpu.make_async_remote_copy(
            src_ref=own1.at[1 - core], dst_ref=c1, send_sem=ta_send, recv_sem=ta_recv,
            device_id=twin(), device_id_type=MESH,
        )

    def t2(n):
        return pltpu.make_async_remote_copy(
            src_ref=c2.at[chip], dst_ref=c2.at[chip], send_sem=tb_send, recv_sem=tb_recv,
            device_id=chip_at((chip + n) % 16), device_id_type=MESH,
        )

    def t3(n, to):
        return pltpu.make_async_remote_copy(
            src_ref=c3.at[core, zc], dst_ref=c3.at[core, zc], send_sem=tc_send, recv_sem=tc_recv,
            device_id={"dp": to, "space": ((zc + n) % 8) * 8 + t8}, device_id_type=MESH,
        )

    def group(ref, send_sem, recv_sem):
        return pltpu.make_async_remote_copy(
            src_ref=ref, dst_ref=ref, send_sem=send_sem, recv_sem=recv_sem,
            device_id=twin(), device_id_type=MESH,
        )

    gx_all, gy_all, gt_all = group(rx, gx_send, gx_recv), group(ry, gy_send, gy_recv), group(rt, gt_send, gt_recv)
    ix_all, iy_all = group(rix, ix_send, ix_recv), group(riy, iy_send, iy_recv)
    p1_got = group(r1.at[0:31], s1_send, s1_recv)
    p1_sent = group(wg.at[0 : CHUNKS - 1], s1_send, s1_recv)
    p1_sent_all = group(wg, s1_send, s1_recv)
    p2_sent = group(r1.at[0:15], s2_send, s2_recv)
    p2_got = group(r2.at[0:7], s2_send, s2_recv)
    p2_got_all = group(r2, s2_send, s2_recv)
    p3_all = group(fin.at[0:15], s3_send, s3_recv)
    t2_all = group(c2.at[0:15], tb_send, tb_recv)
    t3_all = group(c2.at[0:15], tc_send, tc_recv)

    barrier = pltpu.get_barrier_semaphore()
    for d in sorted(NEIGHBOURS, key=lambda d: -3 * abs(d[1]) - 2 * abs(d[0]) - abs(d[2])):
        if d in GREETED:
            continue
        pl.semaphore_signal(barrier, inc=1, device_id=near(*d), device_id_type=MESH)
    for n in range(1, 32):
        pl.semaphore_signal(barrier, inc=1, device_id=plane((men + n) % 32), device_id_type=MESH)
    for n in range(1, 8):
        pl.semaphore_signal(barrier, inc=1, device_id=column((zc + n) % 8), device_id_type=MESH)
        other = {"dp": dp + 1 - 2 * core, "space": ((zc + n) % 8) * 8 + t8}
        pl.semaphore_signal(barrier, inc=1, device_id=other, device_id_type=MESH)

    loads = [
        pltpu.make_async_copy(a, b, l_sem.at[n])
        for n, (a, b) in enumerate(
            (
                (place_two_h, place_two),
                (mask_two_h, mask_two),
                (grad_two_h, grad_two),
                (inp_h, inp),
                (w_two_h, w_two),
                (pooled_h, pooled),
                (place_one_h, place_one),
                (mask_one_h, mask_one),
            )
        )
    ]
    for c in loads:
        c.start()

    er, ec = iota((128, 768), 0), iota((128, 768), 1)
    ez = ec % 128 - (ec // 256 - 1)
    e3 = one_hot((er // 64 == (ec // 128) % 2) & (ez >= 0) & (ez < 128) & (ez // 2 == er % 64))
    e0 = e3[:, 256:512]
    for c in loads[:3]:
        c.wait()
    p_b = place_two[...].astype(F32).astype(BF16)
    p_up = dot(p_b, e0)
    par = (iota((96, 256), 1) % 2).astype(F32)
    keep = jnp.zeros((96, 256), jnp.bool_)
    for dx in range(2):
        for dy in range(2):
            tiles = [(dx * 4 + 2 * qy + dy) * 128 for qy in range(2)]
            m = jnp.concatenate([mask_two[:, t : t + 128] for t in tiles], axis=1)
            keep = keep | ((p_up == par + float(4 * dx + 2 * dy)) & (m == 1))
    kept = dot(one_hot(keep), e0, NT)
    m_f = jnp.where(kept > 0.5, grad_two[...].astype(F32), 0.0)
    p_f = p_b.astype(F32)
    m_b = m_f.astype(BF16)
    mp[0] = m_b
    mp[1] = p_b
    low = iota((96, 128), 1) < 64
    yb[0] = jnp.where(low, m_f, pltpu.roll(p_f, 64, 1)).astype(BF16)
    yb[1] = jnp.where(low, pltpu.roll(m_f, 64, 1), p_f).astype(BF16)
    tr, tc = iota((16, 128), 0), iota((16, 128), 1)
    loads[3].wait()
    row4, lane4 = iota((4, 128), 0), iota((4, 128), 1)
    for side, edge in ((0, 63), (1, 0)):
        pick_m = one_hot((tr < 2) & (tc == tr * 64 + edge))
        pick_p = one_hot((tr >= 2) & (tr < 4) & (tc == (tr - 2) * 64 + edge))
        rows = jnp.concatenate(
            [dot(pick_m, m_b, NT) + dot(pick_p, p_b, NT), jnp.zeros((16, 32), F32)], axis=1
        )
        for x in range(4):
            line = jnp.zeros((1, 128), F32)
            for s in range(S):
                a = jnp.zeros((4, 128), F32)
                for y in range(8):
                    at = (x * 8 + y) * 256 + (128 if side == 0 else 0)
                    v = inp[s, :, at : at + 128].astype(F32)
                    v = v[:, 127:128] if side == 0 else v[:, 0:1]
                    a = jnp.where(lane4 % 8 == y, jnp.broadcast_to(v, (4, 128)), a)
                a = jnp.where(lane4 // 8 == s * 4 + row4, a, 0.0)
                line = line + jnp.sum(a, axis=0, keepdims=True)
            rows = jnp.where(tr == 4 + x, jnp.broadcast_to(line, (16, 128)), rows)
        tk[side] = rows.astype(BF16)

    for q, y in ((0, 0), (1, 7)):
        for x in range(4):
            at = x * 2048 + y * 256
            iyb[q, :, :, x * 256 : (x + 1) * 256] = inp[:, :, at : at + 256]

    pl.semaphore_wait(barrier, 67)

    def g_copy(n, d):
        di, dj, dk = d
        if dk != 0:
            src = tk.at[0 if dk > 0 else 1]
            dst = rt.at[(1 - di) * 3 + 1 - dj, 0 if dk > 0 else 1]
            sems = gt_send, gt_recv
        elif dj == 0:
            src, dst = mp, rx.at[(1 - di) // 2]
            sems = gx_send, gx_recv
        else:
            src = yb.at[(1 + dj) // 2]
            dst = ry.at[1 - di, (1 - dj) // 2]
            sems = gy_send, gy_recv
        return pltpu.make_async_remote_copy(
            src_ref=src, dst_ref=dst, send_sem=sems[0], recv_sem=sems[1],
            device_id=near(*d), device_id_type=MESH,
        )

    def i_copy(n, d):
        di, dj = d
        if dj == 0:
            at = 3 * 2048 if di > 0 else 0
            src, dst = inp.at[:, :, at : at + 2048], rix.at[(1 - di) // 2]
            sems = ix_send, ix_recv
        else:
            q = (1 + dj) // 2
            sems = iy_send, iy_recv
            if di == 0:
                src = iyb.at[q]
                dst = riy.at[(1 - dj) // 2, :, :, 256 : 256 + 1024]
            else:
                at = 768 if di > 0 else 0
                to = 0 if di > 0 else 1280
                src = iyb.at[q, :, :, at : at + 256]
                dst = riy.at[(1 - dj) // 2, :, :, to : to + 256]
        return pltpu.make_async_remote_copy(
            src_ref=src, dst_ref=dst, send_sem=sems[0], recv_sem=sems[1],
            device_id=near(di, dj, 0), device_id_type=MESH,
        )

    g_copies = [g_copy(n, d) for n, d in enumerate(NEIGHBOURS)]
    i_copies = [i_copy(n, d) for n, d in enumerate(XY)]
    for d, c in zip(NEIGHBOURS, g_copies):
        if d[2] != 0:
            c.start()
    for d, c in zip(NEIGHBOURS, g_copies):
        if d[2] == 0:
            c.start()
    for c in i_copies:
        c.start()

    qr, qc = iota((432, 128), 0), iota((432, 128), 1)
    for oy in range(3):
        qo = (qr // 144) * 9 + oy * 3 + (qr // 48) % 3
        qbuf[oy] = one_hot((qr % 4 == qc // 32) & (qc % 32 == qo) & (qr % 48 < 40))
    for c in loads[4:]:
        c.wait()
    for o9 in range(9):
        wp[o9 * 16 : o9 * 16 + 16, :] = jnp.concatenate(
            [w_two[o9 * 3 + b].astype(F32) for b in range(3)], axis=1
        ).astype(BF16)
    pst[...] = jnp.zeros_like(pst)
    for ox in range(3):
        for oy in range(3):
            o9 = ox * 3 + oy
            for qx in range(2):
                for qy in range(4):
                    to = ((qx + 2 - ox) * 6 + qy + 2 - oy) * 128
                    at = (qx * 4 + qy) * 128
                    for s in range(S):
                        pst[s, o9 * 16 : o9 * 16 + 16, to : to + 128] = pooled[
                            s * 16 : s * 16 + 16, at : at + 128
                        ]
    e1r, e1c = iota((128, 256), 0), iota((128, 256), 1)
    e1 = one_hot(e1c // 2 == e1r)
    par1 = (iota((48, 256), 1) % 2).astype(F32)
    for hx in range(2):
        for hy in range(4):
            at = (hx * 4 + hy) * 128
            up = dot(place_one[:, at : at + 128].astype(F32).astype(BF16), e1)
            for dx in range(2):
                for dy in range(2):
                    to = ((2 * hx + dx) * 8 + 2 * hy + dy) * 256
                    ok = (up == par1 + float(4 * dx + 2 * dy)) & (mask_one[:, to : to + 256] == 1)
                    sel[:, to : to + 256] = one_hot(ok)

    in32[...] = jnp.zeros_like(in32)
    for s in range(S):
        for x in range(4):
            for y in range(8):
                at = (x * 8 + y) * 256
                in32[s * 6 + x + 1, 4 * y + 4 : 4 * y + 8, :] = inp[s, :, at : at + 256].astype(F32)
    sr, sc = iota((192, 288), 0), iota((192, 288), 1)
    xp = sr % 32 % 6
    from_i = jnp.where(xp == 0, 0, jnp.where(xp == 5, 2, 1))
    from_x = jnp.where(xp == 0, 3, jnp.where(xp == 5, 0, xp - 1))
    want = (from_i * 3 + (sr // 32) % 3) * 32 + (sr // 96) * 16 + 4 + from_x
    rowsel[...] = one_hot((sc == want) & (sr % 32 < 18))
    yr, yc = iota((48, 128), 0), iota((48, 128), 1)
    same = (yr % 4 == (yc // 8) % 4) & (yc < 96)
    ysel[0] = one_hot(same & (yr // 4 == 0) & (yc % 8 == 7))
    ysel[1] = one_hot(same & (yr // 4 >= 1) & (yr // 4 <= 8) & (yc % 8 == yr // 4 - 1))
    ysel[2] = one_hot(same & (yr // 4 == 9) & (yc % 8 == 0))

    fr, fc = iota((32, 768), 0), iota((32, 768), 1)
    f_in, f_mid, f_b = fc % 128, (fc // 128) % 2, fc // 256
    left = (f_b == 2) & (f_in == 0)
    right = (f_b == 0) & (f_in == 127)

    def halo_rows(row):
        return one_hot((left & (fr == row)) | (right & (fr == 16 + row)))

    f_m, f_p = halo_rows(f_mid), halo_rows(2 + f_mid)
    f_y = [halo_rows(2 * f_mid + q) for q in range(2)]
    lane = (iota((96, 128), 1) % 2).astype(F32)
    dz = [1.0 - lane, lane, 1.0 - lane]
    gt_all.wait_recv()

    def put(b, x, y, dx, dy, um, up):
        v = jnp.where(up == dz[b] + float(4 * dx + 2 * dy), um, 0.0).astype(BF16)
        to = (x * 6 + y) * 128
        for s in range(S):
            z3[s, b * 32 : b * 32 + 32, to : to + 128] = v[s * 32 : s * 32 + 32]

    for dj in (0, -1, 1):
        if dj == -1:
            gy_all.wait_recv()
        for di in (0, -1, 1):
            if dj == 0 and di == -1:
                gx_all.wait_recv()
            stack = rt[(di + 1) * 3 + dj + 1].reshape(32, 128)[:, 0:96]
            xs = {-1: [(0, 1)], 0: [(1, 0), (2, 1)], 1: [(3, 0)]}[di]
            if dj == 0:
                ref = mp if di == 0 else rx.at[(di + 1) // 2]
                um = dot(ref[0], e3) + dot(stack, f_m, TN)
                up = dot(ref[1], e3) + dot(stack, f_p, TN)
                for b in range(3):
                    for qy in range(2):
                        at = (b * 2 + qy) * 128
                        for x, dx in xs:
                            for dy in range(2):
                                put(b, x, 1 + 2 * qy + dy, dx, dy, um[:, at : at + 128], up[:, at : at + 128])
            else:
                q = 1 if dj < 0 else 0
                u = dot(ry[di + 1, (dj + 1) // 2], e3) + dot(stack, f_y[q], TN)
                for b in range(3):
                    at = b * 256
                    for x, dx in xs:
                        put(b, x, 0 if dj < 0 else 5, dx, q, u[:, at : at + 128], u[:, at + 128 : at + 256])

    w2 = jnp.zeros((144, 96), F32)
    for s in range(S):
        w2 = w2 + dot(pst[s], z3[s], NT)
    w2 = jnp.concatenate([w2, jnp.zeros((144, 32), F32)], axis=1)
    for i in range(CHUNKS):
        wg[i] = w2[i * ROWS : i * ROWS + ROWS]
    for o in range(CHUNKS):
        @pl.when(~(owner & (chip == o)))
        def _():
            p1(o).start()

    for s in range(S):
        for x in range(4):
            tbuf[:, x * 768 : x * 768 + 768] = dot(wp[...], z3[s, :, x * 768 : x * 768 + 768])
        for x in range(2):
            for y in range(4):
                a = jnp.zeros((16, 128), F32)
                for ox in range(3):
                    for oy in range(3):
                        r = (ox * 3 + oy) * 16
                        at = ((x + 2 - ox) * 6 + y + 2 - oy) * 128
                        a = a + tbuf[r : r + 16, at : at + 128]
                gp[s * 16 : s * 16 + 16, (x * 4 + y) * 128 : (x * 4 + y) * 128 + 128] = a.astype(BF16)
    gp_copy = pltpu.make_async_copy(gp, gp_h, o_sem.at[0])
    gp_copy.start()

    for hx in range(2):
        for hy in range(4):
            at = (hx * 4 + hy) * 128
            up = dot(gp[:, at : at + 128], e1)
            for dx in range(2):
                for dy in range(2):
                    x, y = 2 * hx + dx, 2 * hy + dy
                    to = (x * 8 + y) * 256
                    v = (up * sel[:, to : to + 256].astype(F32)).astype(BF16)
                    for s in range(S):
                        gc[s, x, y * 16 : y * 16 + 16, :] = v[s * 16 : s * 16 + 16]
    picked = dot(rowsel[...], rt[...].reshape(288, 128))
    picked = jnp.where(iota((192, 128), 1) // 32 == (iota((192, 128), 0) % 32) // 6, picked, 0.0).astype(BF16)
    edges = []
    for side in range(2):
        e = jnp.zeros((48, 32), F32)
        for j in range(3):
            r = side * 96 + j * 32
            e = e + dot(ysel[j], picked[r : r + 32], NT)
        edges.append(jnp.concatenate([e, jnp.zeros((48, 96), F32)], axis=1))
    edge_below, edge_above = edges

    for c in (ix_all, iy_all):
        c.wait_recv()
    for s in range(S):
        for x in range(6):
            for y in range(10):
                if 1 <= y <= 8:
                    if 1 <= x <= 4:
                        continue
                    at = (y - 1) * 256
                    v = rix[0 if x == 0 else 1, s, :, at : at + 256]
                else:
                    v = riy[0 if y == 0 else 1, s, :, x * 256 : x * 256 + 256]
                in32[s * 6 + x, 4 * y : 4 * y + 4, :] = v.astype(F32)

    lane256 = iota((48, 256), 1)
    for l in range(18):
        v = in32[l]
        below = jnp.concatenate([pltpu.roll(edge_below, (0 - l) % 128, 1), jnp.zeros((48, 128), F32)], axis=1)
        above = jnp.concatenate([jnp.zeros((48, 128), F32), pltpu.roll(edge_above, (127 - l) % 128, 1)], axis=1)
        lhs[l, 0:48, :] = jnp.where(lane256 == 0, below, pltpu.roll(v, 1, 1)).astype(BF16)
        lhs[l, 48:96, :] = v.astype(BF16)
        lhs[l, 96:144, :] = jnp.where(lane256 == 255, above, pltpu.roll(v, 255, 1)).astype(BF16)

    a1 = jnp.zeros((128, 432), F32)
    for s in range(S):
        for x in range(4):
            three = lhs[s * 6 + x : s * 6 + x + 3].reshape(432, 256)
            a1 = a1 + dot(gc[s, x], three, NT)
    acc1[...] = a1
    y_lane = (iota((16, 432), 1) % 48) // 4
    parts = []
    for oy in range(3):
        t = jnp.zeros((16, 432), F32)
        for y in range(8):
            t = t + jnp.where(y_lane == y + oy, acc1[y * 16 : y * 16 + 16, :], 0.0)
        parts.append(t)
    w1 = jnp.zeros((16, 128), F32)
    for oy in range(3):
        t = parts[oy]
        hi = t.astype(BF16)
        t = t - hi.astype(F32)
        mid = t.astype(BF16)
        low_part = (t - mid.astype(F32)).astype(BF16)
        r = dot(jnp.concatenate([hi, mid, low_part], axis=0), qbuf[oy])
        w1 = w1 + (r[0:16] + r[16:32] + r[32:48])
    own1[0] = w1[0:8]
    own1[1] = w1[8:16]
    t1().start()

    @pl.when(owner)
    def _():
        p1_got.wait_recv()
        r1[men] = wg[chip]
        total = r1[0]
        for n in range(1, 32):
            total = total + r1[n]
        r2[zc] = total
        for n in range(1, 8):
            p2(n, dp).start()
            p2(n, dp + 1 - 2 * core).start()
        p2(0, dp + 1 - 2 * core).start()

    t1().wait_recv()
    c2[chip] = own1[core] + c1[...]
    for n in range(1, 16):
        t2(n).start()

    @pl.when(owner)
    def _():
        p2_got.wait_recv()

    @pl.when(~owner)
    def _():
        p2_got_all.wait_recv()

    total = r2[0]
    for zz in range(1, 8):
        total = total + r2[zz]
    fin[chip] = total
    for n in range(1, 16):
        p3(n).start()

    t2_all.wait_recv()
    total = c2[0]
    for n in range(1, 16):
        total = total + c2[n]
    c3[core, zc] = total
    for n in range(1, 8):
        t3(n, dp).start()
    t3(0, dp + 1 - 2 * core).start()
    for n in range(1, 8):
        t3(n, dp + 1 - 2 * core).start()

    p3_all.wait_recv()
    fin_copy = pltpu.make_async_copy(fin, fin_h, o_sem.at[1])
    fin_copy.start()
    t3_all.wait_recv()
    for half in range(2):
        total = c3[half, 0]
        for n in range(1, 8):
            total = total + c3[half, n]
        one[half] = total
    one_copy = pltpu.make_async_copy(one, one_h, o_sem.at[2])
    one_copy.start()

    for c in (gt_all, gx_all, gy_all, ix_all, iy_all, t2_all, t3_all, p3_all):
        c.wait_send()
    t1().wait_send()

    @pl.when(owner)
    def _():
        p1_sent.wait_send()
        p2_sent.wait_send()

    @pl.when(~owner)
    def _():
        p1_sent_all.wait_send()

    gp_copy.wait()
    fin_copy.wait()
    one_copy.wait()


def finish(gp, fin, one, gp_out, w1_out, w2_out):
    gp_out[...] = gp[...]
    v = jnp.concatenate([fin[n] for n in range(CHUNKS)], axis=0) * (float(TOTAL // 8) ** -0.5)
    for o9 in range(9):
        for b in range(3):
            w2_out[o9 * 3 + b] = v[o9 * 16 : o9 * 16 + 16, b * 32 : b * 32 + 32]
    for i in range(2):
        v = one[i] * (float(TOTAL) ** -0.5)
        for c in range(4):
            w1_out[c, i * 8 : i * 8 + 8, :] = v[:, c * 32 : c * 32 + 27]


def local(inputs, mask_one, place_one, pooled_one, w_two, mask_two, place_two, grad_two):
    vm = pl.BlockSpec(memory_space=pltpu.VMEM)
    anywhere = pl.BlockSpec(memory_space=pl.ANY)
    dma = pltpu.SemaphoreType.DMA
    gp, fin, one = pl.pallas_call(
        kernel,
        out_shape=(
            jax.ShapeDtypeStruct((48, 1024), BF16),
            jax.ShapeDtypeStruct((CHUNKS, ROWS, 128), F32),
            jax.ShapeDtypeStruct((2, 8, 128), F32),
        ),
        in_specs=[anywhere] * 8,
        out_specs=(anywhere, anywhere, anywhere),
        scratch_shapes=[
            pltpu.VMEM((S, 4, 8192), BF16),
            pltpu.VMEM((48, 8192), I32),
            pltpu.VMEM((48, 1024), I32),
            pltpu.VMEM((48, 1024), BF16),
            pltpu.VMEM((27, 16, 32), BF16),
            pltpu.VMEM((96, 1024), I32),
            pltpu.VMEM((96, 128), I32),
            pltpu.VMEM((96, 128), BF16),
            pltpu.VMEM((48, 1024), BF16),
            pltpu.VMEM((2, 96, 128), BF16),
            pltpu.VMEM((2, 96, 128), BF16),
            pltpu.VMEM((2, 16, 128), BF16),
            pltpu.VMEM((2, 2, 96, 128), BF16),
            pltpu.VMEM((3, 2, 96, 128), BF16),
            pltpu.VMEM((9, 2, 16, 128), BF16),
            pltpu.VMEM((S, 96, 3072), BF16),
            pltpu.VMEM((144, 96), BF16),
            pltpu.VMEM((S, 144, 3072), BF16),
            pltpu.VMEM((144, 3072), F32),
            pltpu.VMEM((2, S, 4, 1024), BF16),
            pltpu.VMEM((2, S, 4, 2048), BF16),
            pltpu.VMEM((2, S, 4, 1536), BF16),
            pltpu.VMEM((18, 48, 256), F32),
            pltpu.VMEM((192, 288), BF16),
            pltpu.VMEM((3, 48, 128), BF16),
            pltpu.VMEM((18, 144, 256), BF16),
            pltpu.VMEM((48, 8192), BF16),
            pltpu.VMEM((S, 4, 128, 256), BF16),
            pltpu.VMEM((128, 432), F32),
            pltpu.VMEM((CHUNKS, ROWS, 128), F32),
            pltpu.VMEM((32, ROWS, 128), F32),
            pltpu.VMEM((8, ROWS, 128), F32),
            pltpu.VMEM((CHUNKS, ROWS, 128), F32),
            pltpu.VMEM((2, 8, 128), F32),
            pltpu.VMEM((3, 432, 128), BF16),
            pltpu.VMEM((2, 8, 128), F32),
            pltpu.VMEM((8, 128), F32),
            pltpu.VMEM((16, 8, 128), F32),
            pltpu.VMEM((2, 8, 8, 128), F32),
            *[dma] * 10,
            *[dma] * 6,
            *[dma] * 6,
            dma((8,)), dma((3,)),
        ],
        compiler_params=pltpu.CompilerParams(
            collective_id=0, has_side_effects=True, vmem_limit_bytes=56 * 1024 * 1024
        ),
        name="whole",
    )(
        inputs.reshape(S, 4, 8192),
        mask_one.reshape(48, 8192),
        place_one.reshape(48, 1024),
        pooled_one.reshape(48, 1024),
        w_two,
        mask_two.reshape(96, 1024),
        place_two.reshape(96, 128),
        grad_two.reshape(96, 128),
    )
    gp, w1, w2 = pl.pallas_call(
        finish,
        out_shape=(
            jax.ShapeDtypeStruct((48, 1024), BF16),
            jax.ShapeDtypeStruct((4, 16, 27), F32),
            jax.ShapeDtypeStruct((27, 16, 32), F32),
        ),
        in_specs=[vm, vm, vm],
        out_specs=(vm, vm, vm),
        name="finish",
    )(gp, fin, one)
    return gp.reshape(S, 1, 16, 1024), w1.transpose(2, 0, 1), w2


def solution(mesh):
    spec = P("dp", "space", None, None)
    return jax.shard_map(
        local,
        mesh=mesh,
        in_specs=(spec, spec, spec, spec, P(), spec, spec, spec),
        out_specs=(spec, P(), P()),
        check_vma=False,
    )
```

```python
import jax
import jax.numpy as jnp
from jax import lax
from jax.experimental import pallas as pl
from jax.experimental.pallas import tpu as pltpu
from jax.sharding import PartitionSpec as P

C_IN, C_ONE, C_TWO = 4, 16, 32
BX, BY, BZ = 4, 8, 256
S = 3
MESH = pl.DeviceIdType.MESH
F32, BF16, I32 = jnp.float32, jnp.bfloat16, jnp.int32
CHUNKS, ROWS = 16, 9
TOTAL = 6291456
NEIGHBOURS = [
    (di, dj, dk)
    for di in (-1, 0, 1)
    for dj in (-1, 0, 1)
    for dk in (-1, 0, 1)
    if (di, dj, dk) != (0, 0, 0)
]
GREETED = [(-1, 0, 0), (1, 0, 0), (0, 0, -1), (0, 0, 1)]
XY = [(di, dj) for di in (-1, 0, 1) for dj in (-1, 0, 1) if (di, dj) != (0, 0)]
NT = (((1,), (1,)), ((), ()))
NN = (((1,), (0,)), ((), ()))
TN = (((0,), (0,)), ((), ()))


def dot(a, b, dims=NN):
    return lax.dot_general(a, b, dims, preferred_element_type=F32)


def iota(shape, dim):
    return lax.broadcasted_iota(I32, shape, dim)


def one_hot(cond):
    return jnp.where(cond, 1.0, 0.0).astype(BF16)


def kernel(
    inp_h, mask_one_h, place_one_h, pooled_h, w_two_h, mask_two_h, place_two_h, grad_two_h,
    gp_h, fin_h, one_h,
    inp, mask_one, place_one, pooled, w_two, mask_two, place_two, grad_two, gp,
    mp, yb, tk, rx, ry, rt, z3, wp, pst, tbuf,
    iyb, rix, riy, in32, rowsel, ysel, lhs, sel, gc, acc1,
    wg, r1, r2, fin, one, qbuf, own1, c1, c2, c3,
    gx_send, gx_recv, gy_send, gy_recv, gt_send, gt_recv,
    ix_send, ix_recv, iy_send, iy_recv,
    s1_send, s1_recv, s2_send, s2_recv, s3_send, s3_recv,
    ta_send, ta_recv, tb_send, tb_recv, tc_send, tc_recv,
    l_sem, o_sem,
):
    dp = lax.axis_index("dp")
    sp = lax.axis_index("space")
    bi, bj, bk = sp // 16, (sp // 4) % 4, sp % 4
    zc, t8 = sp // 8, sp % 8
    men = dp * 8 + t8
    core = dp % 2
    chip = (dp // 2) * 8 + t8
    owner = core == chip % 2

    def near(di, dj, dk):
        other = ((bi + di + 4) % 4) * 16 + ((bj + dj + 4) % 4) * 4 + (bk + dk + 4) % 4
        return {"space": other}

    def plane(n):
        return {"dp": n // 8, "space": zc * 8 + n % 8}

    def column(zz):
        return {"space": zz * 8 + t8}

    def twin():
        return {"dp": dp + 1 - 2 * core}

    def p1(o):
        return pltpu.make_async_remote_copy(
            src_ref=wg.at[o], dst_ref=r1.at[men], send_sem=s1_send, recv_sem=s1_recv,
            device_id={"dp": (o // 8) * 2 + o % 2, "space": zc * 8 + o % 8}, device_id_type=MESH,
        )

    def p2(n, to):
        return pltpu.make_async_remote_copy(
            src_ref=r2.at[zc], dst_ref=r2.at[zc], send_sem=s2_send, recv_sem=s2_recv,
            device_id={"dp": to, "space": ((zc + n) % 8) * 8 + t8}, device_id_type=MESH,
        )

    def p3(n):
        return pltpu.make_async_remote_copy(
            src_ref=fin.at[chip], dst_ref=fin.at[chip], send_sem=s3_send, recv_sem=s3_recv,
            device_id=chip_at((chip + n) % 16), device_id_type=MESH,
        )

    def chip_at(n):
        return {"dp": (n // 8) * 2 + core, "space": zc * 8 + n % 8}

    def t1():
        return pltpu.make_async_remote_copy(
            src_ref=own1.at[1 - core], dst_ref=c1, send_sem=ta_send, recv_sem=ta_recv,
            device_id=twin(), device_id_type=MESH,
        )

    def t2(n):
        return pltpu.make_async_remote_copy(
            src_ref=c2.at[chip], dst_ref=c2.at[chip], send_sem=tb_send, recv_sem=tb_recv,
            device_id=chip_at((chip + n) % 16), device_id_type=MESH,
        )

    def t3(n, to):
        return pltpu.make_async_remote_copy(
            src_ref=c3.at[core, zc], dst_ref=c3.at[core, zc], send_sem=tc_send, recv_sem=tc_recv,
            device_id={"dp": to, "space": ((zc + n) % 8) * 8 + t8}, device_id_type=MESH,
        )

    def group(ref, send_sem, recv_sem):
        return pltpu.make_async_remote_copy(
            src_ref=ref, dst_ref=ref, send_sem=send_sem, recv_sem=recv_sem,
            device_id=twin(), device_id_type=MESH,
        )

    gx_all, gy_all, gt_all = group(rx, gx_send, gx_recv), group(ry, gy_send, gy_recv), group(rt, gt_send, gt_recv)
    ix_all, iy_all = group(rix, ix_send, ix_recv), group(riy, iy_send, iy_recv)
    p1_got = group(r1.at[0:31], s1_send, s1_recv)
    p1_sent = group(wg.at[0 : CHUNKS - 1], s1_send, s1_recv)
    p1_sent_all = group(wg, s1_send, s1_recv)
    p2_sent = group(r1.at[0:15], s2_send, s2_recv)
    p2_got = group(r2.at[0:7], s2_send, s2_recv)
    p2_got_all = group(r2, s2_send, s2_recv)
    p3_all = group(fin.at[0:15], s3_send, s3_recv)
    t2_all = group(c2.at[0:15], tb_send, tb_recv)
    t3_all = group(c2.at[0:15], tc_send, tc_recv)

    barrier = pltpu.get_barrier_semaphore()
    for d in sorted(NEIGHBOURS, key=lambda d: -3 * abs(d[1]) - 2 * abs(d[0]) - abs(d[2])):
        if d in GREETED:
            continue
        pl.semaphore_signal(barrier, inc=1, device_id=near(*d), device_id_type=MESH)
    for n in range(1, 32):
        pl.semaphore_signal(barrier, inc=1, device_id=plane((men + n) % 32), device_id_type=MESH)
    for n in range(1, 8):
        pl.semaphore_signal(barrier, inc=1, device_id=column((zc + n) % 8), device_id_type=MESH)
        other = {"dp": dp + 1 - 2 * core, "space": ((zc + n) % 8) * 8 + t8}
        pl.semaphore_signal(barrier, inc=1, device_id=other, device_id_type=MESH)

    loads = [
        pltpu.make_async_copy(a, b, l_sem.at[n])
        for n, (a, b) in enumerate(
            (
                (place_two_h, place_two),
                (mask_two_h, mask_two),
                (grad_two_h, grad_two),
                (inp_h, inp),
                (w_two_h, w_two),
                (pooled_h, pooled),
                (place_one_h, place_one),
                (mask_one_h, mask_one),
            )
        )
    ]
    for c in loads:
        c.start()

    er, ec = iota((128, 768), 0), iota((128, 768), 1)
    ez = ec % 128 - (ec // 256 - 1)
    e3 = one_hot((er // 64 == (ec // 128) % 2) & (ez >= 0) & (ez < 128) & (ez // 2 == er % 64))
    e0 = e3[:, 256:512]
    for c in loads[:3]:
        c.wait()
    p_b = place_two[...].astype(F32).astype(BF16)
    p_up = dot(p_b, e0)
    par = (iota((96, 256), 1) % 2).astype(F32)
    keep = jnp.zeros((96, 256), jnp.bool_)
    for dx in range(2):
        for dy in range(2):
            tiles = [(dx * 4 + 2 * qy + dy) * 128 for qy in range(2)]
            m = jnp.concatenate([mask_two[:, t : t + 128] for t in tiles], axis=1)
            keep = keep | ((p_up == par + float(4 * dx + 2 * dy)) & (m == 1))
    kept = dot(one_hot(keep), e0, NT)
    m_f = jnp.where(kept > 0.5, grad_two[...].astype(F32), 0.0)
    p_f = p_b.astype(F32)
    m_b = m_f.astype(BF16)
    mp[0] = m_b
    mp[1] = p_b
    low = iota((96, 128), 1) < 64
    yb[0] = jnp.where(low, m_f, pltpu.roll(p_f, 64, 1)).astype(BF16)
    yb[1] = jnp.where(low, pltpu.roll(m_f, 64, 1), p_f).astype(BF16)
    tr, tc = iota((16, 128), 0), iota((16, 128), 1)
    loads[3].wait()
    row4, lane4 = iota((4, 128), 0), iota((4, 128), 1)
    for side, edge in ((0, 63), (1, 0)):
        pick_m = one_hot((tr < 2) & (tc == tr * 64 + edge))
        pick_p = one_hot((tr >= 2) & (tr < 4) & (tc == (tr - 2) * 64 + edge))
        rows = jnp.concatenate(
            [dot(pick_m, m_b, NT) + dot(pick_p, p_b, NT), jnp.zeros((16, 32), F32)], axis=1
        )
        for x in range(4):
            line = jnp.zeros((1, 128), F32)
            for s in range(S):
                a = jnp.zeros((4, 128), F32)
                for y in range(8):
                    at = (x * 8 + y) * 256 + (128 if side == 0 else 0)
                    v = inp[s, :, at : at + 128].astype(F32)
                    v = v[:, 127:128] if side == 0 else v[:, 0:1]
                    a = jnp.where(lane4 % 8 == y, jnp.broadcast_to(v, (4, 128)), a)
                a = jnp.where(lane4 // 8 == s * 4 + row4, a, 0.0)
                line = line + jnp.sum(a, axis=0, keepdims=True)
            rows = jnp.where(tr == 4 + x, jnp.broadcast_to(line, (16, 128)), rows)
        tk[side] = rows.astype(BF16)

    for q, y in ((0, 0), (1, 7)):
        for x in range(4):
            at = x * 2048 + y * 256
            iyb[q, :, :, x * 256 : (x + 1) * 256] = inp[:, :, at : at + 256]

    pl.semaphore_wait(barrier, 67)

    def g_copy(n, d):
        di, dj, dk = d
        if dk != 0:
            src = tk.at[0 if dk > 0 else 1]
            dst = rt.at[(1 - di) * 3 + 1 - dj, 0 if dk > 0 else 1]
            sems = gt_send, gt_recv
        elif dj == 0:
            src, dst = mp, rx.at[(1 - di) // 2]
            sems = gx_send, gx_recv
        else:
            src = yb.at[(1 + dj) // 2]
            dst = ry.at[1 - di, (1 - dj) // 2]
            sems = gy_send, gy_recv
        return pltpu.make_async_remote_copy(
            src_ref=src, dst_ref=dst, send_sem=sems[0], recv_sem=sems[1],
            device_id=near(*d), device_id_type=MESH,
        )

    def i_copy(n, d):
        di, dj = d
        if dj == 0:
            at = 3 * 2048 if di > 0 else 0
            src, dst = inp.at[:, :, at : at + 2048], rix.at[(1 - di) // 2]
            sems = ix_send, ix_recv
        else:
            q = (1 + dj) // 2
            sems = iy_send, iy_recv
            if di == 0:
                src = iyb.at[q]
                dst = riy.at[(1 - dj) // 2, :, :, 256 : 256 + 1024]
            else:
                at = 768 if di > 0 else 0
                to = 0 if di > 0 else 1280
                src = iyb.at[q, :, :, at : at + 256]
                dst = riy.at[(1 - dj) // 2, :, :, to : to + 256]
        return pltpu.make_async_remote_copy(
            src_ref=src, dst_ref=dst, send_sem=sems[0], recv_sem=sems[1],
            device_id=near(di, dj, 0), device_id_type=MESH,
        )

    g_copies = [g_copy(n, d) for n, d in enumerate(NEIGHBOURS)]
    i_copies = [i_copy(n, d) for n, d in enumerate(XY)]
    for d, c in zip(NEIGHBOURS, g_copies):
        if d[2] != 0:
            c.start()
    for d, c in zip(NEIGHBOURS, g_copies):
        if d[2] == 0:
            c.start()
    for c in i_copies:
        c.start()

    qr, qc = iota((432, 128), 0), iota((432, 128), 1)
    for oy in range(3):
        qo = (qr // 144) * 9 + oy * 3 + (qr // 48) % 3
        qbuf[oy] = one_hot((qr % 4 == qc // 32) & (qc % 32 == qo) & (qr % 48 < 40))
    for c in loads[4:]:
        c.wait()
    for o9 in range(9):
        wp[o9 * 16 : o9 * 16 + 16, :] = jnp.concatenate(
            [w_two[o9 * 3 + b].astype(F32) for b in range(3)], axis=1
        ).astype(BF16)
    pst[...] = jnp.zeros_like(pst)
    for ox in range(3):
        for oy in range(3):
            o9 = ox * 3 + oy
            for qx in range(2):
                for qy in range(4):
                    to = ((qx + 2 - ox) * 6 + qy + 2 - oy) * 128
                    at = (qx * 4 + qy) * 128
                    for s in range(S):
                        pst[s, o9 * 16 : o9 * 16 + 16, to : to + 128] = pooled[
                            s * 16 : s * 16 + 16, at : at + 128
                        ]
    e1r, e1c = iota((128, 256), 0), iota((128, 256), 1)
    e1 = one_hot(e1c // 2 == e1r)
    par1 = (iota((48, 256), 1) % 2).astype(F32)
    for hx in range(2):
        for hy in range(4):
            at = (hx * 4 + hy) * 128
            up = dot(place_one[:, at : at + 128].astype(F32).astype(BF16), e1)
            for dx in range(2):
                for dy in range(2):
                    to = ((2 * hx + dx) * 8 + 2 * hy + dy) * 256
                    ok = (up == par1 + float(4 * dx + 2 * dy)) & (mask_one[:, to : to + 256] == 1)
                    sel[:, to : to + 256] = one_hot(ok)

    in32[...] = jnp.zeros_like(in32)
    for s in range(S):
        for x in range(4):
            for y in range(8):
                at = (x * 8 + y) * 256
                in32[s * 6 + x + 1, 4 * y + 4 : 4 * y + 8, :] = inp[s, :, at : at + 256].astype(F32)
    sr, sc = iota((192, 288), 0), iota((192, 288), 1)
    xp = sr % 32 % 6
    from_i = jnp.where(xp == 0, 0, jnp.where(xp == 5, 2, 1))
    from_x = jnp.where(xp == 0, 3, jnp.where(xp == 5, 0, xp - 1))
    want = (from_i * 3 + (sr // 32) % 3) * 32 + (sr // 96) * 16 + 4 + from_x
    rowsel[...] = one_hot((sc == want) & (sr % 32 < 18))
    yr, yc = iota((48, 128), 0), iota((48, 128), 1)
    same = (yr % 4 == (yc // 8) % 4) & (yc < 96)
    ysel[0] = one_hot(same & (yr // 4 == 0) & (yc % 8 == 7))
    ysel[1] = one_hot(same & (yr // 4 >= 1) & (yr // 4 <= 8) & (yc % 8 == yr // 4 - 1))
    ysel[2] = one_hot(same & (yr // 4 == 9) & (yc % 8 == 0))

    fr, fc = iota((32, 768), 0), iota((32, 768), 1)
    f_in, f_mid, f_b = fc % 128, (fc // 128) % 2, fc // 256
    left = (f_b == 2) & (f_in == 0)
    right = (f_b == 0) & (f_in == 127)

    def halo_rows(row):
        return one_hot((left & (fr == row)) | (right & (fr == 16 + row)))

    f_m, f_p = halo_rows(f_mid), halo_rows(2 + f_mid)
    f_y = [halo_rows(2 * f_mid + q) for q in range(2)]
    lane = (iota((96, 128), 1) % 2).astype(F32)
    dz = [1.0 - lane, lane, 1.0 - lane]
    gt_all.wait_recv()

    def put(b, x, y, dx, dy, um, up):
        v = jnp.where(up == (dz[b] + float(4 * dx + 2 * dy)).astype(BF16), um, jnp.zeros((), BF16))
        to = (x * 6 + y) * 128
        for s in range(S):
            z3[s, b * 32 : b * 32 + 32, to : to + 128] = v[s * 32 : s * 32 + 32]

    for dj in (0, -1, 1):
        if dj == -1:
            gy_all.wait_recv()
        for di in (0, -1, 1):
            if dj == 0 and di == -1:
                gx_all.wait_recv()
            stack = rt[(di + 1) * 3 + dj + 1].reshape(32, 128)[:, 0:96]
            xs = {-1: [(0, 1)], 0: [(1, 0), (2, 1)], 1: [(3, 0)]}[di]
            if dj == 0:
                ref = mp if di == 0 else rx.at[(di + 1) // 2]
                um = (dot(ref[0], e3) + dot(stack, f_m, TN)).astype(BF16)
                up = (dot(ref[1], e3) + dot(stack, f_p, TN)).astype(BF16)
                for b in range(3):
                    for qy in range(2):
                        at = (b * 2 + qy) * 128
                        for x, dx in xs:
                            for dy in range(2):
                                put(b, x, 1 + 2 * qy + dy, dx, dy, um[:, at : at + 128], up[:, at : at + 128])
            else:
                q = 1 if dj < 0 else 0
                u = (dot(ry[di + 1, (dj + 1) // 2], e3) + dot(stack, f_y[q], TN)).astype(BF16)
                for b in range(3):
                    at = b * 256
                    for x, dx in xs:
                        put(b, x, 0 if dj < 0 else 5, dx, q, u[:, at : at + 128], u[:, at + 128 : at + 256])

    reach = [(96, 144), (48, 144), (0, 96), (0, 48)]
    thirds = [jnp.zeros((48, 96), F32)] * 3
    for x in range(4):
        r0, r1_ = reach[x]
        part = jnp.zeros((r1_ - r0, 96), F32)
        for s in range(S):
            part = part + dot(
                pst[s, r0:r1_, x * 768 : x * 768 + 768], z3[s, :, x * 768 : x * 768 + 768], NT
            )
        for r in range(r0, r1_, 48):
            thirds[r // 48] = thirds[r // 48] + part[r - r0 : r - r0 + 48]
    w2 = jnp.concatenate(thirds, axis=0)
    w2 = jnp.concatenate([w2, jnp.zeros((144, 32), F32)], axis=1)
    for i in range(CHUNKS):
        wg[i] = w2[i * ROWS : i * ROWS + ROWS]
    for o in range(CHUNKS):
        @pl.when(~(owner & (chip == o)))
        def _():
            p1(o).start()

    for s in range(S):
        for x in range(4):
            r0, r1_ = reach[x]
            tbuf[r0:r1_, x * 768 : x * 768 + 768] = dot(wp[r0:r1_, :], z3[s, :, x * 768 : x * 768 + 768])
        for x in range(2):
            for y in range(4):
                a = jnp.zeros((16, 128), F32)
                for ox in range(3):
                    for oy in range(3):
                        r = (ox * 3 + oy) * 16
                        at = ((x + 2 - ox) * 6 + y + 2 - oy) * 128
                        a = a + tbuf[r : r + 16, at : at + 128]
                gp[s * 16 : s * 16 + 16, (x * 4 + y) * 128 : (x * 4 + y) * 128 + 128] = a.astype(BF16)
    gp_copy = pltpu.make_async_copy(gp, gp_h, o_sem.at[0])
    gp_copy.start()

    for hx in range(2):
        for hy in range(4):
            at = (hx * 4 + hy) * 128
            up = dot(gp[:, at : at + 128], e1)
            for dx in range(2):
                for dy in range(2):
                    x, y = 2 * hx + dx, 2 * hy + dy
                    to = (x * 8 + y) * 256
                    v = (up * sel[:, to : to + 256].astype(F32)).astype(BF16)
                    for s in range(S):
                        gc[s, x, y * 16 : y * 16 + 16, :] = v[s * 16 : s * 16 + 16]
    picked = dot(rowsel[...], rt[...].reshape(288, 128))
    picked = jnp.where(iota((192, 128), 1) // 32 == (iota((192, 128), 0) % 32) // 6, picked, 0.0).astype(BF16)
    edges = []
    for side in range(2):
        e = jnp.zeros((48, 32), F32)
        for j in range(3):
            r = side * 96 + j * 32
            e = e + dot(ysel[j], picked[r : r + 32], NT)
        edges.append(jnp.concatenate([e, jnp.zeros((48, 96), F32)], axis=1))
    edge_below, edge_above = edges

    lane256 = iota((48, 256), 1)
    beside = jnp.zeros((48, 128), F32)
    iy_all.wait_recv()
    for x in (1, 2, 3, 4, 0, 5):
        if x == 0:
            ix_all.wait_recv()
        for s in range(S):
            l = s * 6 + x
            for y in range(10):
                if y in (0, 9):
                    v = riy[0 if y == 0 else 1, s, :, x * 256 : x * 256 + 256]
                elif x in (0, 5):
                    v = rix[0 if x == 0 else 1, s, :, (y - 1) * 256 : y * 256]
                else:
                    continue
                in32[l, 4 * y : 4 * y + 4, :] = v.astype(F32)
            v = in32[l]
            below = jnp.concatenate([pltpu.roll(edge_below, (0 - l) % 128, 1), beside], axis=1)
            above = jnp.concatenate([beside, pltpu.roll(edge_above, (127 - l) % 128, 1)], axis=1)
            lhs[l, 0:48, :] = jnp.where(lane256 == 0, below, pltpu.roll(v, 1, 1)).astype(BF16)
            lhs[l, 48:96, :] = v.astype(BF16)
            lhs[l, 96:144, :] = jnp.where(lane256 == 255, above, pltpu.roll(v, 255, 1)).astype(BF16)

    a1 = jnp.zeros((128, 432), F32)
    for s in range(S):
        for x in range(4):
            three = lhs[s * 6 + x : s * 6 + x + 3].reshape(432, 256)
            a1 = a1 + dot(gc[s, x], three, NT)
    acc1[...] = a1
    y_lane = (iota((16, 432), 1) % 48) // 4
    parts = []
    for oy in range(3):
        t = jnp.zeros((16, 432), F32)
        for y in range(8):
            t = t + jnp.where(y_lane == y + oy, acc1[y * 16 : y * 16 + 16, :], 0.0)
        parts.append(t)
    w1 = jnp.zeros((16, 128), F32)
    for oy in range(3):
        t = parts[oy]
        hi = t.astype(BF16)
        t = t - hi.astype(F32)
        mid = t.astype(BF16)
        low_part = (t - mid.astype(F32)).astype(BF16)
        r = dot(jnp.concatenate([hi, mid, low_part], axis=0), qbuf[oy])
        w1 = w1 + (r[0:16] + r[16:32] + r[32:48])
    own1[0] = w1[0:8]
    own1[1] = w1[8:16]
    t1().start()

    @pl.when(owner)
    def _():
        p1_got.wait_recv()
        r1[men] = wg[chip]
        total = r1[0]
        for n in range(1, 32):
            total = total + r1[n]
        r2[zc] = total
        for n in range(1, 8):
            p2(n, dp).start()
            p2(n, dp + 1 - 2 * core).start()
        p2(0, dp + 1 - 2 * core).start()

    t1().wait_recv()
    c2[chip] = own1[core] + c1[...]
    for n in range(1, 16):
        t2(n).start()

    @pl.when(owner)
    def _():
        p2_got.wait_recv()

    @pl.when(~owner)
    def _():
        p2_got_all.wait_recv()

    total = r2[0]
    for zz in range(1, 8):
        total = total + r2[zz]
    fin[chip] = total
    for n in range(1, 16):
        p3(n).start()

    t2_all.wait_recv()
    total = c2[0]
    for n in range(1, 16):
        total = total + c2[n]
    c3[core, zc] = total
    for n in range(1, 8):
        t3(n, dp).start()
    t3(0, dp + 1 - 2 * core).start()
    for n in range(1, 8):
        t3(n, dp + 1 - 2 * core).start()

    p3_all.wait_recv()
    fin_copy = pltpu.make_async_copy(fin, fin_h, o_sem.at[1])
    fin_copy.start()
    t3_all.wait_recv()
    for half in range(2):
        total = c3[half, 0]
        for n in range(1, 8):
            total = total + c3[half, n]
        one[half] = total
    one_copy = pltpu.make_async_copy(one, one_h, o_sem.at[2])
    one_copy.start()

    for c in (gt_all, gx_all, gy_all, ix_all, iy_all, t2_all, t3_all, p3_all):
        c.wait_send()
    t1().wait_send()

    @pl.when(owner)
    def _():
        p1_sent.wait_send()
        p2_sent.wait_send()

    @pl.when(~owner)
    def _():
        p1_sent_all.wait_send()

    gp_copy.wait()
    fin_copy.wait()
    one_copy.wait()


def finish(gp, fin, one, gp_out, w1_out, w2_out):
    gp_out[...] = gp[...]
    v = jnp.concatenate([fin[n] for n in range(CHUNKS)], axis=0) * (float(TOTAL // 8) ** -0.5)
    for o9 in range(9):
        for b in range(3):
            w2_out[o9 * 3 + b] = v[o9 * 16 : o9 * 16 + 16, b * 32 : b * 32 + 32]
    for i in range(2):
        v = one[i] * (float(TOTAL) ** -0.5)
        for c in range(4):
            w1_out[c, i * 8 : i * 8 + 8, :] = v[:, c * 32 : c * 32 + 27]


def local(inputs, mask_one, place_one, pooled_one, w_two, mask_two, place_two, grad_two):
    vm = pl.BlockSpec(memory_space=pltpu.VMEM)
    anywhere = pl.BlockSpec(memory_space=pl.ANY)
    dma = pltpu.SemaphoreType.DMA
    gp, fin, one = pl.pallas_call(
        kernel,
        out_shape=(
            jax.ShapeDtypeStruct((48, 1024), BF16),
            jax.ShapeDtypeStruct((CHUNKS, ROWS, 128), F32),
            jax.ShapeDtypeStruct((2, 8, 128), F32),
        ),
        in_specs=[anywhere] * 8,
        out_specs=(anywhere, anywhere, anywhere),
        scratch_shapes=[
            pltpu.VMEM((S, 4, 8192), BF16),
            pltpu.VMEM((48, 8192), I32),
            pltpu.VMEM((48, 1024), I32),
            pltpu.VMEM((48, 1024), BF16),
            pltpu.VMEM((27, 16, 32), BF16),
            pltpu.VMEM((96, 1024), I32),
            pltpu.VMEM((96, 128), I32),
            pltpu.VMEM((96, 128), BF16),
            pltpu.VMEM((48, 1024), BF16),
            pltpu.VMEM((2, 96, 128), BF16),
            pltpu.VMEM((2, 96, 128), BF16),
            pltpu.VMEM((2, 16, 128), BF16),
            pltpu.VMEM((2, 2, 96, 128), BF16),
            pltpu.VMEM((3, 2, 96, 128), BF16),
            pltpu.VMEM((9, 2, 16, 128), BF16),
            pltpu.VMEM((S, 96, 3072), BF16),
            pltpu.VMEM((144, 96), BF16),
            pltpu.VMEM((S, 144, 3072), BF16),
            pltpu.VMEM((144, 3072), F32),
            pltpu.VMEM((2, S, 4, 1024), BF16),
            pltpu.VMEM((2, S, 4, 2048), BF16),
            pltpu.VMEM((2, S, 4, 1536), BF16),
            pltpu.VMEM((18, 48, 256), F32),
            pltpu.VMEM((192, 288), BF16),
            pltpu.VMEM((3, 48, 128), BF16),
            pltpu.VMEM((18, 144, 256), BF16),
            pltpu.VMEM((48, 8192), BF16),
            pltpu.VMEM((S, 4, 128, 256), BF16),
            pltpu.VMEM((128, 432), F32),
            pltpu.VMEM((CHUNKS, ROWS, 128), F32),
            pltpu.VMEM((32, ROWS, 128), F32),
            pltpu.VMEM((8, ROWS, 128), F32),
            pltpu.VMEM((CHUNKS, ROWS, 128), F32),
            pltpu.VMEM((2, 8, 128), F32),
            pltpu.VMEM((3, 432, 128), BF16),
            pltpu.VMEM((2, 8, 128), F32),
            pltpu.VMEM((8, 128), F32),
            pltpu.VMEM((16, 8, 128), F32),
            pltpu.VMEM((2, 8, 8, 128), F32),
            *[dma] * 10,
            *[dma] * 6,
            *[dma] * 6,
            dma((8,)), dma((3,)),
        ],
        compiler_params=pltpu.CompilerParams(
            collective_id=0, has_side_effects=True, vmem_limit_bytes=56 * 1024 * 1024
        ),
        name="whole",
    )(
        inputs.reshape(S, 4, 8192),
        mask_one.reshape(48, 8192),
        place_one.reshape(48, 1024),
        pooled_one.reshape(48, 1024),
        w_two,
        mask_two.reshape(96, 1024),
        place_two.reshape(96, 128),
        grad_two.reshape(96, 128),
    )
    gp, w1, w2 = pl.pallas_call(
        finish,
        out_shape=(
            jax.ShapeDtypeStruct((48, 1024), BF16),
            jax.ShapeDtypeStruct((4, 16, 27), F32),
            jax.ShapeDtypeStruct((27, 16, 32), F32),
        ),
        in_specs=[vm, vm, vm],
        out_specs=(vm, vm, vm),
        name="finish",
    )(gp, fin, one)
    return gp.reshape(S, 1, 16, 1024), w1.transpose(2, 0, 1), w2


def solution(mesh):
    spec = P("dp", "space", None, None)
    return jax.shard_map(
        local,
        mesh=mesh,
        in_specs=(spec, spec, spec, spec, P(), spec, spec, spec),
        out_specs=(spec, P(), P()),
        check_vma=False,
    )
```
